32 devices in a mesh: batch: 4 (over x, core), seq: 8 (over z, y).
Axes of the slice: x: 2, y: 2, z: 4, core: 2. Of those that a mesh axis runs over, the one named last changes fastest.
Arguments:
- inputs: bfloat16 [4, 2048, 512], P('batch', 'seq'), may hold values from -6 to 6
- lengths: int32 [4], P('batch'), may hold values from 1228 to 2047
- key_mask: int32 [4, 2048], P('batch', 'seq'), may hold values 0 or 1
- norm_gain: float32 [512], replicated, may hold values from 0.25 to 1.75
- ema_expand: float32 [512, 16], replicated, may hold values from -4 to 4
- ema_alpha: float32 [512, 16], replicated, may hold values from -2 to 2
- ema_delta: float32 [512, 16], replicated, may hold values from -9 to -3
- ema_eta: float32 [512, 16], replicated, may hold values from -0.1 to 0.1
- ema_omega: float32 [512], replicated, may hold values from -4 to 4
- w_value: bfloat16 [512, 1024], replicated, may hold values from -0.25 to 0.25
- w_mix: bfloat16 [512, 2176], replicated, may hold values from -0.25 to 0.25
- qk_affine: float32 [3, 128], replicated, may hold values from -4 to 4
- w_hidden: bfloat16 [1024, 512], replicated, may hold values from -0.5 to 0.5
- ffn_gain: float32 [512], replicated, may hold values from 0.25 to 1.75
- w_up: bfloat16 [512, 1024], replicated, may hold values from -0.25 to 0.25
- w_down: bfloat16 [1024, 512], replicated, may hold values from -0.1875 to 0.1875
- cotangent: bfloat16 [4, 2048, 512], P('batch', 'seq'), may hold values from -6 to 6
Outputs:
- out: bfloat16 [4, 2048, 512], P('batch', 'seq')
- d_input: bfloat16 [4, 2048, 512], P('batch', 'seq')
- grad_norm_gain: float32 [512], replicated
- grad_expand: float32 [512, 16], replicated
- grad_alpha: float32 [512, 16], replicated
- grad_delta: float32 [512, 16], replicated
- grad_eta: float32 [512, 16], replicated
- grad_omega: float32 [512], replicated
- grad_value: float32 [512, 1024], replicated
- grad_mix: float32 [512, 2176], replicated
- grad_qk: float32 [3, 128], replicated
- grad_hidden: float32 [1024, 512], replicated
- grad_ffn_gain: float32 [512], replicated
- grad_up: float32 [512, 1024], replicated
- grad_down: float32 [1024, 512], replicated
The draws below stay inside these ranges and needn't reach their ends.
All inputs are finite; a program needn't handle non-finite values. No bound on the sum of `key_mask` on one device may be relied on, other than what follows from the above.
Results may differ from the reference program's by a relative error of at most 0.03.
Values may be sent and summed in bfloat16 or wider, within the bound.
No kernel may reach another device: no remote copies, remote signals or barrier semaphores. Data moves between devices by JAX's collectives and lax.ppermute only.
A program may use at most 320 MiB of HBM per device.

```python
import jax
import jax.numpy as jnp
from jax import lax

D = 512
Z = 128
V = 1024
H = 16
FF = 1024
BLOCK = 128
WINDOW = 4096
SEQS = 4
LEN = 2048


def place_ends(values, own_key, least, top_value):
    place = [jax.random.randint(jax.random.fold_in(own_key, axis), (), 0, length) for axis, length in enumerate(values.shape)]
    main_axis = values.shape.index(max(values.shape))
    neighbour = place[:main_axis] + [(place[main_axis] + 1) % values.shape[main_axis]] + place[main_axis + 1:]
    return values.at[tuple(place)].set(least).at[tuple(neighbour)].set(top_value)


def shard_levels(stream_key, extent, cuts, low, high):
    def one(axis_at, blocks):
        heights = jax.random.uniform(jax.random.fold_in(jax.random.fold_in(stream_key, 6), axis_at), (blocks,), jnp.float32, low / len(cuts), high / len(cuts))
        return jnp.repeat(jnp.exp(heights), extent[axis_at] // blocks).reshape((-1,) + (1,) * (len(extent) - axis_at - 1))

    factor_of = one(*cuts[0])
    for cut in cuts[1:]:
        factor_of = factor_of * one(*cut)
    return factor_of


def bell_draw(rng, extent, scale, most, split=(), dtype=jnp.bfloat16):
    entries = jax.random.normal(rng, extent, jnp.float32) * scale
    if len(split) > 0:
        entries = shard_levels(rng, extent, split, -0.22, 0.18) * entries
    return jnp.clip(entries, min=-most, max=most).astype(dtype)


def setup_inputs(seed: int = 0) -> dict:
    streams_of = jax.random.split(jax.random.key(seed), 18)
    return {
        "inputs": bell_draw(streams_of[0], (SEQS, LEN, D), 1.0, 6.0, ((0, 4), (1, 8))),
        "lengths": place_ends(jax.random.randint(streams_of[1], (SEQS,), LEN * 6 // 10, LEN), jax.random.fold_in(streams_of[1], 1), LEN * 6 // 10, LEN - 1).astype(jnp.int32),
        "key_mask": place_ends((jax.random.randint(streams_of[2], (SEQS, LEN), 0, 10) < 9).astype(jnp.int32), jax.random.fold_in(streams_of[2], 1), 0, 1),
        "norm_gain": jnp.clip(1.0 + 0.15 * jax.random.normal(streams_of[3], (D,), jnp.float32), 0.25, 1.75),
        "ema_expand": bell_draw(streams_of[4], (D, H), 1.0, 4.0, (), jnp.float32),
        "ema_alpha": jnp.clip(jax.random.uniform(streams_of[5], (D, H), jnp.float32, -2.0, 2.0), -2.0, 2.0),
        "ema_delta": jnp.clip(jax.random.uniform(streams_of[6], (D, H), jnp.float32, -9.0, -3.0), -9.0, -3.0),
        "ema_eta": bell_draw(streams_of[7], (D, H), 0.02, 0.1, (), jnp.float32),
        "ema_omega": bell_draw(streams_of[8], (D,), 1.0, 4.0, (), jnp.float32),
        "w_value": bell_draw(streams_of[9], (D, V), D ** -0.5, 0.25),
        "w_mix": bell_draw(streams_of[10], (D, 2 * D + Z + V), D ** -0.5, 0.25),
        "qk_affine": bell_draw(streams_of[11], (3, Z), 1.0, 4.0, (), jnp.float32),
        "w_hidden": bell_draw(streams_of[12], (V, D), (V // 8) ** -0.5, 0.5),
        "ffn_gain": jnp.clip(1.0 + 0.15 * jax.random.normal(streams_of[13], (D,), jnp.float32), 0.25, 1.75),
        "w_up": bell_draw(streams_of[14], (D, FF), D ** -0.5, 0.25),
        "w_down": bell_draw(streams_of[15], (FF, D), FF ** -0.5, 0.1875),
        "cotangent": bell_draw(streams_of[16], (SEQS, LEN, D), 1.0, 6.0, ((0, 4), (1, 8))),
    }


@jax.custom_vjp
def low(v):
    return lax.optimization_barrier(v.astype(jnp.bfloat16)).astype(jnp.float32)

@jax.custom_vjp
def low_back(v):
    return v

def low_keep(v):
    return (low(v), None)

def low_pass(kept, grad):
    return (grad,)

def back_keep(v):
    return (v, None)

def back_low(kept, grad):
    return (low(grad),)
low.defvjp(low_keep, low_pass)
low_back.defvjp(back_keep, back_low)

def layer_norm(values, gain):
    center = lax.optimization_barrier(jnp.mean(values, axis=-1, keepdims=True))
    shifted = values - center
    spread = lax.optimization_barrier(jnp.mean(shifted * shifted, axis=-1, keepdims=True))
    return shifted * lax.rsqrt(spread + 1e-05) * gain

def product(left, right):
    return jnp.dot(left, right, precision=lax.Precision.HIGHEST)

def ema_kernel(expand, alpha_logit, delta_logit, eta):
    alpha = jax.nn.sigmoid(alpha_logit)
    delta = jax.nn.sigmoid(delta_logit)
    log_decay = jnp.log(1.0 - alpha * delta)
    coeff = eta * alpha * expand
    lags = jnp.arange(WINDOW).astype(jnp.float32)
    powers = jnp.exp(log_decay[:, :, None] * lags[None, None, :])
    return jnp.einsum('jh,jhl->lj', coeff, powers, precision=lax.Precision.HIGHEST)

def long_conv(signal, kernel):
    total = LEN + WINDOW
    spectrum = jnp.fft.rfft(signal, n=total, axis=0) * jnp.fft.rfft(kernel, n=total, axis=0)
    return jnp.fft.irfft(spectrum, n=total, axis=0)[:LEN]

def forward(x_row, keep, allowed, norm_gain, ema_expand, ema_alpha, ema_delta, ema_eta, ema_omega, w_value, w_mix, qk_affine, w_hidden, ffn_gain, w_up, w_down):
    normed_low = low(layer_norm(x_row, norm_gain))
    masked = normed_low * keep[:, None]
    ema = long_conv(masked, ema_kernel(ema_expand, ema_alpha, ema_delta, ema_eta))
    mix_in = low(jax.nn.silu(ema + ema_omega * masked))
    value = low(jax.nn.silu(low_back(product(normed_low, w_value))))
    mixed = low_back(product(mix_in, w_mix))
    update = jax.nn.sigmoid(mixed[:, :D])
    shared = jax.nn.silu(mixed[:, D:D + Z])
    reset = jax.nn.silu(mixed[:, D + Z:D + Z + V])
    hidden_in = mixed[:, D + Z + V:]
    groups = LEN // BLOCK
    query = low(shared * qk_affine[0] + qk_affine[1]).reshape(groups, BLOCK, Z)
    keys = low(shared * qk_affine[2]).reshape(groups, BLOCK, Z)
    scores = low_back(jnp.einsum('gad,gbd->gab', query, keys, precision=lax.Precision.HIGHEST)) * Z ** (-0.5)
    probs = jax.nn.softmax(jnp.where(allowed, scores, -1000000000.0), axis=-1)
    attended = low_back(jnp.einsum('gab,gbv->gav', low(probs), value.reshape(groups, BLOCK, V), precision=lax.Precision.HIGHEST)).reshape(LEN, V)
    gated = low(attended * reset)
    cand = jax.nn.silu(hidden_in + low_back(product(gated, w_hidden)))
    resid = x_row + update * (cand - x_row)
    ffn_in = low(layer_norm(resid, ffn_gain))
    inner = low(jax.nn.silu(low_back(product(ffn_in, w_up))))
    return resid + low_back(product(inner, w_down))

def row_masks(length, mask_row):
    places = jnp.arange(LEN).astype(jnp.int32)
    keep = (places < length).astype(jnp.float32)
    key_ok = (keep * mask_row.astype(jnp.float32)).reshape(LEN // BLOCK, BLOCK)
    steps = jnp.arange(BLOCK)
    diagonal = (steps[:, None] == steps[None, :])[None]
    earlier = (steps[:, None] > steps[None, :])[None]
    allowed = diagonal | earlier & (key_ok[:, None, :] > 0.5)
    return (keep, allowed)

def reference(inputs, lengths, key_mask, norm_gain, ema_expand, ema_alpha, ema_delta, ema_eta, ema_omega, w_value, w_mix, qk_affine, w_hidden, ffn_gain, w_up, w_down, cotangent):
    params = (norm_gain, ema_expand, ema_alpha, ema_delta, ema_eta, ema_omega, w_value.astype(jnp.float32), w_mix.astype(jnp.float32), qk_affine, w_hidden.astype(jnp.float32), ffn_gain, w_up.astype(jnp.float32), w_down.astype(jnp.float32))

    def one_seq(carry, item):
        x_row, length, mask_row, cot_row = item
        keep, allowed = row_masks(length, mask_row)

        def run(x_in, *weights):
            return forward(x_in, keep, allowed, *weights)
        result, pull = jax.vjp(run, x_row.astype(jnp.float32), *params)
        grads = pull(cot_row.astype(jnp.float32))
        summed = tuple((total + grad for total, grad in zip(carry, grads[1:])))
        return (summed, (result.astype(jnp.bfloat16), grads[0].astype(jnp.bfloat16)))
    start = tuple((jnp.zeros(p.shape, jnp.float32) for p in params))
    sums, (outputs, input_grads) = lax.scan(one_seq, start, (inputs, lengths, key_mask, cotangent))
    return (outputs, input_grads) + sums
```

```python
import functools

import jax
import jax.numpy as jnp
from jax import lax
from jax.experimental import pallas as pl
from jax.experimental.pallas import tpu as pltpu
from jax.sharding import PartitionSpec as P

D = 512
Z = 128
V = 1024
H = 16
FF = 1024
BLOCK = 128
WINDOW = 4096
MIX = 2 * D + Z + V
AXES = ("batch", "seq")
F32 = jnp.float32
BF16 = jnp.bfloat16
PIECES = 32
VMEM_LIMIT = 40 * 2**20


def sigmoid(v):
    return 1.0 / (1.0 + jnp.exp(-v))


def dot(a, b):
    return lax.dot_general(a, b, (((1,), (0,)), ((), ())), preferred_element_type=F32)


def dot_nt(a, b):
    return lax.dot_general(a, b, (((1,), (1,)), ((), ())), preferred_element_type=F32)


def dot_tn(a, b):
    return lax.dot_general(a, b, (((0,), (0,)), ((), ())), preferred_element_type=F32)


def call(body, outs, scratch=(), smem=0, flops=10**9, count=1):
    spec = pl.BlockSpec(memory_space=pltpu.VMEM)
    small = pl.BlockSpec(memory_space=pltpu.SMEM)

    def run(*args):
        return pl.pallas_call(
            body,
            out_shape=[jax.ShapeDtypeStruct(s, d) for s, d in outs],
            in_specs=[small] * smem + [spec] * (len(args) - smem),
            out_specs=[spec] * len(outs),
            scratch_shapes=list(scratch),
            compiler_params=pltpu.CompilerParams(vmem_limit_bytes=VMEM_LIMIT),
            cost_estimate=pl.CostEstimate(
                flops=flops, bytes_accessed=4 * 2**20, transcendentals=0
            ),
        )(*args)

    return run


def row8(ref, t):
    return jnp.broadcast_to(ref[pl.ds(t, 1), :], (8, D))


LANES = 128


def put8(part_ref, t, rows, eight):
    for j in range(D // LANES):
        base = pl.multiple_of(j * rows * 8 + t * 8, 8)
        part_ref[pl.ds(base, 8), :] = eight[:, j * LANES : (j + 1) * LANES]


def fold8(part_ref, out_ref, rows):
    def one(g, _):
        at = pl.multiple_of(g * 8, 8)
        for j in range(D // LANES):
            base = pl.multiple_of(j * rows * 8 + g * 64, 64)
            acc = part_ref[pl.ds(base, 8, stride=8), :]
            for k in range(1, 8):
                acc = acc + part_ref[pl.ds(base + k, 8, stride=8), :]
            out_ref[pl.ds(at, 8), j * LANES : (j + 1) * LANES] = acc
        return 0

    lax.fori_loop(0, rows // 8, one, 0)


def norm_kernel(rows, lim_ref, x_ref, gain_ref, a_ref, normed_ref, masked_ref, state_ref, m_ref):
    x = x_ref[...].astype(F32)
    center = jnp.mean(x, axis=1, keepdims=True)
    shifted = x - center
    spread = jnp.mean(shifted * shifted, axis=1, keepdims=True)
    normed = (shifted * lax.rsqrt(spread + 1e-05) * gain_ref[...]).astype(BF16)
    normed_ref[...] = normed
    place = lax.broadcasted_iota(jnp.int32, (rows, 1), 0)
    masked = jnp.where(place < lim_ref[0], normed.astype(F32), 0.0)
    masked_ref[...] = masked.astype(BF16)
    m_ref[...] = masked
    a = (a_ref[0:8, :], a_ref[8:16, :])

    def step(g, carry):
        s, q = carry
        for k in range(8):
            row = row8(m_ref, g * 8 + k)
            grown = tuple(a[i] * s[i] for i in range(2))
            q = tuple(a[i] * q[i] + grown[i] for i in range(2))
            s = tuple(grown[i] + row for i in range(2))
        return s, q

    zero = jnp.zeros((8, D), F32)
    s, q = lax.fori_loop(0, rows // 8, step, ((zero, zero), (zero, zero)))
    state_ref[0:8, :] = s[0].astype(BF16)
    state_ref[8:16, :] = s[1].astype(BF16)
    state_ref[16:24, :] = q[0].astype(BF16)
    state_ref[24:32, :] = q[1].astype(BF16)


def pack(table_ref, keep_ref, send_ref, at, src_ref, piece_rows):
    cols = src_ref.shape[1]
    for pos in range(PIECES):
        dst = keep_ref if pos < PIECES // 2 else send_ref
        slot = pos % (PIECES // 2)
        row = pl.multiple_of(table_ref[pos] * piece_rows, 16)
        tile = at
        for r in range(piece_rows // 16):
            for c in range(cols // 128):
                dst[slot, tile * 16 : tile * 16 + 16, :] = src_ref[
                    pl.ds(row + r * 16, 16), c * 128 : c * 128 + 128
                ]
                tile += 1


def forward_kernel(
    rows,
    lim_ref,
    table_ref,
    x_ref,
    masked_ref,
    value_ref,
    far_ref,
    carry_ref,
    a_ref,
    c_ref,
    omega_ref,
    gain_ref,
    qk_ref,
    mask_ref,
    cot_ref,
    wmix_ref,
    whid_ref,
    wup_ref,
    wdown_ref,
    out_ref,
    pre_ref,
    mixlow_ref,
    mixed_ref,
    probs_ref,
    att_ref,
    gated_ref,
    candpre_ref,
    gres_ref,
    ggain_ref,
    keep_ref,
    send_ref,
    m_ref,
    part_ref,
    up_ref,
    gdown_ref,
    gup_ref,
):
    masked = masked_ref[...].astype(F32)
    m_ref[...] = masked
    a = (a_ref[0:8, :], a_ref[8:16, :])
    c = (c_ref[0:8, :], c_ref[8:16, :])

    def step(g, s):
        for k in range(8):
            t = g * 8 + k
            row = row8(m_ref, t)
            s = tuple(a[i] * s[i] + row for i in range(2))
            put8(part_ref, t, rows, c[0] * s[0] + c[1] * s[1])
        return s

    lax.fori_loop(0, rows // 8, step, (carry_ref[0:8, :], carry_ref[8:16, :]))
    fold8(part_ref, pre_ref, rows)
    pre = pre_ref[...] + far_ref[...] + omega_ref[...] * masked
    pre_ref[...] = pre
    mix_low = (pre * sigmoid(pre)).astype(BF16)
    mixlow_ref[...] = mix_low
    mixed_ref[...] = dot(mix_low, wmix_ref[...])
    shared_pre = mixed_ref[:, D : D + Z]
    shared = shared_pre * sigmoid(shared_pre)
    query = (shared * qk_ref[0:1, :] + qk_ref[1:2, :]).astype(BF16)
    key = (shared * qk_ref[2:3, :]).astype(BF16)
    places = lax.broadcasted_iota(jnp.int32, (BLOCK, BLOCK), 0)
    others = lax.broadcasted_iota(jnp.int32, (BLOCK, BLOCK), 1)
    for g in range(rows // BLOCK):
        lo = g * BLOCK
        ok = (mask_ref[:, lo : lo + BLOCK] > 0) & (
            lax.broadcasted_iota(jnp.int32, (1, BLOCK), 1) + lo < lim_ref[0]
        )
        ok = jnp.broadcast_to(ok.astype(F32), (BLOCK, BLOCK)) > 0.5
        allowed = (places == others) | ((places > others) & ok)
        scores = dot_nt(query[lo : lo + BLOCK], key[lo : lo + BLOCK]) * (Z**-0.5)
        scores = jnp.where(allowed, scores, -1000000000.0)
        grown = jnp.exp(scores - jnp.max(scores, axis=1, keepdims=True))
        probs = grown / jnp.sum(grown, axis=1, keepdims=True)
        probs_ref[lo : lo + BLOCK, :] = probs
        att_ref[lo : lo + BLOCK, :] = dot(probs.astype(BF16), value_ref[lo : lo + BLOCK, :])
    reset_pre = mixed_ref[:, D + Z : D + Z + V]
    gated = (att_ref[...] * (reset_pre * sigmoid(reset_pre))).astype(BF16)
    gated_ref[...] = gated
    cand_pre = mixed_ref[:, D + Z + V :] + dot(gated, whid_ref[...])
    candpre_ref[...] = cand_pre
    cand = cand_pre * sigmoid(cand_pre)
    x = x_ref[...].astype(F32)
    resid = x + sigmoid(mixed_ref[:, :D]) * (cand - x)
    center = jnp.mean(resid, axis=1, keepdims=True)
    shifted = resid - center
    inv = lax.rsqrt(jnp.mean(shifted * shifted, axis=1, keepdims=True) + 1e-05)
    unit = shifted * inv
    ffn_low = (unit * gain_ref[...]).astype(BF16)
    up_ref[...] = dot(ffn_low, wup_ref[...])
    up = up_ref[...]
    sig = sigmoid(up)
    inner = (up * sig).astype(BF16)
    out_ref[...] = (resid + dot(inner, wdown_ref[...])).astype(BF16)
    cot = cot_ref[...]
    gdown_ref[...] = dot_tn(inner, cot).astype(BF16)
    gup_low = (dot_nt(cot, wdown_ref[...]) * (sig * (1.0 + up * (1.0 - sig)))).astype(BF16)
    gup_ref[...] = dot_tn(ffn_low, gup_low).astype(BF16)
    g_ffn = dot_nt(gup_low, wup_ref[...])
    ggain_ref[...] = jnp.sum(g_ffn * unit, axis=0, keepdims=True)
    e = g_ffn * gain_ref[...]
    g_norm = inv * (
        e
        - jnp.mean(e, axis=1, keepdims=True)
        - unit * jnp.mean(e * unit, axis=1, keepdims=True)
    )
    gres_ref[...] = cot.astype(F32) + g_norm
    pack(table_ref, keep_ref, send_ref, 0, gdown_ref, FF // PIECES)
    pack(table_ref, keep_ref, send_ref, 8, gup_ref, D // PIECES)


def slope(v, sig):
    return sig * (1.0 + v * (1.0 - sig))


def backward_kernel(
    rows,
    table_ref,
    x_ref,
    masked_ref,
    normed_ref,
    valuepre_ref,
    value_ref,
    pre_ref,
    mixlow_ref,
    mixed_ref,
    probs_ref,
    att_ref,
    gated_ref,
    candpre_ref,
    gres_ref,
    a_ref,
    qk_ref,
    wmix_ref,
    whid_ref,
    wvalue_ref,
    keep_a_ref,
    send_a_ref,
    keep_b_ref,
    send_b_ref,
    gqk_ref,
    gpre_ref,
    gskip_ref,
    gnorm_ref,
    gomega_ref,
    adj_ref,
    gmixed_ref,
    ghid_ref,
    gval_ref,
    gmix_ref,
):
    x = x_ref[...].astype(F32)
    g_resid = gres_ref[...]
    update = sigmoid(mixed_ref[:, :D])
    cand_pre = candpre_ref[...]
    sig = sigmoid(cand_pre)
    g_update = g_resid * update
    g_hid = (g_update * slope(cand_pre, sig)).astype(BF16)
    gskip_ref[...] = g_resid - g_update
    gmixed_ref[:, :D] = (g_update * (1.0 - update) * (cand_pre * sig - x)).astype(BF16)
    gmixed_ref[:, D + Z + V :] = g_hid
    g_gated = dot_nt(g_hid, whid_ref[...])
    reset_pre = mixed_ref[:, D + Z : D + Z + V]
    sig = sigmoid(reset_pre)
    g_att = (g_gated * (reset_pre * sig)).astype(BF16)
    gmixed_ref[:, D + Z : D + Z + V] = (
        g_gated * att_ref[...] * slope(reset_pre, sig)
    ).astype(BF16)
    ghid_ref[...] = dot_tn(gated_ref[...], g_hid).astype(BF16)
    shared_pre = mixed_ref[:, D : D + Z]
    ssig = sigmoid(shared_pre)
    shared = shared_pre * ssig
    query = (shared * qk_ref[0:1, :] + qk_ref[1:2, :]).astype(BF16)
    key = (shared * qk_ref[2:3, :]).astype(BF16)
    g_query, g_key, g_value = [], [], []
    for g in range(rows // BLOCK):
        part = slice(g * BLOCK, (g + 1) * BLOCK)
        probs = probs_ref[part, :]
        g_probs = dot_nt(g_att[part], value_ref[part, :])
        g_value.append(dot_tn(probs.astype(BF16), g_att[part]))
        inner = jnp.sum(g_probs * probs, axis=1, keepdims=True)
        g_scores = (probs * (g_probs - inner) * (Z**-0.5)).astype(BF16)
        g_query.append(dot(g_scores, key[part]))
        g_key.append(dot_tn(g_scores, query[part]))
    g_query = jnp.concatenate(g_query, axis=0)
    g_key = jnp.concatenate(g_key, axis=0)
    g_value = jnp.concatenate(g_value, axis=0)
    gqk_ref[0:1, :] = jnp.sum(g_query * shared, axis=0, keepdims=True)
    gqk_ref[1:2, :] = jnp.sum(g_query, axis=0, keepdims=True)
    gqk_ref[2:3, :] = jnp.sum(g_key * shared, axis=0, keepdims=True)
    g_shared = g_query * qk_ref[0:1, :] + g_key * qk_ref[2:3, :]
    gmixed_ref[:, D : D + Z] = (g_shared * slope(shared_pre, ssig)).astype(BF16)
    value_pre = valuepre_ref[...]
    vsig = sigmoid(value_pre)
    g_vpre = (g_value * slope(value_pre, vsig)).astype(BF16)
    gval_ref[...] = dot_tn(normed_ref[...], g_vpre).astype(BF16)
    gnorm_ref[...] = dot_nt(g_vpre, wvalue_ref[...])
    gmix_ref[...] = dot_tn(mixlow_ref[...], gmixed_ref[...]).astype(BF16)
    pre = pre_ref[...]
    psig = sigmoid(pre)
    g_pre = dot_nt(gmixed_ref[...], wmix_ref[...]) * slope(pre, psig)
    gpre_ref[...] = g_pre
    gomega_ref[...] = jnp.sum(g_pre * masked_ref[...].astype(F32), axis=0, keepdims=True)
    pack(table_ref, keep_a_ref, send_a_ref, 0, ghid_ref, V // PIECES)
    pack(table_ref, keep_a_ref, send_a_ref, 8, gval_ref, D // PIECES)
    pack(table_ref, keep_b_ref, send_b_ref, 0, gmix_ref, D // PIECES)
    a = (a_ref[0:8, :], a_ref[8:16, :])

    def step(g, m):
        for k in range(8):
            row = row8(gpre_ref, rows - 1 - (g * 8 + k))
            m = tuple(a[i] * (m[i] + row) for i in range(2))
        return m

    zero = jnp.zeros((8, D), F32)
    m = lax.fori_loop(0, rows // 8, step, (zero, zero))
    adj_ref[0:8, :] = m[0].astype(BF16)
    adj_ref[8:16, :] = m[1].astype(BF16)


def ema_back_kernel(
    rows,
    lim_ref,
    x_ref,
    masked_ref,
    gpre_ref,
    gskip_ref,
    gnorm_ref,
    far_ref,
    carry_ref,
    adj_ref,
    a_ref,
    c_ref,
    omega_ref,
    gain_ref,
    din_ref,
    ggain_ref,
    gcoeff_ref,
    gdecay_ref,
    m_ref,
    part_ref,
    gx_ref,
):
    m_ref[...] = masked_ref[...].astype(F32)
    a = (a_ref[0:8, :], a_ref[8:16, :])
    c = (c_ref[0:8, :], c_ref[8:16, :])

    def ahead(g, carry):
        s, q, dc, dq = carry
        for k in range(8):
            t = g * 8 + k
            row = row8(m_ref, t)
            grad = row8(gpre_ref, t)
            grown = tuple(a[i] * s[i] for i in range(2))
            q = tuple(a[i] * q[i] + grown[i] for i in range(2))
            s = tuple(grown[i] + row for i in range(2))
            dc = tuple(dc[i] + grad * s[i] for i in range(2))
            dq = tuple(dq[i] + grad * q[i] for i in range(2))
        return s, q, dc, dq

    zero = jnp.zeros((8, D), F32)
    _, _, dc, dq = lax.fori_loop(
        0,
        rows // 8,
        ahead,
        (
            (carry_ref[0:8, :], carry_ref[8:16, :]),
            (carry_ref[16:24, :], carry_ref[24:32, :]),
            (zero, zero),
            (zero, zero),
        ),
    )
    for i in range(2):
        gcoeff_ref[i * 8 : i * 8 + 8, :] = dc[i]
        gdecay_ref[i * 8 : i * 8 + 8, :] = dq[i] * c[i]

    def back(g, m):
        for k in range(8):
            t = rows - 1 - (g * 8 + k)
            row = row8(gpre_ref, t)
            lam = tuple(m[i] + row for i in range(2))
            put8(part_ref, t, rows, c[0] * lam[0] + c[1] * lam[1])
            m = tuple(a[i] * lam[i] for i in range(2))
        return m

    lax.fori_loop(0, rows // 8, back, (adj_ref[0:8, :], adj_ref[8:16, :]))
    fold8(part_ref, gx_ref, rows)
    g_masked = gx_ref[...] + far_ref[...] + omega_ref[...] * gpre_ref[...]
    place = lax.broadcasted_iota(jnp.int32, (rows, 1), 0)
    e = jnp.where(place < lim_ref[0], g_masked, 0.0) + gnorm_ref[...]
    x = x_ref[...].astype(F32)
    shifted = x - jnp.mean(x, axis=1, keepdims=True)
    inv = lax.rsqrt(jnp.mean(shifted * shifted, axis=1, keepdims=True) + 1e-05)
    unit = shifted * inv
    ggain_ref[...] = jnp.sum(e * unit, axis=0, keepdims=True)
    e = e * gain_ref[...]
    g_in = inv * (
        e
        - jnp.mean(e, axis=1, keepdims=True)
        - unit * jnp.mean(e * unit, axis=1, keepdims=True)
    )
    din_ref[...] = (g_in + gskip_ref[...]).astype(BF16)


def unpack_kernel(plan, table_ref, keep_ref, other_ref, *out_refs):
    for (at, piece_rows), out_ref in zip(plan, out_refs):
        cols = out_ref.shape[1]
        for pos in range(PIECES):
            src = keep_ref if pos < PIECES // 2 else other_ref
            slot = pos % (PIECES // 2)
            row = pl.multiple_of(table_ref[pos] * piece_rows, 16)
            tile = at
            for r in range(piece_rows // 16):
                for col in range(cols // 128):
                    out_ref[pl.ds(row + r * 16, 16), col * 128 : col * 128 + 128] = src[
                        slot, tile * 16 : tile * 16 + 16, :
                    ].astype(F32)
                    tile += 1


def flips(sizes):
    batches, seqs = sizes

    def pairs(turn):
        out = []
        for b in range(batches):
            for s in range(seqs):
                nb, ns = turn(b, s)
                out.append((b * seqs + s, nb * seqs + ns))
        return out

    halving = [
        pairs(lambda b, s: (b ^ 1, s)),
        pairs(lambda b, s: (b, s ^ 1) if b & 1 else (b ^ 2, s)),
        pairs(lambda b, s: (b ^ 2, s) if b & 1 else (b, s ^ 1)),
        pairs(lambda b, s: (b, s ^ 2)),
        pairs(lambda b, s: (b, s ^ 4)),
    ]
    rest = []
    bit = 8
    while bit < seqs:
        rest.append(pairs(lambda b, s, bit=bit: (b, s ^ bit)))
        bit *= 2
    return halving, rest


def piece_table():
    b, s = lax.axis_index("batch"), lax.axis_index("seq")
    pos = jnp.arange(PIECES, dtype=jnp.int32)
    core = (b & 1) ^ (pos >> 4)
    one, two = (pos >> 3) & 1, (pos >> 2) & 1
    x = ((b >> 1) & 1) ^ jnp.where(core == 0, one, two)
    y = (s & 1) ^ jnp.where(core == 0, two, one)
    z1 = ((s >> 1) & 1) ^ ((pos >> 1) & 1)
    z2 = ((s >> 2) & 1) ^ (pos & 1)
    return core * 16 + x * 8 + y * 4 + z1 * 2 + z2


def add_low(left, right):
    return (left.astype(F32) + right.astype(F32)).astype(BF16)


def sum_pieces(keep, send, halving, rest):
    now = add_low(keep, lax.ppermute(send, AXES, halving[0]))
    for stage in halving[1:]:
        half = now.shape[0] // 2
        now = add_low(now[:half], lax.ppermute(now[half:], AXES, stage))
    for stage in rest:
        now = add_low(now, lax.ppermute(now, AXES, stage))
    return now


def spread_pieces(now, halving):
    for stage in halving[:0:-1]:
        now = jnp.concatenate([now, lax.ppermute(now, AXES, stage)], axis=0)
    return now, lax.ppermute(now, AXES, halving[0])


def shifted_pairs(seqs, by):
    return [(i, i + by) for i in range(seqs) if 0 <= i + by < seqs]


def moved(state, log_decay, steps):
    fade = jnp.exp(log_decay * steps)
    if state.shape[0] == H:
        return fade * state
    return jnp.concatenate([fade * state[:H], fade * (state[H:] + steps * state[:H])], axis=0)


def neighbour_states(state, log_decay, own_len, direction):
    seqs = lax.axis_size("seq")
    me = lax.axis_index("seq")
    reach = WINDOW // own_len
    own = state.astype(F32)
    if seqs % 2 == 0 and seqs <= reach:
        swap = [(i, i ^ 1) for i in range(seqs)]
        other = lax.ppermute(state, "seq", swap).astype(F32)
        late = (me & 1) if direction == 1 else 1 - (me & 1)
        late = late.astype(F32)
        first = jnp.where(late > 0.5, other, own)
        second = jnp.where(late > 0.5, own, other)
        pair = (moved(first, log_decay, float(own_len)) + second).astype(BF16)
        total = late * other
        for k in range(1, seqs // 2):
            far = lax.ppermute(pair, "seq", shifted_pairs(seqs, 2 * k * direction))
            total = total + moved(far.astype(F32), log_decay, (2 * (k - 1) + late) * own_len)
        return total
    total = jnp.zeros_like(own)
    for k in range(1, min(seqs, reach)):
        far = lax.ppermute(state, "seq", shifted_pairs(seqs, k * direction))
        total = total + moved(far.astype(F32), log_decay, float((k - 1) * own_len))
    return total


def far_part(signal, log_decay, coeff):
    own_len = signal.shape[0]
    steps = jnp.arange(own_len).astype(F32)[:, None, None]
    held = jnp.exp(log_decay[None] * (WINDOW - 1.0 - steps)) * signal[:, None, :]
    after = lax.cumsum(held, axis=0, reverse=True) - held
    return jnp.sum(coeff[None] * jnp.exp(log_decay[None] * (steps + 1.0)) * after, axis=1)


def on_device(
    inputs,
    lengths,
    key_mask,
    norm_gain,
    ema_expand,
    ema_alpha,
    ema_delta,
    ema_eta,
    ema_omega,
    w_value,
    w_mix,
    qk_affine,
    w_hidden,
    ffn_gain,
    w_up,
    w_down,
    cotangent,
):
    _, rows, _ = inputs.shape
    seqs = lax.axis_size("seq")
    reach = WINDOW // rows
    halving, rest = flips((lax.axis_size("batch"), seqs))
    table = piece_table()
    limit = lengths - lax.axis_index("seq") * rows
    x = inputs.reshape(rows, D)
    cot = cotangent.reshape(rows, D)
    tables = (ema_expand.T, ema_alpha.T, ema_delta.T, ema_eta.T)

    def decay_tables(expand, alpha_logit, delta_logit, eta):
        alpha = jax.nn.sigmoid(alpha_logit)
        delta = jax.nn.sigmoid(delta_logit)
        return jnp.log(1.0 - alpha * delta), eta * alpha * expand

    (log_decay, coeff), tables_pull = jax.vjp(decay_tables, *tables)
    decay = jnp.exp(log_decay)
    omega = ema_omega.reshape(1, D)
    gain1 = norm_gain.reshape(1, D)
    gain2 = ffn_gain.reshape(1, D)

    normed, masked, state = call(
        functools.partial(norm_kernel, rows),
        [((rows, D), BF16), ((rows, D), BF16), ((2 * H, D), BF16)],
        [pltpu.VMEM((rows, D), F32)],
        smem=1,
    )(limit, x, gain1, decay)
    carry = neighbour_states(state, log_decay, rows, 1)
    far_here = seqs > reach
    if far_here:
        behind = lax.ppermute(masked, "seq", shifted_pairs(seqs, reach)).astype(F32)
        far, far_pull = jax.vjp(far_part, behind, log_decay, coeff)
    else:
        far = jnp.zeros((1, D), F32)
    value_pre = jnp.dot(normed, w_value, preferred_element_type=F32)
    value_low = jax.nn.silu(value_pre).astype(BF16)

    half = PIECES // 2
    (
        out,
        pre,
        mix_low,
        mixed,
        probs,
        attended,
        gated,
        cand_pre,
        g_resid,
        g_ffn_gain,
        keep1,
        send1,
    ) = call(
        functools.partial(forward_kernel, rows),
        [
            ((rows, D), BF16),
            ((rows, D), F32),
            ((rows, D), BF16),
            ((rows, MIX), F32),
            ((rows, BLOCK), F32),
            ((rows, V), F32),
            ((rows, V), BF16),
            ((rows, D), F32),
            ((rows, D), F32),
            ((1, D), F32),
            ((half, 256, 128), BF16),
            ((half, 256, 128), BF16),
        ],
        [
            pltpu.VMEM((rows, D), F32),
            pltpu.VMEM((rows * 8 * (D // LANES), LANES), F32),
            pltpu.VMEM((rows, FF), F32),
            pltpu.VMEM((FF, D), BF16),
            pltpu.VMEM((D, FF), BF16),
        ],
        smem=2,
    )(
        limit,
        table,
        x,
        masked,
        value_low,
        far,
        carry,
        decay,
        coeff,
        omega,
        gain2,
        qk_affine,
        key_mask,
        cot,
        w_mix,
        w_hidden,
        w_up,
        w_down,
    )
    (
        keep2,
        send2,
        keep3,
        send3,
        g_qk,
        g_pre,
        g_skip,
        g_normed,
        g_omega,
        adjoint,
    ) = call(
        functools.partial(backward_kernel, rows),
        [
            ((half, 256, 128), BF16),
            ((half, 256, 128), BF16),
            ((half, 272, 128), BF16),
            ((half, 272, 128), BF16),
            ((3, Z), F32),
            ((rows, D), F32),
            ((rows, D), F32),
            ((rows, D), F32),
            ((1, D), F32),
            ((H, D), BF16),
        ],
        [
            pltpu.VMEM((rows, MIX), BF16),
            pltpu.VMEM((V, D), BF16),
            pltpu.VMEM((D, V), BF16),
            pltpu.VMEM((D, MIX), BF16),
        ],
        smem=1,
    )(
        table,
        x,
        masked,
        normed,
        value_pre,
        value_low,
        pre,
        mix_low,
        mixed,
        probs,
        attended,
        gated,
        cand_pre,
        g_resid,
        decay,
        qk_affine,
        w_mix,
        w_hidden,
        w_value,
    )
    after = neighbour_states(adjoint, log_decay, rows, -1)
    if far_here:
        g_behind, far_log, far_coeff = far_pull(g_pre)
        g_far = lax.ppermute(
            g_behind.astype(BF16), "seq", shifted_pairs(seqs, -reach)
        ).astype(F32)
    else:
        g_far = jnp.zeros((1, D), F32)
    d_input, g_norm_gain, g_coeff, g_log = call(
        functools.partial(ema_back_kernel, rows),
        [((rows, D), BF16), ((1, D), F32), ((H, D), F32), ((H, D), F32)],
        [
            pltpu.VMEM((rows, D), F32),
            pltpu.VMEM((rows * 8 * (D // LANES), LANES), F32),
            pltpu.VMEM((rows, D), F32),
        ],
        smem=1,
    )(limit, x, masked, g_pre, g_skip, g_normed, g_far, carry, after, decay, coeff, omega, gain1)
    if far_here:
        g_coeff = g_coeff + far_coeff
        g_log = g_log + far_log

    small = jnp.concatenate(
        [
            g_coeff,
            g_log,
            g_norm_gain,
            g_omega,
            g_ffn_gain,
            jnp.pad(g_qk.reshape(1, 3 * Z), ((0, 0), (0, D - 3 * Z))),
        ],
        axis=0,
    )
    for stage in halving + rest:
        small = small + lax.ppermute(small, AXES, stage)
    g_expand, g_alpha, g_delta, g_eta = tables_pull((small[H : 2 * H], small[:H]))

    def finish(keep, send, plan, outs):
        mine, other = spread_pieces(sum_pieces(keep, send, halving, rest), halving)
        return call(
            functools.partial(unpack_kernel, plan), [(s, F32) for s in outs], smem=1
        )(table, mine, other)

    grad_down, grad_up = finish(
        keep1, send1, [(0, FF // PIECES), (8, D // PIECES)], [(FF, D), (D, FF)]
    )
    grad_hidden, grad_value = finish(
        keep2, send2, [(0, V // PIECES), (8, D // PIECES)], [(V, D), (D, V)]
    )
    (grad_mix,) = finish(keep3, send3, [(0, D // PIECES)], [(D, MIX)])
    return (
        out.reshape(inputs.shape),
        d_input.reshape(inputs.shape),
        small[2 * H],
        g_expand.T,
        g_alpha.T,
        g_delta.T,
        g_eta.T,
        small[2 * H + 1],
        grad_value,
        grad_mix,
        small[2 * H + 3, : 3 * Z].reshape(3, Z),
        grad_hidden,
        small[2 * H + 2],
        grad_up,
        grad_down,
    )


def solution(mesh):
    row = P("batch", "seq", None)
    return jax.shard_map(
        on_device,
        mesh=mesh,
        in_specs=(row, P("batch"), P("batch", "seq")) + (P(),) * 13 + (row,),
        out_specs=(row, row) + (P(),) * 13,
        check_vma=False,
    )
```

```python
import functools

import jax
import jax.numpy as jnp
from jax import lax
from jax.experimental import pallas as pl
from jax.experimental.pallas import tpu as pltpu
from jax.sharding import PartitionSpec as P

D = 512
Z = 128
V = 1024
H = 16
FF = 1024
BLOCK = 128
WINDOW = 4096
MIX = 2 * D + Z + V
AXES = ("batch", "seq")
F32 = jnp.float32
BF16 = jnp.bfloat16
PIECES = 32
MIB = 2**20
VMEM_NORM = 8
VMEM_VALUE = 8
VMEM_FORWARD = 32
VMEM_GATES = 20
VMEM_ATT = 16
VMEM_TABLES = 16
VMEM_INPUT = 12
VMEM_OUT = 16


def sigmoid(v):
    return 1.0 / (1.0 + jnp.exp(-v))


def dot(a, b):
    return lax.dot_general(a, b, (((1,), (0,)), ((), ())), preferred_element_type=F32)


def dot_nt(a, b):
    return lax.dot_general(a, b, (((1,), (1,)), ((), ())), preferred_element_type=F32)


def dot_tn(a, b):
    return lax.dot_general(a, b, (((0,), (0,)), ((), ())), preferred_element_type=F32)


class Late:
    def __init__(self, copy, ref):
        self.copy, self.ref, self.waited = copy, ref, False

    def __call__(self):
        if not self.waited:
            self.copy.wait()
            self.waited = True
        return self.ref


SPACES = {"s": pltpu.SMEM, "v": pltpu.VMEM, "h": pltpu.HBM, "o": pltpu.HBM}


def call(body, outs, args, scratch=(), vmem=16, flops=10**9, alias=None):
    late = [i for i, (kind, _) in enumerate(args) if kind == "h"]
    n_in, n_out = len(args), len(outs)

    def run(*refs):
        ins = list(refs[:n_in])
        mine = refs[n_in : n_in + n_out + len(scratch)]
        if late:
            rest = refs[n_in + n_out + len(scratch) :]
            for k, i in enumerate(late):
                copy = pltpu.make_async_copy(ins[i], rest[k], rest[-1].at[k])
                copy.start()
                ins[i] = Late(copy, rest[k])
        body(*ins, *mine)
        for i in late:
            ins[i]()

    buffers = [pltpu.VMEM(args[i][1].shape, args[i][1].dtype) for i in late]
    if late:
        buffers.append(pltpu.SemaphoreType.DMA((len(late),)))
    return pl.pallas_call(
        run,
        out_shape=[jax.ShapeDtypeStruct(shape, dtype) for _, shape, dtype in outs],
        in_specs=[pl.BlockSpec(memory_space=SPACES[kind]) for kind, _ in args],
        out_specs=[pl.BlockSpec(memory_space=SPACES[kind]) for kind, _, _ in outs],
        scratch_shapes=list(scratch) + buffers,
        input_output_aliases=alias or {},
        compiler_params=pltpu.CompilerParams(vmem_limit_bytes=vmem * MIB),
        name=getattr(body, "func", body).__name__,
        cost_estimate=pl.CostEstimate(
            flops=flops, bytes_accessed=4 * MIB, transcendentals=0
        ),
    )(
        *[
            pltpu.with_memory_space_constraint(array, pltpu.HBM) if kind in "ho" else array
            for kind, array in args
        ]
    )


def row8(ref, t):
    return jnp.broadcast_to(ref[pl.ds(t, 1), :], (8, D))


LANES = 128


def put8(part_ref, t, rows, eight):
    for j in range(D // LANES):
        base = pl.multiple_of(j * rows * 8 + t * 8, 8)
        part_ref[pl.ds(base, 8), :] = eight[:, j * LANES : (j + 1) * LANES]


def fold8(part_ref, out_ref, rows):
    def one(g, _):
        at = pl.multiple_of(g * 8, 8)
        for j in range(D // LANES):
            base = pl.multiple_of(j * rows * 8 + g * 64, 64)
            acc = part_ref[pl.ds(base, 8, stride=8), :]
            for k in range(1, 8):
                acc = acc + part_ref[pl.ds(base + k, 8, stride=8), :]
            out_ref[pl.ds(at, 8), j * LANES : (j + 1) * LANES] = acc
        return 0

    lax.fori_loop(0, rows // 8, one, 0)


def norm_kernel(
    rows,
    powers,
    lim_ref,
    x,
    gain,
    alpha,
    delta,
    expand,
    eta,
    wvalue_ref,
    normed_ref,
    masked_ref,
    state_ref,
    a_ref,
    c_ref,
    fade_ref,
    wvalue_out_ref,
    m_ref,
    sem,
):
    copy = pltpu.make_async_copy(wvalue_ref, wvalue_out_ref, sem)
    copy.start()
    x = x()[...].astype(F32)
    center = jnp.mean(x, axis=1, keepdims=True)
    shifted = x - center
    spread = jnp.mean(shifted * shifted, axis=1, keepdims=True)
    normed = (shifted * lax.rsqrt(spread + 1e-05) * gain()[...]).astype(BF16)
    normed_ref[...] = normed
    place = lax.broadcasted_iota(jnp.int32, (rows, 1), 0)
    masked = jnp.where(place < lim_ref[0], normed.astype(F32), 0.0)
    masked_ref[...] = masked.astype(BF16)
    m_ref[...] = masked
    alpha = sigmoid(alpha()[...])
    decay = 1.0 - alpha * sigmoid(delta()[...])
    a_ref[...] = decay
    c_ref[...] = eta()[...] * alpha * expand()[...]
    log_decay = jnp.log(decay)
    for i, power in enumerate(powers):
        fade_ref[i] = jnp.exp(log_decay * power)
    a = (decay[0:8, :], decay[8:16, :])

    def step(g, carry):
        s, q = carry
        for k in range(8):
            row = row8(m_ref, g * 8 + k)
            grown = tuple(a[i] * s[i] for i in range(2))
            q = tuple(a[i] * q[i] + grown[i] for i in range(2))
            s = tuple(grown[i] + row for i in range(2))
        return s, q

    zero = jnp.zeros((8, D), F32)
    s, q = lax.fori_loop(0, rows // 8, step, ((zero, zero), (zero, zero)))
    state_ref[0:8, :] = s[0].astype(BF16)
    state_ref[8:16, :] = s[1].astype(BF16)
    state_ref[16:24, :] = q[0].astype(BF16)
    state_ref[24:32, :] = q[1].astype(BF16)
    copy.wait()


def value_kernel(normed_ref, wvalue_ref, pre_ref, low_ref):
    for lo in range(0, V, D):
        pre = dot(normed_ref[...], wvalue_ref[:, lo : lo + D])
        pre_ref[:, lo : lo + D] = pre
        low_ref[:, lo : lo + D] = (pre * sigmoid(pre)).astype(BF16)


def moved(state, fade, steps):
    if state.shape[0] == H:
        return fade * state
    return jnp.concatenate([fade * state[:H], fade * (state[H:] + steps * state[:H])], axis=0)


def join_kernel(own_len, level, direction, me_ref, group_ref, other_ref, fade_ref, out_ref):
    late = ((me_ref[0] >> level) & 1) == (1 if direction == 1 else 0)
    group, other = group_ref[...].astype(F32), other_ref[...].astype(F32)
    first, second = jnp.where(late, other, group), jnp.where(late, group, other)
    out_ref[...] = (moved(first, fade_ref[level], float(own_len << level)) + second).astype(BF16)


def carried(own_len, direction, me, others, fades):
    total = None
    for i, other_ref in enumerate(others):
        other = other_ref[...].astype(F32)
        blocks = me if direction == 1 else ~me
        late = ((me >> i) & 1) == (1 if direction == 1 else 0)
        for j in range(i):
            on = ((blocks >> j) & 1) == 1
            other = jnp.where(on, moved(other, fades[j], float(own_len << j)), other)
        other = jnp.where(late, other, 0.0)
        total = other if total is None else total + other
    return total


def pack(table_ref, keep_ref, send_ref, at, src_ref, piece_rows):
    cols = src_ref.shape[1]
    for pos in range(PIECES):
        dst = keep_ref if pos < PIECES // 2 else send_ref
        slot = pos % (PIECES // 2)
        row = pl.multiple_of(table_ref[pos] * piece_rows, 16)
        tile = at
        for r in range(piece_rows // 16):
            for c in range(cols // 128):
                dst[slot, tile * 16 : tile * 16 + 16, :] = src_ref[
                    pl.ds(row + r * 16, 16), c * 128 : c * 128 + 128
                ]
                tile += 1


def forward_kernel(
    rows,
    n_others,
    lim_ref,
    me_ref,
    table_ref,
    fade_ref,
    masked_ref,
    value_ref,
    a_ref,
    c_ref,
    *refs,
):
    others, refs = refs[:n_others], refs[n_others:]
    (
        far,
        omega,
        wmix,
        qk,
        mask,
        whid,
        x,
        gain,
        wup,
        wdown,
        cot,
        out_ref,
        carry_ref,
        pre_ref,
        mixlow_ref,
        mixed_ref,
        probs_ref,
        att_ref,
        gated_ref,
        candpre_ref,
        gres_ref,
        ggain_ref,
        keep_ref,
        send_ref,
        m_ref,
        part_ref,
        up_ref,
        gdown_ref,
        gup_ref,
    ) = refs
    masked = masked_ref[...].astype(F32)
    m_ref[...] = masked
    if n_others == 1:
        carry_ref[...] = others[0][...].astype(F32)
    else:
        carry_ref[...] = carried(rows, 1, me_ref[0], others, fade_ref)
    a = (a_ref[0:8, :], a_ref[8:16, :])
    c = (c_ref[0:8, :], c_ref[8:16, :])

    def step(g, s):
        for k in range(8):
            t = g * 8 + k
            row = row8(m_ref, t)
            s = tuple(a[i] * s[i] + row for i in range(2))
            put8(part_ref, t, rows, c[0] * s[0] + c[1] * s[1])
        return s

    lax.fori_loop(0, rows // 8, step, (carry_ref[0:8, :], carry_ref[8:16, :]))
    fold8(part_ref, pre_ref, rows)
    pre = pre_ref[...] + far()[...] + omega()[...] * masked
    pre_ref[...] = pre
    mix_low = (pre * sigmoid(pre)).astype(BF16)
    mixlow_ref[...] = mix_low
    mixed_ref[...] = dot(mix_low, wmix()[...])
    shared_pre = mixed_ref[:, D : D + Z]
    shared = shared_pre * sigmoid(shared_pre)
    qk_ref, mask_ref = qk(), mask()
    query = (shared * qk_ref[0:1, :] + qk_ref[1:2, :]).astype(BF16)
    key = (shared * qk_ref[2:3, :]).astype(BF16)
    places = lax.broadcasted_iota(jnp.int32, (BLOCK, BLOCK), 0)
    others = lax.broadcasted_iota(jnp.int32, (BLOCK, BLOCK), 1)
    for g in range(rows // BLOCK):
        lo = g * BLOCK
        ok = (mask_ref[:, lo : lo + BLOCK] > 0) & (
            lax.broadcasted_iota(jnp.int32, (1, BLOCK), 1) + lo < lim_ref[0]
        )
        ok = jnp.broadcast_to(ok.astype(F32), (BLOCK, BLOCK)) > 0.5
        allowed = (places == others) | ((places > others) & ok)
        scores = dot_nt(query[lo : lo + BLOCK], key[lo : lo + BLOCK]) * (Z**-0.5)
        scores = jnp.where(allowed, scores, -1000000000.0)
        grown = jnp.exp(scores - jnp.max(scores, axis=1, keepdims=True))
        probs = grown / jnp.sum(grown, axis=1, keepdims=True)
        probs_ref[lo : lo + BLOCK, :] = probs
        att_ref[lo : lo + BLOCK, :] = dot(probs.astype(BF16), value_ref[lo : lo + BLOCK, :])
    reset_pre = mixed_ref[:, D + Z : D + Z + V]
    gated = (att_ref[...] * (reset_pre * sigmoid(reset_pre))).astype(BF16)
    gated_ref[...] = gated
    cand_pre = mixed_ref[:, D + Z + V :] + dot(gated, whid()[...])
    candpre_ref[...] = cand_pre
    cand = cand_pre * sigmoid(cand_pre)
    x = x()[...].astype(F32)
    resid = x + sigmoid(mixed_ref[:, :D]) * (cand - x)
    center = jnp.mean(resid, axis=1, keepdims=True)
    shifted = resid - center
    inv = lax.rsqrt(jnp.mean(shifted * shifted, axis=1, keepdims=True) + 1e-05)
    unit = shifted * inv
    gain = gain()[...]
    ffn_low = (unit * gain).astype(BF16)
    up_ref[...] = dot(ffn_low, wup()[...])
    up = up_ref[...]
    sig = sigmoid(up)
    inner = (up * sig).astype(BF16)
    out_ref[...] = (resid + dot(inner, wdown()[...])).astype(BF16)
    cot = cot()[...]
    gdown_ref[...] = dot_tn(inner, cot).astype(BF16)
    gup_low = (dot_nt(cot, wdown()[...]) * (sig * (1.0 + up * (1.0 - sig)))).astype(BF16)
    gup_ref[...] = dot_tn(ffn_low, gup_low).astype(BF16)
    g_ffn = dot_nt(gup_low, wup()[...])
    ggain_ref[...] = jnp.sum(g_ffn * unit, axis=0, keepdims=True)
    e = g_ffn * gain
    g_norm = inv * (
        e
        - jnp.mean(e, axis=1, keepdims=True)
        - unit * jnp.mean(e * unit, axis=1, keepdims=True)
    )
    gres_ref[...] = cot.astype(F32) + g_norm
    pack(table_ref, keep_ref, send_ref, 0, gdown_ref, FF // PIECES)
    pack(table_ref, keep_ref, send_ref, 8, gup_ref, D // PIECES)


def slope(v, sig):
    return sig * (1.0 + v * (1.0 - sig))


def gates_kernel(
    table_ref,
    x,
    whid,
    mixlow_ref,
    mixed_ref,
    att_ref,
    gated_ref,
    candpre_ref,
    gres_ref,
    keep_ref,
    send_ref,
    gskip_ref,
    gupd_ref,
    ghid_ref,
    greset_ref,
    gatt_ref,
    whid_grad_ref,
    wmix_grad_ref,
    wreset_grad_ref,
):
    x = x()[...].astype(F32)
    g_resid = gres_ref[...]
    update = sigmoid(mixed_ref[:, :D])
    cand_pre = candpre_ref[...]
    sig = sigmoid(cand_pre)
    g_update = g_resid * update
    g_hid = (g_update * slope(cand_pre, sig)).astype(BF16)
    ghid_ref[...] = g_hid
    gskip_ref[...] = g_resid - g_update
    gupd_ref[...] = (g_update * (1.0 - update) * (cand_pre * sig - x)).astype(BF16)
    whid_grad_ref[...] = dot_tn(gated_ref[...], g_hid).astype(BF16)
    wmix_grad_ref[:, :D] = dot_tn(mixlow_ref[...], gupd_ref[...]).astype(BF16)
    wmix_grad_ref[:, D:] = dot_tn(mixlow_ref[...], g_hid).astype(BF16)
    g_gated = dot_nt(g_hid, whid()[...])
    reset_pre = mixed_ref[:, D + Z : D + Z + V]
    sig = sigmoid(reset_pre)
    gatt_ref[...] = (g_gated * (reset_pre * sig)).astype(BF16)
    greset_ref[...] = (g_gated * att_ref[...] * slope(reset_pre, sig)).astype(BF16)
    wreset_grad_ref[...] = dot_tn(mixlow_ref[...], greset_ref[...]).astype(BF16)
    pack(table_ref, keep_ref, send_ref, 0, whid_grad_ref, V // PIECES)
    pack(table_ref, keep_ref, send_ref, 8, wmix_grad_ref, D // PIECES)
    pack(table_ref, keep_ref, send_ref, 16, wreset_grad_ref, D // PIECES)


def attention_kernel(
    rows,
    table_ref,
    normed_ref,
    valuepre_ref,
    value_ref,
    mixlow_ref,
    mixed_ref,
    probs_ref,
    gatt_ref,
    wvalue_ref,
    qk,
    keep_ref,
    send_ref,
    gqk_ref,
    gshared_ref,
    gnorm_ref,
    wvalue_grad_ref,
    wshared_grad_ref,
):
    qk_ref = qk()
    shared_pre = mixed_ref[:, D : D + Z]
    ssig = sigmoid(shared_pre)
    shared = shared_pre * ssig
    query = (shared * qk_ref[0:1, :] + qk_ref[1:2, :]).astype(BF16)
    key = (shared * qk_ref[2:3, :]).astype(BF16)
    g_query, g_key, g_value = [], [], []
    for g in range(rows // BLOCK):
        part = slice(g * BLOCK, (g + 1) * BLOCK)
        probs = probs_ref[part, :]
        g_probs = dot_nt(gatt_ref[part, :], value_ref[part, :])
        g_value.append(dot_tn(probs.astype(BF16), gatt_ref[part, :]))
        inner = jnp.sum(g_probs * probs, axis=1, keepdims=True)
        g_scores = (probs * (g_probs - inner) * (Z**-0.5)).astype(BF16)
        g_query.append(dot(g_scores, key[part]))
        g_key.append(dot_tn(g_scores, query[part]))
    g_query = jnp.concatenate(g_query, axis=0)
    g_key = jnp.concatenate(g_key, axis=0)
    g_value = jnp.concatenate(g_value, axis=0)
    gqk_ref[0:1, :] = jnp.sum(g_query * shared, axis=0, keepdims=True)
    gqk_ref[1:2, :] = jnp.sum(g_query, axis=0, keepdims=True)
    gqk_ref[2:3, :] = jnp.sum(g_key * shared, axis=0, keepdims=True)
    g_shared = g_query * qk_ref[0:1, :] + g_key * qk_ref[2:3, :]
    gshared_ref[...] = (g_shared * slope(shared_pre, ssig)).astype(BF16)
    wshared_grad_ref[...] = dot_tn(mixlow_ref[...], gshared_ref[...]).astype(BF16)
    value_pre = valuepre_ref[...]
    vsig = sigmoid(value_pre)
    g_vpre = (g_value * slope(value_pre, vsig)).astype(BF16)
    wvalue_grad_ref[...] = dot_tn(normed_ref[...], g_vpre).astype(BF16)
    gnorm_ref[...] = dot_nt(g_vpre, wvalue_ref[...])
    pack(table_ref, keep_ref, send_ref, 0, wvalue_grad_ref, D // PIECES)
    pack(table_ref, keep_ref, send_ref, 8, wshared_grad_ref, D // PIECES)


SMALL = 4 * H + 4


def tables_kernel(
    rows,
    table_ref,
    keep_in_ref,
    send_in_ref,
    masked_ref,
    normed_ref,
    pre_ref,
    gupd_ref,
    gshared_ref,
    greset_ref,
    ghid_ref,
    gnorm_ref,
    gqk_ref,
    gffn_ref,
    carry_ref,
    a_ref,
    c_ref,
    wmix,
    far,
    expand,
    alpha,
    delta,
    eta,
    gain,
    keep_ref,
    send_ref,
    gpre_ref,
    adj_ref,
    m_ref,
    small_ref,
):
    wmix_ref = wmix()
    m_ref[...] = masked_ref[...].astype(F32)
    pre = pre_ref[...]
    psig = sigmoid(pre)
    g_mix_low = dot_nt(gupd_ref[...], wmix_ref[:, :D])
    g_mix_low += dot_nt(gshared_ref[...], wmix_ref[:, D : D + Z])
    g_mix_low += dot_nt(greset_ref[...], wmix_ref[:, D + Z : D + Z + V])
    g_mix_low += dot_nt(ghid_ref[...], wmix_ref[:, D + Z + V :])
    g_pre = g_mix_low * slope(pre, psig)
    gpre_ref[...] = g_pre
    a = (a_ref[0:8, :], a_ref[8:16, :])

    def step(g, carry):
        s, q, dc, dq, m = carry
        for k in range(8):
            t = g * 8 + k
            row = row8(m_ref, t)
            grad = row8(gpre_ref, t)
            late = row8(gpre_ref, rows - 1 - t)
            grown = tuple(a[i] * s[i] for i in range(2))
            q = tuple(a[i] * q[i] + grown[i] for i in range(2))
            s = tuple(grown[i] + row for i in range(2))
            dc = tuple(dc[i] + grad * s[i] for i in range(2))
            dq = tuple(dq[i] + grad * q[i] for i in range(2))
            m = tuple(a[i] * (m[i] + late) for i in range(2))
        return s, q, dc, dq, m

    zero = jnp.zeros((8, D), F32)
    _, _, dc, dq, m = lax.fori_loop(
        0,
        rows // 8,
        step,
        (
            (carry_ref[0:8, :], carry_ref[8:16, :]),
            (carry_ref[16:24, :], carry_ref[24:32, :]),
            (zero, zero),
            (zero, zero),
            (zero, zero),
        ),
    )
    adj_ref[0:8, :] = m[0].astype(BF16)
    adj_ref[8:16, :] = m[1].astype(BF16)
    far_ref = far()
    g_coeff = jnp.concatenate(dc, axis=0) + far_ref[0:H, :]
    expand, eta = expand()[...], eta()[...]
    alpha, delta = sigmoid(alpha()[...]), sigmoid(delta()[...])
    g_log = (c_ref[...] * jnp.concatenate(dq, axis=0) + far_ref[H:, :]) / a_ref[...]
    g_expand = g_coeff * (eta * alpha)
    g_eta = g_coeff * (alpha * expand)
    g_alpha = (g_coeff * (eta * expand) - g_log * delta) * (alpha * (1.0 - alpha))
    g_delta = -(g_log * alpha) * (delta * (1.0 - delta))
    small_ref[...] = jnp.zeros_like(small_ref)
    for i, part in enumerate((g_expand, g_alpha, g_delta, g_eta)):
        for j in range(D // LANES):
            at = (i * 4 + j) * H
            small_ref[at : at + H, :] = part[:, j * LANES : (j + 1) * LANES]
    g_gain = jnp.sum(
        g_pre * pre + normed_ref[...].astype(F32) * gnorm_ref[...], axis=0, keepdims=True
    ) / gain()[...]
    g_omega = jnp.sum(g_pre * m_ref[...], axis=0, keepdims=True)
    for i, part in enumerate((g_gain, g_omega, gffn_ref[...])):
        for j in range(D // LANES):
            at = 16 * H + j * H + i
            small_ref[at : at + 1, :] = part[:, j * LANES : (j + 1) * LANES]
    for j in range(3):
        at = 16 * H + j * H + 3
        small_ref[at : at + 1, :] = gqk_ref[j : j + 1, :]
    for pos in range(PIECES):
        src, dst = (keep_in_ref, keep_ref) if pos < PIECES // 2 else (send_in_ref, send_ref)
        slot = pos % (PIECES // 2)
        row = pl.multiple_of(table_ref[pos] * 16, 16)
        dst[slot, : 9 * 16, :] = src[slot]
        dst[slot, 9 * 16 :, :] = small_ref[pl.ds(row, 16), :].astype(BF16)


def input_kernel(
    rows,
    n_others,
    lim_ref,
    me_ref,
    fade_ref,
    gpre_ref,
    gskip_ref,
    gnorm_ref,
    a_ref,
    c_ref,
    *refs,
):
    others, refs = refs[:n_others], refs[n_others:]
    x, far, omega, gain, din_ref, part_ref, gx_ref = refs
    if n_others == 1:
        adjoint = others[0][...].astype(F32)
    else:
        adjoint = carried(rows, -1, me_ref[0], others, fade_ref)
    a = (a_ref[0:8, :], a_ref[8:16, :])
    c = (c_ref[0:8, :], c_ref[8:16, :])

    def back(g, m):
        for k in range(8):
            t = rows - 1 - (g * 8 + k)
            row = row8(gpre_ref, t)
            lam = tuple(m[i] + row for i in range(2))
            put8(part_ref, t, rows, c[0] * lam[0] + c[1] * lam[1])
            m = tuple(a[i] * lam[i] for i in range(2))
        return m

    lax.fori_loop(0, rows // 8, back, (adjoint[0:8, :], adjoint[8:16, :]))
    fold8(part_ref, gx_ref, rows)
    g_masked = gx_ref[...] + far()[...] + omega()[...] * gpre_ref[...]
    place = lax.broadcasted_iota(jnp.int32, (rows, 1), 0)
    e = jnp.where(place < lim_ref[0], g_masked, 0.0) + gnorm_ref[...]
    x = x()[...].astype(F32)
    shifted = x - jnp.mean(x, axis=1, keepdims=True)
    inv = lax.rsqrt(jnp.mean(shifted * shifted, axis=1, keepdims=True) + 1e-05)
    unit = shifted * inv
    e = e * gain()[...]
    g_in = inv * (
        e
        - jnp.mean(e, axis=1, keepdims=True)
        - unit * jnp.mean(e * unit, axis=1, keepdims=True)
    )
    din_ref[...] = (g_in + gskip_ref[...]).astype(BF16)


def unpack(table_ref, mine_ref, other_ref, segments, sem):
    copies = []
    for pos in range(PIECES):
        src = mine_ref if pos < PIECES // 2 else other_ref
        slot = pos % (PIECES // 2)
        piece = table_ref[pos]
        for at, piece_rows, cols, buffer_ref, out_ref, col in segments:
            row = pl.multiple_of(piece * piece_rows, 16)
            tile = at
            for r in range(piece_rows // 16):
                for c in range(cols // 128):
                    buffer_ref[
                        pos * piece_rows + r * 16 : pos * piece_rows + r * 16 + 16,
                        c * 128 : c * 128 + 128,
                    ] = src[slot, tile * 16 : tile * 16 + 16, :].astype(F32)
                    tile += 1
            copy = pltpu.make_async_copy(
                buffer_ref.at[pl.ds(pos * piece_rows, piece_rows), :],
                out_ref.at[pl.ds(row, piece_rows), pl.ds(col, cols)],
                sem.at[len(copies)],
            )
            copy.start()
            copies.append(copy)
    return copies


def unpack_ffn(table_ref, mine_ref, other_ref, down_ref, up_ref, down_buf, up_buf, sem):
    copies = unpack(
        table_ref,
        mine_ref,
        other_ref,
        [
            (0, FF // PIECES, D, down_buf, down_ref, 0),
            (8, D // PIECES, FF, up_buf, up_ref, 0),
        ],
        sem,
    )
    for copy in copies:
        copy.wait()


def unpack_gates(
    table_ref, mine_ref, other_ref, hid_ref, mix_ref, hid_buf, upd_buf, in_buf, reset_buf, sem
):
    rows = D // PIECES
    copies = unpack(
        table_ref,
        mine_ref,
        other_ref,
        [
            (0, V // PIECES, D, hid_buf, hid_ref, 0),
            (8, rows, D, upd_buf, mix_ref, 0),
            (12, rows, D, in_buf, mix_ref, D + Z + V),
            (16, rows, V, reset_buf, mix_ref, D + Z),
        ],
        sem,
    )
    for copy in copies:
        copy.wait()


def unpack_rest(
    table_ref,
    mine_ref,
    other_ref,
    mix_in_ref,
    mix_ref,
    value_ref,
    expand_ref,
    alpha_ref,
    delta_ref,
    eta_ref,
    gain_ref,
    omega_ref,
    ffn_ref,
    qk_ref,
    value_buf,
    shared_buf,
    small_ref,
    sem,
):
    rows = D // PIECES
    copies = unpack(
        table_ref,
        mine_ref,
        other_ref,
        [
            (0, rows, V, value_buf, value_ref, 0),
            (8, rows, Z, shared_buf, mix_ref, D),
        ],
        sem,
    )
    for pos in range(PIECES):
        src = mine_ref if pos < PIECES // 2 else other_ref
        row = pl.multiple_of(table_ref[pos] * 16, 16)
        small_ref[pl.ds(row, 16), :] = src[pos % (PIECES // 2), 9 * 16 : 10 * 16, :].astype(F32)
    for i, out_ref in enumerate((expand_ref, alpha_ref, delta_ref, eta_ref)):
        for j in range(D // LANES):
            at = (i * 4 + j) * H
            out_ref[:, j * LANES : (j + 1) * LANES] = small_ref[at : at + H, :]
    for i, out_ref in enumerate((gain_ref, omega_ref, ffn_ref)):
        for j in range(D // LANES):
            at = 16 * H + j * H + i
            out_ref[:, j * LANES : (j + 1) * LANES] = small_ref[at : at + 1, :]
    for j in range(3):
        at = 16 * H + j * H + 3
        qk_ref[j : j + 1, :] = small_ref[at : at + 1, :]
    for copy in copies:
        copy.wait()


def exchanges(batches, seqs):
    def pairs(turn):
        out = []
        for b in range(batches):
            for s in range(seqs):
                nb, ns = turn(b, s)
                out.append((b * seqs + s, nb * seqs + ns))
        return out

    halving = [
        pairs(lambda b, s: (b ^ 1, s)),
        pairs(lambda b, s: (b, s ^ 1) if b & 1 else (b ^ 2, s)),
        pairs(lambda b, s: (b ^ 2, s) if b & 1 else (b, s ^ 1)),
        pairs(lambda b, s: (b, s ^ 2)),
    ]
    whole = []
    bit = 4
    while bit < seqs:
        whole.append(pairs(lambda b, s, bit=bit: (b, s ^ bit)))
        bit *= 2
    return halving, whole


def piece_table():
    b, s = lax.axis_index("batch"), lax.axis_index("seq")
    pos = jnp.arange(PIECES, dtype=jnp.int32)
    core = (b & 1) ^ (pos >> 4)
    one, two = (pos >> 3) & 1, (pos >> 2) & 1
    x = ((b >> 1) & 1) ^ jnp.where(core == 0, one, two)
    y = (s & 1) ^ jnp.where(core == 0, two, one)
    z = ((s >> 1) & 1) ^ ((pos >> 1) & 1)
    return core * 16 + x * 8 + y * 4 + z * 2 + (pos & 1)


def add_low(left, right):
    return (left.astype(F32) + right.astype(F32)).astype(BF16)


def tied(token, *arrays):
    return lax.optimization_barrier((token,) + arrays)[1:]


class Summed:
    def __init__(self, keep, send, halving, whole):
        self.keep, self.send, self.halving, self.whole = keep, send, halving, whole

    def first(self):
        self.came = lax.ppermute(self.send, AXES, self.halving[0])

    def halve(self, level, token):
        half = self.keep.shape[0] // 2
        keep, came = tied(token, self.keep, self.came)
        self.send = add_low(keep[half:], came[half:])
        self.keep = add_low(keep[:half], came[:half])
        self.came = lax.ppermute(self.send, AXES, self.halving[level])
        return self.send

    def exchange(self, token):
        keep, came = tied(token, self.keep, self.came)
        now = add_low(keep, came)
        for stage in self.whole[:-1]:
            now = add_low(now, lax.ppermute(now, AXES, stage))
        self.came = lax.ppermute(now, AXES, self.whole[-1])
        self.now = now
        return now

    def turn(self, token):
        now, came = tied(token, self.now, self.came)
        self.now = add_low(now, came)
        self.came = lax.ppermute(self.now, AXES, self.halving[-1])
        return self.now

    def double(self, level, token):
        now, came = tied(token, self.now, self.came)
        self.now = jnp.concatenate([now, came], axis=0)
        self.came = lax.ppermute(self.now, AXES, self.halving[level])
        return self.now


def shifted_pairs(seqs, by):
    return [(i, i + by) for i in range(seqs) if 0 <= i + by < seqs]


def state_powers(seqs, own_len):
    reach = WINDOW // own_len
    if by_levels(own_len):
        return [float(own_len << i) for i in range(seqs.bit_length() - 1)]
    return [float(own_len * i) for i in range(min(seqs, reach))]


def by_levels(own_len):
    seqs = lax.axis_size("seq")
    return seqs & (seqs - 1) == 0 and 4 <= seqs <= WINDOW // own_len


class States:
    def __init__(self, state, fades, me, own_len, direction):
        self.group, self.fades, self.me = state, fades, me
        self.own_len, self.direction = own_len, direction
        self.others = []

    def level(self, i, token=None):
        seqs = lax.axis_size("seq")
        if i > 0:
            other = self.others[-1]
            if token is not None:
                (other,) = tied(token, other)
            (self.group,) = call(
                functools.partial(join_kernel, self.own_len, i - 1, self.direction),
                [("v", self.group.shape, BF16)],
                [("s", self.me), ("v", self.group), ("v", other), ("v", self.fades)],
                vmem=4,
                flops=10**8,
            )
        elif token is not None:
            (self.group,) = tied(token, self.group)
        pairs = [(j, j ^ (1 << i)) for j in range(seqs)]
        self.others.append(lax.ppermute(self.group, "seq", pairs))
        return self.group

    def direct(self):
        seqs = lax.axis_size("seq")
        total = jnp.zeros(self.group.shape, F32)
        for k in range(1, min(seqs, WINDOW // self.own_len)):
            far = lax.ppermute(self.group, "seq", shifted_pairs(seqs, k * self.direction))
            fade = self.fades[k - 1]
            total = total + moved(far.astype(F32), fade, float((k - 1) * self.own_len))
        self.others.append(total)
        return total


def far_part(signal, log_decay, coeff):
    own_len = signal.shape[0]
    steps = jnp.arange(own_len).astype(F32)[:, None, None]
    held = jnp.exp(log_decay[None] * (WINDOW - 1.0 - steps)) * signal[:, None, :]
    after = lax.cumsum(held, axis=0, reverse=True) - held
    return jnp.sum(coeff[None] * jnp.exp(log_decay[None] * (steps + 1.0)) * after, axis=1)


def out_sems(n):
    return pltpu.SemaphoreType.DMA((n * PIECES,))


def finish(who, given, results):
    if who == "A":
        return call(
            unpack_ffn,
            [("o", (FF, D), F32), ("o", (D, FF), F32)],
            given,
            [pltpu.VMEM((FF, D), F32), pltpu.VMEM((D, FF), F32), out_sems(2)],
            vmem=VMEM_OUT,
        )
    if who == "B":
        return call(
            unpack_gates,
            [("o", (V, D), F32), ("o", (D, MIX), F32)],
            given,
            [
                pltpu.VMEM((V, D), F32),
                pltpu.VMEM((D, D), F32),
                pltpu.VMEM((D, D), F32),
                pltpu.VMEM((D, V), F32),
                out_sems(4),
            ],
            vmem=VMEM_OUT,
        )
    return call(
        unpack_rest,
        [("o", (D, MIX), F32), ("o", (D, V), F32)]
        + [("v", (H, D), F32)] * 4
        + [("v", (1, D), F32)] * 3
        + [("v", (3, Z), F32)],
        given + [("o", results["B"][1])],
        [
            pltpu.VMEM((D, V), F32),
            pltpu.VMEM((D, Z), F32),
            pltpu.VMEM((PIECES * 16, 128), F32),
            out_sems(2),
        ],
        vmem=VMEM_OUT,
        alias={3: 0},
    )


ORDER = (
    "Ah2 Bh2 e0 Ch1 Ah3 e1 Ch2 Ax Bh3 e2 At Ch3 Bx K Ad2 Cx Bt Ad1 Ct Bd2 Ad0 Cd2 Bd1 Au Cd1 Bd0 Bu Cd0 Cu"
).split()


def on_device(
    inputs,
    lengths,
    key_mask,
    norm_gain,
    ema_expand,
    ema_alpha,
    ema_delta,
    ema_eta,
    ema_omega,
    w_value,
    w_mix,
    qk_affine,
    w_hidden,
    ffn_gain,
    w_up,
    w_down,
    cotangent,
):
    _, rows, _ = inputs.shape
    seqs = lax.axis_size("seq")
    reach = WINDOW // rows
    halving, whole = exchanges(lax.axis_size("batch"), seqs)
    table = piece_table()
    limit = lengths - lax.axis_index("seq") * rows
    x = inputs.reshape(rows, D)
    cot = cotangent.reshape(rows, D)
    expand, alpha, delta, eta = ema_expand.T, ema_alpha.T, ema_delta.T, ema_eta.T
    omega = ema_omega.reshape(1, D)
    gain1 = norm_gain.reshape(1, D)
    gain2 = ffn_gain.reshape(1, D)
    powers = state_powers(seqs, rows)
    half = PIECES // 2
    me = jnp.full((1,), lax.axis_index("seq"), jnp.int32)

    def buffers(tiles):
        return [("v", (half, tiles * 16, 128), BF16)] * 2

    tall = rows * 8 * (D // LANES)
    normed, masked, state, decay, coeff, fades, w_value_near = call(
        functools.partial(norm_kernel, rows, powers),
        [
            ("v", (rows, D), BF16),
            ("v", (rows, D), BF16),
            ("v", (2 * H, D), BF16),
            ("v", (H, D), F32),
            ("v", (H, D), F32),
            ("v", (len(powers), H, D), F32),
            ("v", (D, V), BF16),
        ],
        [("s", limit)]
        + [("h", t) for t in (x, gain1, alpha, delta, expand, eta)]
        + [("o", w_value)],
        [pltpu.VMEM((rows, D), F32), pltpu.SemaphoreType.DMA],
        vmem=VMEM_NORM,
    )
    before = States(state, fades, me, rows, 1)
    if by_levels(rows):
        for i in range(len(powers)):
            before.level(i)
    else:
        before.direct()
    others = before.others
    far_here = seqs > reach
    far = jnp.zeros((1, D), F32)
    if far_here:
        behind = lax.ppermute(masked, "seq", shifted_pairs(seqs, reach)).astype(F32)
        far, far_pull = jax.vjp(far_part, behind, jnp.log(decay), coeff)
    value_pre, value_low = call(
        value_kernel,
        [("v", (rows, V), F32), ("v", (rows, V), BF16)],
        [("v", normed), ("v", w_value_near)],
        vmem=VMEM_VALUE,
    )
    (
        out,
        carry,
        pre,
        mix_low,
        mixed,
        probs,
        attended,
        gated,
        cand_pre,
        g_resid,
        g_ffn_gain,
        keep1,
        send1,
    ) = call(
        functools.partial(forward_kernel, rows, len(others)),
        [
            ("v", (rows, D), BF16),
            ("v", (2 * H, D), F32),
            ("v", (rows, D), F32),
            ("v", (rows, D), BF16),
            ("v", (rows, MIX), F32),
            ("v", (rows, BLOCK), F32),
            ("v", (rows, V), F32),
            ("v", (rows, V), BF16),
            ("v", (rows, D), F32),
            ("v", (rows, D), F32),
            ("v", (1, D), F32),
        ]
        + buffers(16),
        [("s", limit), ("s", me), ("s", table)]
        + [("v", t) for t in (fades, masked, value_low, decay, coeff, *others)]
        + [
            ("h", t)
            for t in (
                far,
                omega,
                w_mix,
                qk_affine,
                key_mask,
                w_hidden,
                x,
                gain2,
                w_up,
                w_down,
                cot,
            )
        ],
        [
            pltpu.VMEM((rows, D), F32),
            pltpu.VMEM((tall, LANES), F32),
            pltpu.VMEM((rows, FF), F32),
            pltpu.VMEM((FF, D), BF16),
            pltpu.VMEM((D, FF), BF16),
        ],
        vmem=VMEM_FORWARD,
        flops=8 * 10**9,
    )
    ffn = Summed(keep1, send1, halving, whole)
    ffn.first()
    keep2, send2, g_skip, g_upd, g_hid, g_reset, g_att = call(
        gates_kernel,
        buffers(24)
        + [
            ("v", (rows, D), F32),
            ("v", (rows, D), BF16),
            ("v", (rows, D), BF16),
            ("v", (rows, V), BF16),
            ("v", (rows, V), BF16),
        ],
        [("s", table), ("h", x), ("h", w_hidden)]
        + [("v", t) for t in (mix_low, mixed, attended, gated, cand_pre, g_resid)],
        [pltpu.VMEM((V, D), BF16), pltpu.VMEM((D, 2 * D), BF16), pltpu.VMEM((D, V), BF16)],
        vmem=VMEM_GATES,
        flops=3 * 10**9,
    )
    token = ffn.halve(1, g_skip)
    gates = Summed(keep2, send2, halving, whole)
    gates.first()
    (g_att,) = tied(token, g_att)
    keep3, send3, g_qk, g_shared, g_normed = call(
        functools.partial(attention_kernel, rows),
        buffers(9) + [("v", (3, Z), F32), ("v", (rows, Z), BF16), ("v", (rows, D), F32)],
        [("s", table)]
        + [
            ("v", t)
            for t in (
                normed,
                value_pre,
                value_low,
                mix_low,
                mixed,
                probs,
                g_att,
                w_value_near,
            )
        ]
        + [("h", qk_affine)],
        [pltpu.VMEM((D, V), BF16), pltpu.VMEM((D, Z), BF16)],
        vmem=VMEM_ATT,
        flops=3 * 10**9,
    )
    token = gates.halve(1, g_normed)
    (g_upd,) = tied(token, g_upd)
    g_far_tables = jnp.zeros((2 * H, D), F32)
    g_far = jnp.zeros((1, D), F32)
    if far_here:
        g_mixed = jnp.concatenate([g_upd, g_shared, g_reset, g_hid], axis=1)
        g_early = lax.dot_general(
            g_mixed, w_mix, (((1,), (1,)), ((), ())), preferred_element_type=F32
        )
        sig = jax.nn.sigmoid(pre)
        g_behind, far_log, far_coeff = far_pull(g_early * (sig * (1.0 + pre * (1.0 - sig))))
        g_far_tables = jnp.concatenate([far_coeff, far_log], axis=0)
        g_far = lax.ppermute(
            g_behind.astype(BF16), "seq", shifted_pairs(seqs, -reach)
        ).astype(F32)
    keep3, send3, g_pre, adjoint = call(
        functools.partial(tables_kernel, rows),
        buffers(10) + [("v", (rows, D), F32), ("v", (H, D), BF16)],
        [("s", table)]
        + [
            ("v", t)
            for t in (
                keep3,
                send3,
                masked,
                normed,
                pre,
                g_upd,
                g_shared,
                g_reset,
                g_hid,
                g_normed,
                g_qk,
                g_ffn_gain,
                carry,
                decay,
                coeff,
            )
        ]
        + [("h", t) for t in (w_mix, g_far_tables, expand, alpha, delta, eta, gain1)],
        [pltpu.VMEM((rows, D), F32), pltpu.VMEM((PIECES * 16, 128), F32)],
        vmem=VMEM_TABLES,
        flops=5 * 10**9,
    )
    rest = Summed(keep3, send3, halving, whole)
    rest.first()
    after = States(adjoint, fades, me, rows, -1)
    token = g_pre
    steps = ORDER if by_levels(rows) else [step for step in ORDER if step[0] != "e"]
    if not by_levels(rows):
        token = after.direct()
    chunks = {"A": ffn, "B": gates, "C": rest}
    results = {}
    for step in steps:
        who, what = step[0], step[1:]
        if who == "e":
            token = after.level(int(what), token)
        elif who == "K":
            (g_pre,) = tied(token, g_pre)
            (d_input,) = call(
                functools.partial(input_kernel, rows, len(after.others)),
                [("v", (rows, D), BF16)],
                [("s", limit), ("s", me)]
                + [("v", t) for t in (fades, g_pre, g_skip, g_normed, decay, coeff)]
                + [("v", t) for t in after.others]
                + [("h", t) for t in (x, g_far, omega, gain1)],
                [pltpu.VMEM((tall, LANES), F32), pltpu.VMEM((rows, D), F32)],
                vmem=VMEM_INPUT,
                flops=3 * 10**9,
            )
            token = d_input
        else:
            chunk = chunks[who]
            if what == "x":
                token = chunk.exchange(token)
            elif what == "t":
                token = chunk.turn(token)
            elif what[0] == "h":
                token = chunk.halve(int(what[1:]), token)
            elif what[0] == "d":
                token = chunk.double(int(what[1:]), token)
            else:
                now, came = tied(token, chunk.now, chunk.came)
                given = [("s", table), ("v", now), ("v", came)]
                results[who] = finish(who, given, results)
                token = results[who][0]
    grad_down, grad_up = results["A"]
    grad_hidden, _ = results["B"]
    (
        grad_mix,
        grad_value,
        g_expand,
        g_alpha,
        g_delta,
        g_eta,
        g_norm_gain,
        g_omega,
        g_ffn_gain,
        g_qk,
    ) = results["C"]
    return (
        out.reshape(inputs.shape),
        d_input.reshape(inputs.shape),
        g_norm_gain.reshape(D),
        g_expand.T,
        g_alpha.T,
        g_delta.T,
        g_eta.T,
        g_omega.reshape(D),
        grad_value,
        grad_mix,
        g_qk,
        grad_hidden,
        g_ffn_gain.reshape(D),
        grad_up,
        grad_down,
    )


def solution(mesh):
    row = P("batch", "seq", None)
    return jax.shard_map(
        on_device,
        mesh=mesh,
        in_specs=(row, P("batch"), P("batch", "seq")) + (P(),) * 13 + (row,),
        out_specs=(row, row) + (P(),) * 13,
        check_vma=False,
    )
```

```python
import functools

import jax
import jax.numpy as jnp
from jax import lax
from jax.experimental import pallas as pl
from jax.experimental.pallas import tpu as pltpu
from jax.sharding import PartitionSpec as P

D = 512
Z = 128
V = 1024
H = 16
FF = 1024
BLOCK = 128
WINDOW = 4096
MIX = 2 * D + Z + V
AXES = ("batch", "seq")
F32 = jnp.float32
BF16 = jnp.bfloat16
COSTS = {
    "norm_kernel": 10**9,
    "join_kernel": 10**9,
    "value_kernel": 10**9,
    "forward_kernel": 10**9,
    "gates_kernel": 10**9,
    "attention_kernel": 10**9,
    "tables_kernel": 10**9,
    "input_kernel": 10**9,
}
VMEM_LIMIT = 24 * 2**20


def sigmoid(v):
    return 1.0 / (1.0 + jnp.exp(-v))


def dot(a, b):
    return lax.dot_general(a, b, (((1,), (0,)), ((), ())), preferred_element_type=F32)


def dot_nt(a, b):
    return lax.dot_general(a, b, (((1,), (1,)), ((), ())), preferred_element_type=F32)


def dot_tn(a, b):
    return lax.dot_general(a, b, (((0,), (0,)), ((), ())), preferred_element_type=F32)


class Late:
    def __init__(self, copy, ref):
        self.copy, self.ref, self.waited = copy, ref, False

    def __call__(self):
        if not self.waited:
            self.copy.wait()
            self.waited = True
        return self.ref


SPACES = {"s": pltpu.SMEM, "v": pltpu.VMEM, "h": pltpu.HBM, "o": pltpu.HBM}


def call(body, outs, args, scratch=(), alias=None):
    late = [i for i, (kind, _) in enumerate(args) if kind == "h"]
    n_in, n_out = len(args), len(outs)

    def run(*refs):
        ins = list(refs[:n_in])
        mine = refs[n_in : n_in + n_out + len(scratch)]
        if late:
            rest = refs[n_in + n_out + len(scratch) :]
            for k, i in enumerate(late):
                copy = pltpu.make_async_copy(ins[i], rest[k], rest[-1].at[k])
                copy.start()
                ins[i] = Late(copy, rest[k])
        body(*ins, *mine)
        for i in late:
            ins[i]()

    name = getattr(body, "func", body).__name__
    buffers = [pltpu.VMEM(args[i][1].shape, args[i][1].dtype) for i in late]
    if late:
        buffers.append(pltpu.SemaphoreType.DMA((len(late),)))
    return pl.pallas_call(
        run,
        out_shape=[jax.ShapeDtypeStruct(shape, dtype) for _, shape, dtype in outs],
        in_specs=[pl.BlockSpec(memory_space=SPACES[kind]) for kind, _ in args],
        out_specs=[pl.BlockSpec(memory_space=SPACES[kind]) for kind, _, _ in outs],
        scratch_shapes=list(scratch) + buffers,
        input_output_aliases=alias or {},
        compiler_params=pltpu.CompilerParams(vmem_limit_bytes=VMEM_LIMIT),
        name=name,
        cost_estimate=pl.CostEstimate(flops=COSTS.get(name, 10**10), bytes_accessed=0, transcendentals=0),
    )(
        *[
            pltpu.with_memory_space_constraint(array, pltpu.HBM) if kind in "ho" else array
            for kind, array in args
        ]
    )


def row8(ref, t):
    return jnp.broadcast_to(ref[pl.ds(t, 1), :], (8, D))


LANES = 128


def put8(part_ref, t, rows, eight):
    for j in range(D // LANES):
        base = pl.multiple_of(j * rows * 8 + t * 8, 8)
        part_ref[pl.ds(base, 8), :] = eight[:, j * LANES : (j + 1) * LANES]


def fold8(part_ref, out_ref, rows):
    def one(g, _):
        at = pl.multiple_of(g * 8, 8)
        for j in range(D // LANES):
            base = pl.multiple_of(j * rows * 8 + g * 64, 64)
            acc = part_ref[pl.ds(base, 8, stride=8), :]
            for k in range(1, 8):
                acc = acc + part_ref[pl.ds(base + k, 8, stride=8), :]
            out_ref[pl.ds(at, 8), j * LANES : (j + 1) * LANES] = acc
        return 0

    lax.fori_loop(0, rows // 8, one, 0)


def norm_kernel(
    rows,
    powers,
    lim_ref,
    x,
    gain,
    alpha,
    delta,
    expand,
    eta,
    wvalue_ref,
    whid_ref,
    normed_ref,
    masked_ref,
    state_ref,
    a_ref,
    c_ref,
    fade_ref,
    wvalue_out_ref,
    whid_out_ref,
    m_ref,
    sem,
):
    copies = bring(((wvalue_ref, wvalue_out_ref), (whid_ref, whid_out_ref)), sem)
    x = x()[...].astype(F32)
    center = jnp.mean(x, axis=1, keepdims=True)
    shifted = x - center
    spread = jnp.mean(shifted * shifted, axis=1, keepdims=True)
    normed = (shifted * lax.rsqrt(spread + 1e-05) * gain()[...]).astype(BF16)
    normed_ref[...] = normed
    place = lax.broadcasted_iota(jnp.int32, (rows, 1), 0)
    masked = jnp.where(place < lim_ref[0], normed.astype(F32), 0.0)
    masked_ref[...] = masked.astype(BF16)
    m_ref[...] = masked
    alpha = sigmoid(alpha()[...])
    decay = 1.0 - alpha * sigmoid(delta()[...])
    a_ref[...] = decay
    c_ref[...] = eta()[...] * alpha * expand()[...]
    log_decay = jnp.log(decay)
    for i, power in enumerate(powers):
        fade_ref[i] = jnp.exp(log_decay * power)
    a = (decay[0:8, :], decay[8:16, :])

    def step(g, carry):
        s, q = carry
        for k in range(8):
            row = row8(m_ref, g * 8 + k)
            grown = tuple(a[i] * s[i] for i in range(2))
            q = tuple(a[i] * q[i] + grown[i] for i in range(2))
            s = tuple(grown[i] + row for i in range(2))
        return s, q

    zero = jnp.zeros((8, D), F32)
    s, q = lax.fori_loop(0, rows // 8, step, ((zero, zero), (zero, zero)))
    state_ref[0:8, :] = s[0].astype(BF16)
    state_ref[8:16, :] = s[1].astype(BF16)
    state_ref[16:24, :] = q[0].astype(BF16)
    state_ref[24:32, :] = q[1].astype(BF16)
    for copy in copies:
        copy.wait()


def bring(pairs, sem):
    copies = []
    for i, (src, dst) in enumerate(pairs):
        copy = pltpu.make_async_copy(src, dst, sem.at[i])
        copy.start()
        copies.append(copy)
    return copies


def value_kernel(
    normed_ref,
    wvalue_ref,
    wmix_ref,
    wup_ref,
    wdown_ref,
    pre_ref,
    low_ref,
    wmix_out_ref,
    wup_out_ref,
    wdown_out_ref,
    sem,
):
    copies = bring(
        ((wmix_ref, wmix_out_ref), (wup_ref, wup_out_ref), (wdown_ref, wdown_out_ref)), sem
    )
    for lo in range(0, V, D):
        pre = dot(normed_ref[...], wvalue_ref[:, lo : lo + D])
        pre_ref[:, lo : lo + D] = pre
        low_ref[:, lo : lo + D] = (pre * sigmoid(pre)).astype(BF16)
    for copy in copies:
        copy.wait()


def moved(state, fade, steps):
    if state.shape[0] == H:
        return fade * state
    return jnp.concatenate([fade * state[:H], fade * (state[H:] + steps * state[:H])], axis=0)


def joined(own_len, level, direction, me, group, other, fades):
    late = ((me >> level) & 1) == (1 if direction == 1 else 0)
    first, second = jnp.where(late, other, group), jnp.where(late, group, other)
    return (moved(first, fades[level], float(own_len << level)) + second).astype(BF16)


def join_kernel(own_len, level, me_ref, group_ref, other_ref, fade_ref, out_ref):
    group, other = group_ref[...].astype(F32), other_ref[...].astype(F32)
    out_ref[...] = joined(own_len, level, 1, me_ref[0], group, other, fade_ref)


def carried(own_len, direction, me, others, fades):
    total = None
    for i, other in enumerate(others):
        blocks = me if direction == 1 else ~me
        late = ((me >> i) & 1) == (1 if direction == 1 else 0)
        for j in range(i):
            on = ((blocks >> j) & 1) == 1
            other = jnp.where(on, moved(other, fades[j], float(own_len << j)), other)
        other = jnp.where(late, other, 0.0)
        total = other if total is None else total + other
    return total


def place(slots_ref, dst, side, at, grad):
    rows, cols = grad.shape
    piece = rows // 16
    for g in range(4):
        slot = slots_ref[1 + 4 * side + g]
        for z in range(4):
            tile = at
            for lo in range((g * 4 + z) * piece, (g * 4 + z + 1) * piece, 16):
                for c in range(0, cols, 128):
                    dst[slot, z, tile * 16 : tile * 16 + 16, :] = grad[lo : lo + 16, c : c + 128]
                    tile += 1


def outer(slots_ref, keep_ref, send_ref, at, left_ref, right):
    half = left_ref.shape[1] // 2
    for side, dst in enumerate((keep_ref, send_ref)):
        core = slots_ref[0] ^ side
        left = left_ref[:, pl.ds(pl.multiple_of(core * half, half), half)]
        place(slots_ref, dst, side, at, dot_tn(left, right).astype(BF16))


def forward_kernel(
    rows,
    n_others,
    has_far,
    lim_ref,
    me_ref,
    slots_ref,
    fade_ref,
    masked_ref,
    value_ref,
    a_ref,
    c_ref,
    wmix_ref,
    whid_ref,
    wup_ref,
    wdown_ref,
    *refs,
):
    others, refs = refs[:n_others], refs[n_others:]
    far, refs = (refs[0], refs[1:]) if has_far else (None, refs)
    (
        omega,
        qk,
        mask,
        x,
        gain,
        cot,
        out_ref,
        carry_ref,
        pre_ref,
        mixlow_ref,
        mixed_ref,
        probs_ref,
        att_ref,
        gated_ref,
        candpre_ref,
        gres_ref,
        ggain_ref,
        keep_ref,
        send_ref,
        m_ref,
        part_ref,
        up_ref,
        inner_ref,
        ffn_ref,
    ) = refs
    masked = masked_ref[...].astype(F32)
    m_ref[...] = masked
    if n_others == 1:
        carry_ref[...] = others[0][...].astype(F32)
    else:
        states = [ref[...].astype(F32) for ref in others]
        carry_ref[...] = carried(rows, 1, me_ref[0], states, fade_ref)
    a = (a_ref[0:8, :], a_ref[8:16, :])
    c = (c_ref[0:8, :], c_ref[8:16, :])

    def step(g, s):
        for k in range(8):
            t = g * 8 + k
            row = row8(m_ref, t)
            s = tuple(a[i] * s[i] + row for i in range(2))
            put8(part_ref, t, rows, c[0] * s[0] + c[1] * s[1])
        return s

    lax.fori_loop(0, rows // 8, step, (carry_ref[0:8, :], carry_ref[8:16, :]))
    fold8(part_ref, pre_ref, rows)
    pre = pre_ref[...] + omega()[...] * masked
    if has_far:
        pre = pre + far()[...]
    pre_ref[...] = pre
    mix_low = (pre * sigmoid(pre)).astype(BF16)
    mixlow_ref[...] = mix_low
    mixed_ref[...] = dot(mix_low, wmix_ref[...])
    shared_pre = mixed_ref[:, D : D + Z]
    shared = shared_pre * sigmoid(shared_pre)
    qk_ref, mask_ref = qk(), mask()
    query = (shared * qk_ref[0:1, :] + qk_ref[1:2, :]).astype(BF16)
    key = (shared * qk_ref[2:3, :]).astype(BF16)
    places = lax.broadcasted_iota(jnp.int32, (BLOCK, BLOCK), 0)
    others = lax.broadcasted_iota(jnp.int32, (BLOCK, BLOCK), 1)
    for g in range(rows // BLOCK):
        lo = g * BLOCK
        ok = (mask_ref[:, lo : lo + BLOCK] > 0) & (
            lax.broadcasted_iota(jnp.int32, (1, BLOCK), 1) + lo < lim_ref[0]
        )
        ok = jnp.broadcast_to(ok.astype(F32), (BLOCK, BLOCK)) > 0.5
        allowed = (places == others) | ((places > others) & ok)
        scores = dot_nt(query[lo : lo + BLOCK], key[lo : lo + BLOCK]) * (Z**-0.5)
        scores = jnp.where(allowed, scores, -1000000000.0)
        grown = jnp.exp(scores - jnp.max(scores, axis=1, keepdims=True))
        probs = grown / jnp.sum(grown, axis=1, keepdims=True)
        probs_ref[lo : lo + BLOCK, :] = probs
        att_ref[lo : lo + BLOCK, :] = dot(probs.astype(BF16), value_ref[lo : lo + BLOCK, :])
    reset_pre = mixed_ref[:, D + Z : D + Z + V]
    gated = (att_ref[...] * (reset_pre * sigmoid(reset_pre))).astype(BF16)
    gated_ref[...] = gated
    cand_pre = mixed_ref[:, D + Z + V :] + dot(gated, whid_ref[...])
    candpre_ref[...] = cand_pre
    cand = cand_pre * sigmoid(cand_pre)
    x = x()[...].astype(F32)
    resid = x + sigmoid(mixed_ref[:, :D]) * (cand - x)
    center = jnp.mean(resid, axis=1, keepdims=True)
    shifted = resid - center
    inv = lax.rsqrt(jnp.mean(shifted * shifted, axis=1, keepdims=True) + 1e-05)
    unit = shifted * inv
    gain = gain()[...]
    ffn_low = (unit * gain).astype(BF16)
    ffn_ref[...] = ffn_low
    up_ref[...] = dot(ffn_low, wup_ref[...])
    up = up_ref[...]
    sig = sigmoid(up)
    inner = (up * sig).astype(BF16)
    inner_ref[...] = inner
    out_ref[...] = (resid + dot(inner, wdown_ref[...])).astype(BF16)
    cot = cot()[...]
    outer(slots_ref, keep_ref, send_ref, 0, inner_ref, cot)
    gup_low = (dot_nt(cot, wdown_ref[...]) * (sig * (1.0 + up * (1.0 - sig)))).astype(BF16)
    outer(slots_ref, keep_ref, send_ref, 8, ffn_ref, gup_low)
    g_ffn = dot_nt(gup_low, wup_ref[...])
    ggain_ref[...] = jnp.sum(g_ffn * unit, axis=0, keepdims=True)
    e = g_ffn * gain
    g_norm = inv * (
        e
        - jnp.mean(e, axis=1, keepdims=True)
        - unit * jnp.mean(e * unit, axis=1, keepdims=True)
    )
    gres_ref[...] = cot.astype(F32) + g_norm


def slope(v, sig):
    return sig * (1.0 + v * (1.0 - sig))


def gates_kernel(
    slots_ref,
    x,
    whid_ref,
    mixlow_ref,
    mixed_ref,
    att_ref,
    gated_ref,
    candpre_ref,
    gres_ref,
    keep_ref,
    send_ref,
    gskip_ref,
    gupd_ref,
    ghid_ref,
    greset_ref,
    gatt_ref,
):
    g_resid = gres_ref[...]
    update = sigmoid(mixed_ref[:, :D])
    cand_pre = candpre_ref[...]
    sig = sigmoid(cand_pre)
    g_update = g_resid * update
    g_hid = (g_update * slope(cand_pre, sig)).astype(BF16)
    ghid_ref[...] = g_hid
    gskip_ref[...] = g_resid - g_update
    outer(slots_ref, keep_ref, send_ref, 0, gated_ref, g_hid)
    g_gated = dot_nt(g_hid, whid_ref[...])
    outer(slots_ref, keep_ref, send_ref, 12, mixlow_ref, g_hid)
    x = x()[...].astype(F32)
    g_upd = (g_update * (1.0 - update) * (cand_pre * sig - x)).astype(BF16)
    gupd_ref[...] = g_upd
    outer(slots_ref, keep_ref, send_ref, 8, mixlow_ref, g_upd)
    reset_pre = mixed_ref[:, D + Z : D + Z + V]
    sig = sigmoid(reset_pre)
    gatt_ref[...] = (g_gated * (reset_pre * sig)).astype(BF16)
    g_reset = (g_gated * att_ref[...] * slope(reset_pre, sig)).astype(BF16)
    greset_ref[...] = g_reset


def attention_kernel(
    rows,
    slots_ref,
    normed_ref,
    valuepre_ref,
    value_ref,
    mixlow_ref,
    mixed_ref,
    probs_ref,
    gatt_ref,
    greset_ref,
    wvalue_ref,
    qk,
    keep_ref,
    send_ref,
    gqk_ref,
    gshared_ref,
    gnorm_ref,
):
    qk_ref = qk()
    shared_pre = mixed_ref[:, D : D + Z]
    ssig = sigmoid(shared_pre)
    shared = shared_pre * ssig
    query = (shared * qk_ref[0:1, :] + qk_ref[1:2, :]).astype(BF16)
    key = (shared * qk_ref[2:3, :]).astype(BF16)
    g_query, g_key, g_value = [], [], []
    for g in range(rows // BLOCK):
        part = slice(g * BLOCK, (g + 1) * BLOCK)
        probs = probs_ref[part, :]
        g_probs = dot_nt(gatt_ref[part, :], value_ref[part, :])
        g_value.append(dot_tn(probs.astype(BF16), gatt_ref[part, :]))
        inner = jnp.sum(g_probs * probs, axis=1, keepdims=True)
        g_scores = (probs * (g_probs - inner) * (Z**-0.5)).astype(BF16)
        g_query.append(dot(g_scores, key[part]))
        g_key.append(dot_tn(g_scores, query[part]))
    g_query = jnp.concatenate(g_query, axis=0)
    g_key = jnp.concatenate(g_key, axis=0)
    g_value = jnp.concatenate(g_value, axis=0)
    gqk_ref[0:1, :] = jnp.sum(g_query * shared, axis=0, keepdims=True)
    gqk_ref[1:2, :] = jnp.sum(g_query, axis=0, keepdims=True)
    gqk_ref[2:3, :] = jnp.sum(g_key * shared, axis=0, keepdims=True)
    g_shared = g_query * qk_ref[0:1, :] + g_key * qk_ref[2:3, :]
    g_shared = (g_shared * slope(shared_pre, ssig)).astype(BF16)
    gshared_ref[...] = g_shared
    outer(slots_ref, keep_ref, send_ref, 8, mixlow_ref, g_shared)
    value_pre = valuepre_ref[...]
    vsig = sigmoid(value_pre)
    g_vpre = (g_value * slope(value_pre, vsig)).astype(BF16)
    outer(slots_ref, keep_ref, send_ref, 0, normed_ref, g_vpre)
    outer(slots_ref, keep_ref, send_ref, 9, mixlow_ref, greset_ref[...])
    gnorm_ref[...] = dot_nt(g_vpre, wvalue_ref[...])


SMALL = 4 * H + 4


def tables_kernel(
    rows,
    has_far,
    slots_ref,
    keep_in_ref,
    send_in_ref,
    masked_ref,
    normed_ref,
    pre_ref,
    gupd_ref,
    gshared_ref,
    greset_ref,
    ghid_ref,
    gnorm_ref,
    gqk_ref,
    gffn_ref,
    carry_ref,
    a_ref,
    c_ref,
    wmix_ref,
    *refs,
):
    far, refs = (refs[0], refs[1:]) if has_far else (None, refs)
    expand, alpha, delta, eta, gain, *refs = refs
    keep_ref, send_ref, gpre_ref, adj_ref, m_ref, small_ref = refs
    m_ref[...] = masked_ref[...].astype(F32)
    pre = pre_ref[...]
    psig = sigmoid(pre)
    g_mix_low = dot_nt(gupd_ref[...], wmix_ref[:, :D])
    g_mix_low += dot_nt(gshared_ref[...], wmix_ref[:, D : D + Z])
    g_mix_low += dot_nt(greset_ref[...], wmix_ref[:, D + Z : D + Z + V])
    g_mix_low += dot_nt(ghid_ref[...], wmix_ref[:, D + Z + V :])
    g_pre = g_mix_low * slope(pre, psig)
    gpre_ref[...] = g_pre
    a = (a_ref[0:8, :], a_ref[8:16, :])

    def step(g, carry):
        s, q, dc, dq, m = carry
        for k in range(8):
            t = g * 8 + k
            row = row8(m_ref, t)
            grad = row8(gpre_ref, t)
            late = row8(gpre_ref, rows - 1 - t)
            grown = tuple(a[i] * s[i] for i in range(2))
            q = tuple(a[i] * q[i] + grown[i] for i in range(2))
            s = tuple(grown[i] + row for i in range(2))
            dc = tuple(dc[i] + grad * s[i] for i in range(2))
            dq = tuple(dq[i] + grad * q[i] for i in range(2))
            m = tuple(a[i] * (m[i] + late) for i in range(2))
        return s, q, dc, dq, m

    zero = jnp.zeros((8, D), F32)
    _, _, dc, dq, m = lax.fori_loop(
        0,
        rows // 8,
        step,
        (
            (carry_ref[0:8, :], carry_ref[8:16, :]),
            (carry_ref[16:24, :], carry_ref[24:32, :]),
            (zero, zero),
            (zero, zero),
            (zero, zero),
        ),
    )
    adj_ref[0:8, :] = m[0].astype(BF16)
    adj_ref[8:16, :] = m[1].astype(BF16)
    g_coeff = jnp.concatenate(dc, axis=0)
    g_log = c_ref[...] * jnp.concatenate(dq, axis=0)
    if has_far:
        far_ref = far()
        g_coeff, g_log = g_coeff + far_ref[0:H, :], g_log + far_ref[H:, :]
    expand, eta = expand()[...], eta()[...]
    alpha, delta = sigmoid(alpha()[...]), sigmoid(delta()[...])
    g_log = g_log / a_ref[...]
    g_expand = g_coeff * (eta * alpha)
    g_eta = g_coeff * (alpha * expand)
    g_alpha = (g_coeff * (eta * expand) - g_log * delta) * (alpha * (1.0 - alpha))
    g_delta = -(g_log * alpha) * (delta * (1.0 - delta))
    small_ref[...] = jnp.zeros_like(small_ref)
    for i, part in enumerate((g_expand, g_alpha, g_delta, g_eta)):
        for j in range(D // LANES):
            at = (i * 4 + j) * H
            small_ref[at : at + H, :] = part[:, j * LANES : (j + 1) * LANES]
    g_gain = jnp.sum(
        g_pre * pre + normed_ref[...].astype(F32) * gnorm_ref[...], axis=0, keepdims=True
    ) / gain()[...]
    g_omega = jnp.sum(g_pre * m_ref[...], axis=0, keepdims=True)
    for i, part in enumerate((g_gain, g_omega, gffn_ref[...])):
        for j in range(D // LANES):
            at = 16 * H + j * H + i
            small_ref[at : at + 1, :] = part[:, j * LANES : (j + 1) * LANES]
    for j in range(3):
        at = 16 * H + j * H + 3
        small_ref[at : at + 1, :] = gqk_ref[j : j + 1, :]
    for side, (src, dst) in enumerate(((keep_in_ref, keep_ref), (send_in_ref, send_ref))):
        dst[:, :, : 17 * 16, :] = src[...]
        row = pl.multiple_of((slots_ref[0] ^ side) * 256, 256)
        place(slots_ref, dst, side, 17, small_ref[pl.ds(row, 256), :].astype(BF16))


def input_kernel(
    rows,
    n_others,
    has_far,
    lim_ref,
    me_ref,
    fade_ref,
    gpre_ref,
    gskip_ref,
    gnorm_ref,
    a_ref,
    c_ref,
    *refs,
):
    others, refs = refs[:n_others], refs[n_others:]
    far, refs = (refs[0], refs[1:]) if has_far else (None, refs)
    x, omega, gain, din_ref, part_ref, gx_ref = refs
    if n_others == 1:
        adjoint = others[0][...].astype(F32)
    else:
        adjoint = carried(rows, -1, me_ref[0], [state_in(ref) for ref in others], fade_ref)
    a = (a_ref[0:8, :], a_ref[8:16, :])
    c = (c_ref[0:8, :], c_ref[8:16, :])

    def back(g, m):
        for k in range(8):
            t = rows - 1 - (g * 8 + k)
            row = row8(gpre_ref, t)
            lam = tuple(m[i] + row for i in range(2))
            put8(part_ref, t, rows, c[0] * lam[0] + c[1] * lam[1])
            m = tuple(a[i] * lam[i] for i in range(2))
        return m

    lax.fori_loop(0, rows // 8, back, (adjoint[0:8, :], adjoint[8:16, :]))
    fold8(part_ref, gx_ref, rows)
    g_masked = gx_ref[...] + omega()[...] * gpre_ref[...]
    if has_far:
        g_masked = g_masked + far()[...]
    place = lax.broadcasted_iota(jnp.int32, (rows, 1), 0)
    e = jnp.where(place < lim_ref[0], g_masked, 0.0) + gnorm_ref[...]
    x = x()[...].astype(F32)
    shifted = x - jnp.mean(x, axis=1, keepdims=True)
    inv = lax.rsqrt(jnp.mean(shifted * shifted, axis=1, keepdims=True) + 1e-05)
    unit = shifted * inv
    e = e * gain()[...]
    g_in = inv * (
        e
        - jnp.mean(e, axis=1, keepdims=True)
        - unit * jnp.mean(e * unit, axis=1, keepdims=True)
    )
    din_ref[...] = (g_in + gskip_ref[...]).astype(BF16)


def unpack(slots_ref, sources, first, segments, sem):
    copies = []
    for at, rows, cols, buffer_ref, out_ref, col in segments:
        group, piece = rows // 8, rows // 32
        for side, src in sources:
            for slot in range(2):
                block = len(copies) % 4
                for z in range(4):
                    tile = at
                    for lo in range(z * piece, (z + 1) * piece, 16):
                        for c in range(0, cols, 128):
                            buffer_ref[block, lo : lo + 16, c : c + 128] = src[
                                slot, z, tile * 16 : tile * 16 + 16, :
                            ].astype(F32)
                            tile += 1
                place_of = slots_ref[9 + 4 * side + first + slot]
                row = pl.multiple_of(
                    (slots_ref[0] ^ side) * (rows // 2) + place_of * group, group
                )
                copy = pltpu.make_async_copy(
                    buffer_ref.at[block],
                    out_ref.at[pl.ds(row, group), pl.ds(col, cols)],
                    sem.at[len(copies)],
                )
                copy.start()
                copies.append(copy)
    return copies


def ffn_segments(down_buf, up_buf, down_ref, up_ref):
    return [(0, FF, D, down_buf, down_ref, 0), (8, D, FF, up_buf, up_ref, 0)]


def gates_segments(hid_buf, upd_buf, in_buf, hid_ref, mix_ref):
    return [
        (0, V, D, hid_buf, hid_ref, 0),
        (8, D, D, upd_buf, mix_ref, 0),
        (12, D, D, in_buf, mix_ref, D + Z + V),
    ]


def rest_segments(value_buf, shared_buf, reset_buf, mix_ref, value_ref):
    return [
        (0, D, V, value_buf, value_ref, 0),
        (8, D, Z, shared_buf, mix_ref, D),
        (9, D, V, reset_buf, mix_ref, D + Z),
    ]


def unpack_kernel(segments, n_out, n_given, first, slots_ref, mine_ref, twin_ref, *refs):
    refs = refs[n_given:]
    outs, refs = refs[:n_out], refs[n_out:]
    parts = segments(*refs[:-1], *outs)
    for copy in unpack(slots_ref, ((0, mine_ref), (1, twin_ref)), first, parts, refs[-1]):
        copy.wait()


def unpack_rest_kernel(
    slots_ref,
    mine_ref,
    twin_ref,
    early_ref,
    twin_early_ref,
    mix_in_ref,
    value_in_ref,
    mix_ref,
    value_ref,
    expand_ref,
    alpha_ref,
    delta_ref,
    eta_ref,
    gain_ref,
    omega_ref,
    ffn_ref,
    qk_ref,
    value_buf,
    shared_buf,
    reset_buf,
    small_ref,
    sem,
):
    parts = rest_segments(value_buf, shared_buf, reset_buf, mix_ref, value_ref)
    copies = unpack(slots_ref, ((0, mine_ref), (1, twin_ref)), 2, parts, sem)
    for side, pair in enumerate(((early_ref, mine_ref), (twin_early_ref, twin_ref))):
        for slot in range(4):
            place_of = slots_ref[9 + 4 * side + slot]
            row = pl.multiple_of((slots_ref[0] ^ side) * 256 + place_of * 64, 64)
            for z in range(4):
                small_ref[pl.ds(row + z * 16, 16), :] = pair[slot // 2][
                    slot % 2, z, 17 * 16 : 18 * 16, :
                ].astype(F32)
    for i, out_ref in enumerate((expand_ref, alpha_ref, delta_ref, eta_ref)):
        for j in range(D // LANES):
            at = (i * 4 + j) * H
            out_ref[:, j * LANES : (j + 1) * LANES] = small_ref[at : at + H, :]
    for i, out_ref in enumerate((gain_ref, omega_ref, ffn_ref)):
        for j in range(D // LANES):
            at = 16 * H + j * H + i
            out_ref[:, j * LANES : (j + 1) * LANES] = small_ref[at : at + 1, :]
    for j in range(3):
        at = 16 * H + j * H + 3
        qk_ref[j : j + 1, :] = small_ref[at : at + 1, :]
    for copy in copies:
        copy.wait()


def added(left, right):
    return (left.astype(F32) + right.astype(F32)).astype(BF16)


def plain_halve_kernel(level, me_ref, keep_ref, came_ref, send_ref, kept_ref):
    if level < 3:
        half = keep_ref.shape[0] // 2
        send_ref[...] = added(keep_ref[half:], came_ref[half:])
        kept_ref[...] = added(keep_ref[:half], came_ref[:half])
        return
    half = keep_ref.shape[1] // 2
    mine = (me_ref[0] >> 1) & 1
    other = pl.ds((1 - mine) * half, half)
    send_ref[0] = added(keep_ref[0, other], came_ref[0, other])
    own = pl.ds(mine * half, half)
    kept_ref[0] = added(keep_ref[0, own], came_ref[0, own])


def add_kernel(left_ref, right_ref, out_ref):
    out_ref[...] = added(left_ref[...], right_ref[...])


def add_start_kernel(left_ref, right_ref, out_ref):
    pieces, rows = out_ref.shape[1:3]
    for i in range(pieces):
        part = slice(i * rows, (i + 1) * rows)
        out_ref[0, i] = added(left_ref[part, :], right_ref[part, :])


def pair_kernel(me_ref, now_ref, came_ref, out_ref):
    half = now_ref.shape[1]
    mine = (me_ref[0] >> 1) & 1
    out_ref[0, pl.ds(mine * half, half)] = now_ref[0]
    out_ref[0, pl.ds((1 - mine) * half, half)] = came_ref[0]


def stack_kernel(now_ref, came_ref, out_ref):
    out_ref[0] = now_ref[0]
    out_ref[1] = came_ref[0]


STATE = 4 * H


def state_in(ref):
    if ref.shape[1] == D:
        return ref[...].astype(F32)
    base = ref.shape[0] - STATE
    return jnp.concatenate([ref[base + j * H : base + (j + 1) * H, :] for j in range(4)], axis=1).astype(F32)


def put_state(ref, state):
    base = ref.shape[0] - STATE
    for j in range(4):
        ref[base + j * H : base + (j + 1) * H, :] = state[:, j * LANES : (j + 1) * LANES].astype(BF16)


def halve_kernel(level, own_len, me_ref, core_ref, fade_ref, adj_ref, keep_ref, came_ref, *refs):
    groups, pieces, rows, _ = keep_ref.shape
    size = pieces * rows

    def sums(g, z0, zn):
        keep = keep_ref[g, pl.ds(z0, zn)].reshape(zn * rows, 128)
        if len(came_ref.shape) == 4:
            came = came_ref[g, pl.ds(z0, zn)].reshape(zn * rows, 128)
        else:
            start = g * size + z0 * rows
            came = came_ref[pl.ds(pl.multiple_of(start, 16), zn * rows), :]
        return added(keep, came)

    if level < 3:
        send_ref, kept_ref = refs
        put_state(send_ref, adj_ref[...].astype(F32))
        half = groups // 2
        for g in range(half):
            send_ref[g * size : (g + 1) * size, :] = sums(half + g, 0, pieces)
        for g in range(half):
            kept_ref[g] = sums(g, 0, pieces).reshape(pieces, rows, 128)
        return
    first_ref, send_ref, kept_ref, other_ref, group_ref = refs
    me = me_ref[0]
    mine = (me >> 1) & 1
    other = jnp.where(core_ref[0] == 1, state_in(first_ref), state_in(came_ref))
    other_ref[...] = other.astype(BF16)
    group = joined(own_len, 0, -1, me, adj_ref[...].astype(F32), other, fade_ref)
    group_ref[...] = group
    put_state(send_ref, group.astype(F32))
    half = pieces // 2
    send_ref[: half * rows, :] = sums(0, (1 - mine) * half, half)
    kept_ref[0] = sums(0, mine * half, half).reshape(half, rows, 128)


def exchange_kernel(own_len, me_ref, fade_ref, group_ref, keep_ref, came_ref, now_ref):
    _, pieces, rows, _ = keep_ref.shape
    keep = keep_ref[0].reshape(pieces * rows, 128)
    now_ref[: pieces * rows, :] = added(keep, came_ref[: pieces * rows, :])
    group, other = group_ref[...].astype(F32), state_in(came_ref)
    put_state(now_ref, joined(own_len, 1, -1, me_ref[0], group, other, fade_ref).astype(F32))


def exchanges(batches, seqs):
    def pairs(turn):
        out = []
        for b in range(batches):
            for s in range(seqs):
                nb, ns = turn(b, s)
                out.append((b * seqs + s, nb * seqs + ns))
        return out

    halving = [
        pairs(lambda b, s: (b ^ 1, s)),
        pairs(lambda b, s: (b, s ^ 1) if b & 1 else (b ^ 2, s)),
        pairs(lambda b, s: (b ^ 2, s) if b & 1 else (b, s ^ 1)),
        pairs(lambda b, s: (b, s ^ 2)),
    ]
    whole = []
    bit = 4
    while bit < seqs:
        whole.append(pairs(lambda b, s, bit=bit: (b, s ^ bit)))
        bit *= 2
    return halving, whole


def slot_table():
    b, s = lax.axis_index("batch"), lax.axis_index("seq")
    core, here = b & 1, ((b >> 1) & 1) * 2 + (s & 1)
    at = jnp.arange(17, dtype=jnp.int32)
    part, four = (at - 1) >> 2, (at - 1) & 3

    def swapped(v):
        return (v >> 1) | ((v & 1) << 1)

    turned = (core ^ (part & 1)) == 1
    slot = jnp.where(turned, swapped(four ^ here), four ^ here)
    group = jnp.where(turned, swapped(four) ^ here, four ^ here)
    return jnp.where(at == 0, core, jnp.where(part < 2, slot, group))


def tied(token, *arrays):
    return lax.optimization_barrier((token,) + arrays)[1:]


class Summed:
    def __init__(self, keep, send, halving, whole):
        self.keep, self.send, self.halving, self.whole = keep, send, halving, whole
        self.me = jnp.full((1,), lax.axis_index("seq"), jnp.int32)

    def first(self, token):
        (send,) = tied(token, self.send)
        self.came = lax.ppermute(send, AXES, self.halving[0])
        return send

    def halve(self, level, token):
        keep, came = tied(token, self.keep, self.came)
        groups, pieces, rows, _ = keep.shape
        shape = (groups // 2, pieces, rows, 128) if level < 3 else (1, pieces // 2, rows, 128)
        self.send, self.keep = call(
            functools.partial(plain_halve_kernel, level),
            [("v", shape, BF16)] * 2,
            [("s", self.me), ("v", keep), ("v", came)],
        )
        self.came = lax.ppermute(self.send, AXES, self.halving[level])
        return self.send

    def exchange(self, token):
        now = self.sum(self.keep, self.came, token)
        for stage in self.whole[:-1]:
            now = self.sum(now, lax.ppermute(now, AXES, stage), token)
        self.came = lax.ppermute(now, AXES, self.whole[-1])
        self.now = now
        return now

    def turn(self, token):
        self.now = self.sum(self.now, self.came, token)
        self.came = lax.ppermute(self.now, AXES, self.halving[-1])
        return self.now

    def sum(self, left, right, token):
        left, right = tied(token, left, right)
        return call(add_kernel, [("v", left.shape, BF16)], [("v", left), ("v", right)])[0]

    def double(self, level, token):
        now, came = tied(token, self.now, self.came)
        groups, pieces, rows, _ = now.shape
        if level == 2:
            (self.now,) = call(
                pair_kernel,
                [("v", (1, 2 * pieces, rows, 128), BF16)],
                [("s", self.me), ("v", now), ("v", came)],
            )
        else:
            (self.now,) = call(
                stack_kernel,
                [("v", (2, pieces, rows, 128), BF16)],
                [("v", now), ("v", came)],
            )
            self.twin = lax.ppermute(self.now, AXES, self.halving[0])
        self.came = lax.ppermute(self.now, AXES, self.halving[level])
        return self.now

    def last(self, token):
        (self.late,) = tied(token, self.came)
        self.late_twin = lax.ppermute(self.late, AXES, self.halving[0])
        return self.late


class SummedWithStates(Summed):
    def __init__(self, keep, send, halving, whole, adjoint, fades, own_len):
        super().__init__(keep, send, halving, whole)
        self.adjoint, self.fades, self.own_len = adjoint, fades, own_len
        self.core = jnp.full((1,), lax.axis_index("batch") & 1, jnp.int32)
        self.earlier = None

    def halve(self, level, token):
        keep, came = tied(token, self.keep, self.came)
        groups, pieces, rows, _ = keep.shape
        args = [("s", self.me), ("s", self.core)]
        args += [("v", t) for t in (self.fades, self.adjoint, keep, came)]
        if level < 3:
            kept = (groups // 2, pieces, rows, 128)
            extra = []
        else:
            kept = (1, pieces // 2, rows, 128)
            args.append(("v", self.earlier))
            extra = [("v", (H, D), BF16)] * 2
        sent = (kept[0] * kept[1] * rows + STATE, 128)
        self.send, self.keep, *states = call(
            functools.partial(halve_kernel, level, self.own_len),
            [("v", sent, BF16), ("v", kept, BF16)] + extra,
            args,
        )
        if states:
            self.others = [states[0]]
            self.group = states[1]
        self.earlier = came
        self.came = lax.ppermute(self.send, AXES, self.halving[level])
        return self.send

    def exchange(self, token):
        keep, came = tied(token, self.keep, self.came)
        self.others.append(came)
        _, pieces, rows, _ = keep.shape
        self.shape = keep.shape
        (self.now,) = call(
            functools.partial(exchange_kernel, self.own_len),
            [("v", (pieces * rows + STATE, 128), BF16)],
            [("s", self.me)] + [("v", t) for t in (self.fades, self.group, keep, came)],
        )
        self.came = lax.ppermute(self.now, AXES, self.whole[-1])
        return self.now

    def turn(self, token):
        now, came = tied(token, self.now, self.came)
        self.others.append(came)
        (self.now,) = call(
            add_start_kernel, [("v", self.shape, BF16)], [("v", now), ("v", came)]
        )
        self.came = lax.ppermute(self.now, AXES, self.halving[-1])
        return self.now


def shifted_pairs(seqs, by):
    return [(i, i + by) for i in range(seqs) if 0 <= i + by < seqs]


def state_powers(seqs, own_len):
    reach = WINDOW // own_len
    if by_levels(own_len):
        return [float(own_len << i) for i in range(seqs.bit_length() - 1)]
    return [float(own_len * i) for i in range(min(seqs, reach))]


def by_levels(own_len):
    return lax.axis_size("seq") == 8 and 8 <= WINDOW // own_len


def states_before(state, fades, me, own_len):
    if not by_levels(own_len):
        return [direct_states(state, fades, own_len, 1)]
    seqs = lax.axis_size("seq")
    group, others = state, []
    levels = seqs.bit_length() - 1
    for i in range(levels):
        others.append(lax.ppermute(group, "seq", [(j, j ^ (1 << i)) for j in range(seqs)]))
        if i < levels - 1:
            (group,) = call(
                functools.partial(join_kernel, own_len, i),
                [("v", state.shape, BF16)],
                [("s", me), ("v", group), ("v", others[-1]), ("v", fades)],
            )
    return others


def direct_states(state, fades, own_len, direction):
    seqs = lax.axis_size("seq")
    total = jnp.zeros(state.shape, F32)
    for k in range(1, min(seqs, WINDOW // own_len)):
        far = lax.ppermute(state, "seq", shifted_pairs(seqs, k * direction))
        total = total + moved(far.astype(F32), fades[k - 1], float((k - 1) * own_len))
    return total


def far_part(signal, log_decay, coeff):
    own_len = signal.shape[0]
    steps = jnp.arange(own_len).astype(F32)[:, None, None]
    held = jnp.exp(log_decay[None] * (WINDOW - 1.0 - steps)) * signal[:, None, :]
    after = lax.cumsum(held, axis=0, reverse=True) - held
    return jnp.sum(coeff[None] * jnp.exp(log_decay[None] * (steps + 1.0)) * after, axis=1)


def start_unpack(who, slots, chunk, results):
    segments, outs, scratch = PLANS[who]
    given = [("s", slots), ("v", chunk.now), ("v", chunk.twin)]
    alias = {}
    if who != "A" and "mix" in results:
        alias = {len(given): outs.index(MIX_OUT)}
        given.append(("o", results["mix"]))
    return call(
        functools.partial(unpack_kernel, segments, len(outs), len(alias), 0),
        outs,
        given,
        scratch(),
        alias=alias,
    )


def end_unpack(who, slots, chunk, results):
    given = [("s", slots), ("v", chunk.late), ("v", chunk.late_twin)]
    if who == "C":
        return call(
            unpack_rest_kernel,
            PLANS[who][1]
            + [("v", (H, D), F32)] * 4
            + [("v", (1, D), F32)] * 3
            + [("v", (3, Z), F32)],
            given
            + [("v", chunk.now), ("v", chunk.twin)]
            + [("o", results["mix"]), ("o", results["C"][1])],
            rest_buffers()[:-1] + [pltpu.VMEM((512, 128), F32), pltpu.SemaphoreType.DMA((12,))],
            alias={5: 0, 6: 1},
        )
    segments, outs, scratch = PLANS[who]
    before = list(results[who])
    if who != "A":
        before[outs.index(MIX_OUT)] = results["mix"]
    return call(
        functools.partial(unpack_kernel, segments, len(outs), len(outs), 2),
        outs,
        given + [("o", t) for t in before],
        scratch(),
        alias={3 + i: i for i in range(len(outs))},
    )


def wide(*shapes):
    buffers = [pltpu.VMEM((4, rows // 8, cols), F32) for rows, cols in shapes]
    return buffers + [pltpu.SemaphoreType.DMA((4 * len(shapes),))]


def rest_buffers():
    return wide((D, V), (D, Z), (D, V))


MIX_OUT = ("o", (D, MIX), F32)
PLANS = {
    "A": (
        ffn_segments,
        [("o", (FF, D), F32), ("o", (D, FF), F32)],
        lambda: wide((FF, D), (D, FF)),
    ),
    "B": (
        gates_segments,
        [("o", (V, D), F32), MIX_OUT],
        lambda: wide((V, D), (D, D), (D, D)),
    ),
    "C": (rest_segments, [MIX_OUT, ("o", (D, V), F32)], rest_buffers),
}


ORDER = (
    "Ac", "G", "Bc", "Ah1", "T", "Bh1", "E", "Cc", "Ah2", "Bh2", "Ah3", "Ch1", "Bh3", "Ax",
    "Ch2", "At", "Bx", "Ad2", "Ch3", "Ad1", "Bt", "Cx", "Bd2", "Aa", "Ad0", "Bd1", "Ct", "Ba",
    "Cd2", "Bd0", "Au", "Cd1", "K", "Ca", "Bu", "Cd0", "Cu",
)


def advance(chunk, who, what, token, slots, results):
    if what == "c":
        return chunk.first(token)
    if what == "x":
        return chunk.exchange(token)
    if what == "t":
        return chunk.turn(token)
    if what[0] == "h":
        return chunk.halve(int(what[1:]), token)
    if what == "d0":
        return chunk.last(token)
    if what[0] == "d":
        return chunk.double(int(what[1:]), token)
    if what == "a":
        chunk.now, chunk.twin = tied(token, chunk.now, chunk.twin)
        results[who] = list(start_unpack(who, slots, chunk, results))
    else:
        chunk.late, chunk.late_twin = tied(token, chunk.late, chunk.late_twin)
        results[who] = list(end_unpack(who, slots, chunk, results))
    if who != "A":
        results["mix"] = results[who][1 if who == "B" else 0]
    return results[who][0]


def on_device(
    inputs,
    lengths,
    key_mask,
    norm_gain,
    ema_expand,
    ema_alpha,
    ema_delta,
    ema_eta,
    ema_omega,
    w_value,
    w_mix,
    qk_affine,
    w_hidden,
    ffn_gain,
    w_up,
    w_down,
    cotangent,
):
    _, rows, _ = inputs.shape
    seqs = lax.axis_size("seq")
    reach = WINDOW // rows
    halving, whole = exchanges(lax.axis_size("batch"), seqs)
    slots = slot_table()
    limit = lengths - lax.axis_index("seq") * rows
    x = inputs.reshape(rows, D)
    cot = cotangent.reshape(rows, D)
    expand, alpha, delta, eta = ema_expand.T, ema_alpha.T, ema_delta.T, ema_eta.T
    omega = ema_omega.reshape(1, D)
    gain1 = norm_gain.reshape(1, D)
    gain2 = ffn_gain.reshape(1, D)
    powers = state_powers(seqs, rows)
    me = jnp.full((1,), lax.axis_index("seq"), jnp.int32)

    def buffers(tiles):
        return [("v", (4, 4, tiles * 16, 128), BF16)] * 2

    tall = rows * 8 * (D // LANES)
    normed, masked, state, decay, coeff, fades, w_value_near, w_hidden_near = call(
        functools.partial(norm_kernel, rows, powers),
        [
            ("v", (rows, D), BF16),
            ("v", (rows, D), BF16),
            ("v", (2 * H, D), BF16),
            ("v", (H, D), F32),
            ("v", (H, D), F32),
            ("v", (len(powers), H, D), F32),
            ("v", (D, V), BF16),
            ("v", (V, D), BF16),
        ],
        [("s", limit)]
        + [("h", t) for t in (x, gain1, alpha, delta, expand, eta)]
        + [("o", w_value), ("o", w_hidden)],
        [pltpu.VMEM((rows, D), F32), pltpu.SemaphoreType.DMA((2,))],
    )
    others = states_before(state, fades, me, rows)
    far_here = seqs > reach
    far, far_back, far_tables = [], [], []
    if far_here:
        behind = lax.ppermute(masked, "seq", shifted_pairs(seqs, reach)).astype(F32)
        early, far_pull = jax.vjp(far_part, behind, jnp.log(decay), coeff)
        far = [("h", early)]
    value_pre, value_low, w_mix_near, w_up_near, w_down_near = call(
        value_kernel,
        [
            ("v", (rows, V), F32),
            ("v", (rows, V), BF16),
            ("v", (D, MIX), BF16),
            ("v", (D, FF), BF16),
            ("v", (FF, D), BF16),
        ],
        [("v", normed), ("v", w_value_near), ("o", w_mix), ("o", w_up), ("o", w_down)],
        [pltpu.SemaphoreType.DMA((3,))],
    )
    (
        out,
        carry,
        pre,
        mix_low,
        mixed,
        probs,
        attended,
        gated,
        cand_pre,
        g_resid,
        g_ffn_gain,
        keep1,
        send1,
    ) = call(
        functools.partial(forward_kernel, rows, len(others), far_here),
        [
            ("v", (rows, D), BF16),
            ("v", (2 * H, D), F32),
            ("v", (rows, D), F32),
            ("v", (rows, D), BF16),
            ("v", (rows, MIX), F32),
            ("v", (rows, BLOCK), F32),
            ("v", (rows, V), F32),
            ("v", (rows, V), BF16),
            ("v", (rows, D), F32),
            ("v", (rows, D), F32),
            ("v", (1, D), F32),
        ]
        + buffers(16),
        [("s", limit), ("s", me), ("s", slots)]
        + [("v", t) for t in (fades, masked, value_low, decay, coeff)]
        + [("v", t) for t in (w_mix_near, w_hidden_near, w_up_near, w_down_near, *others)]
        + far
        + [("h", t) for t in (omega, qk_affine, key_mask, x, gain2, cot)],
        [
            pltpu.VMEM((rows, D), F32),
            pltpu.VMEM((tall, LANES), F32),
            pltpu.VMEM((rows, FF), F32),
            pltpu.VMEM((rows, FF), BF16),
            pltpu.VMEM((rows, D), BF16),
        ],
    )
    token = g_resid
    chunks = {"A": Summed(keep1, send1, halving, whole)}
    results = {}
    for step in ORDER:
        who, what = step[0], step[1:]
        if step == "G":
            (g_resid,) = tied(token, g_resid)
            keep2, send2, g_skip, g_upd, g_hid, g_reset, g_att = call(
                gates_kernel,
                buffers(16)
                + [
                    ("v", (rows, D), F32),
                    ("v", (rows, D), BF16),
                    ("v", (rows, D), BF16),
                    ("v", (rows, V), BF16),
                    ("v", (rows, V), BF16),
                ],
                [("s", slots), ("h", x), ("v", w_hidden_near)]
                + [("v", t) for t in (mix_low, mixed, attended, gated, cand_pre, g_resid)],
            )
            chunks["B"] = Summed(keep2, send2, halving, whole)
            token = g_skip
        elif step == "T":
            (g_att,) = tied(token, g_att)
            keep3, send3, g_qk, g_shared, g_normed = call(
                functools.partial(attention_kernel, rows),
                buffers(17) + [("v", (3, Z), F32), ("v", (rows, Z), BF16), ("v", (rows, D), F32)],
                [("s", slots)]
                + [
                    ("v", t)
                    for t in (
                        normed,
                        value_pre,
                        value_low,
                        mix_low,
                        mixed,
                        probs,
                        g_att,
                        g_reset,
                        w_value_near,
                    )
                ]
                + [("h", qk_affine)],
            )
            token = g_normed
        elif step == "E":
            (g_upd,) = tied(token, g_upd)
            if far_here:
                g_mixed = jnp.concatenate([g_upd, g_shared, g_reset, g_hid], axis=1)
                g_early = lax.dot_general(
                    g_mixed, w_mix, (((1,), (1,)), ((), ())), preferred_element_type=F32
                )
                sig = jax.nn.sigmoid(pre)
                g_behind, far_log, far_coeff = far_pull(g_early * (sig * (1.0 + pre * (1.0 - sig))))
                far_tables = [("h", jnp.concatenate([far_coeff, far_log], axis=0))]
                g_far = lax.ppermute(g_behind.astype(BF16), "seq", shifted_pairs(seqs, -reach))
                far_back = [("h", g_far.astype(F32))]
            keep3, send3, g_pre, adjoint = call(
                functools.partial(tables_kernel, rows, far_here),
                buffers(18) + [("v", (rows, D), F32), ("v", (H, D), BF16)],
                [("s", slots)]
                + [
                    ("v", t)
                    for t in (
                        keep3,
                        send3,
                        masked,
                        normed,
                        pre,
                        g_upd,
                        g_shared,
                        g_reset,
                        g_hid,
                        g_normed,
                        g_qk,
                        g_ffn_gain,
                        carry,
                        decay,
                        coeff,
                        w_mix_near,
                    )
                ]
                + far_tables
                + [("h", t) for t in (expand, alpha, delta, eta, gain1)],
                [pltpu.VMEM((rows, D), F32), pltpu.VMEM((512, 128), F32)],
            )
            if by_levels(rows):
                chunks["C"] = SummedWithStates(
                    keep3, send3, halving, whole, adjoint, fades, rows
                )
            else:
                chunks["C"] = Summed(keep3, send3, halving, whole)
                chunks["C"].others = [direct_states(adjoint, fades, rows, -1)]
            token = g_pre
        elif step == "K":
            others = chunks["C"].others
            (g_pre,) = tied(token, g_pre)
            (d_input,) = call(
                functools.partial(input_kernel, rows, len(others), far_here),
                [("v", (rows, D), BF16)],
                [("s", limit), ("s", me)]
                + [("v", t) for t in (fades, g_pre, g_skip, g_normed, decay, coeff)]
                + [("v", t) for t in others]
                + far_back
                + [("h", t) for t in (x, omega, gain1)],
                [pltpu.VMEM((tall, LANES), F32), pltpu.VMEM((rows, D), F32)],
            )
            token = d_input
        else:
            token = advance(chunks[who], who, what, token, slots, results)
    grad_down, grad_up = results["A"]
    grad_hidden, _ = results["B"]
    grad_mix = results["mix"]
    (
        _,
        grad_value,
        g_expand,
        g_alpha,
        g_delta,
        g_eta,
        g_norm_gain,
        g_omega,
        g_ffn_gain,
        g_qk,
    ) = results["C"]
    return (
        out.reshape(inputs.shape),
        d_input.reshape(inputs.shape),
        g_norm_gain.reshape(D),
        g_expand.T,
        g_alpha.T,
        g_delta.T,
        g_eta.T,
        g_omega.reshape(D),
        grad_value,
        grad_mix,
        g_qk,
        grad_hidden,
        g_ffn_gain.reshape(D),
        grad_up,
        grad_down,
    )


def solution(mesh):
    row = P("batch", "seq", None)
    return jax.shard_map(
        on_device,
        mesh=mesh,
        in_specs=(row, P("batch"), P("batch", "seq")) + (P(),) * 13 + (row,),
        out_specs=(row, row) + (P(),) * 13,
        check_vma=False,
    )
```

```python
import functools

import jax
import jax.numpy as jnp
from jax import lax
from jax.experimental import pallas as pl
from jax.experimental.pallas import tpu as pltpu
from jax.sharding import PartitionSpec as P

D = 512
Z = 128
V = 1024
H = 16
FF = 1024
BLOCK = 128
WINDOW = 4096
MIX = 2 * D + Z + V
AXES = ("batch", "seq")
F32 = jnp.float32
BF16 = jnp.bfloat16
COSTS = {
    "norm_kernel": 10**9,
    "join_kernel": 10**9,
    "local_kernel": 10**9,
    "value_kernel": 10**9,
    "inner_kernel": 10**9,
    "forward_kernel": 10**9,
    "resid_kernel": 10**9,
    "gates_kernel": 10**9,
    "output_kernel": 10**9,
    "attention_kernel": 12 * 10**9,
    "tables_kernel": 10**9,
    "input_kernel": 10**9,
}
VMEM_LIMIT = 24 * 2**20


def sigmoid(v):
    return 1.0 / (1.0 + jnp.exp(-v))


def dot(a, b):
    return lax.dot_general(a, b, (((1,), (0,)), ((), ())), preferred_element_type=F32)


def dot_nt(a, b):
    return lax.dot_general(a, b, (((1,), (1,)), ((), ())), preferred_element_type=F32)


def dot_tn(a, b):
    return lax.dot_general(a, b, (((0,), (0,)), ((), ())), preferred_element_type=F32)


class Late:
    def __init__(self, copy, ref):
        self.copy, self.ref, self.waited = copy, ref, False

    def __call__(self):
        if not self.waited:
            self.copy.wait()
            self.waited = True
        return self.ref


SPACES = {"s": pltpu.SMEM, "v": pltpu.VMEM, "h": pltpu.HBM, "o": pltpu.HBM}


def call(body, outs, args, scratch=(), alias=None):
    late = [i for i, (kind, _) in enumerate(args) if kind == "h"]
    n_in, n_out = len(args), len(outs)

    def run(*refs):
        ins = list(refs[:n_in])
        mine = refs[n_in : n_in + n_out + len(scratch)]
        if late:
            rest = refs[n_in + n_out + len(scratch) :]
            for k, i in enumerate(late):
                copy = pltpu.make_async_copy(ins[i], rest[k], rest[-1].at[k])
                copy.start()
                ins[i] = Late(copy, rest[k])
        body(*ins, *mine)
        for i in late:
            ins[i]()

    name = getattr(body, "func", body).__name__
    buffers = [pltpu.VMEM(args[i][1].shape, args[i][1].dtype) for i in late]
    if late:
        buffers.append(pltpu.SemaphoreType.DMA((len(late),)))
    return pl.pallas_call(
        run,
        out_shape=[jax.ShapeDtypeStruct(shape, dtype) for _, shape, dtype in outs],
        in_specs=[pl.BlockSpec(memory_space=SPACES[kind]) for kind, _ in args],
        out_specs=[pl.BlockSpec(memory_space=SPACES[kind]) for kind, _, _ in outs],
        scratch_shapes=list(scratch) + buffers,
        input_output_aliases=alias or {},
        compiler_params=pltpu.CompilerParams(vmem_limit_bytes=VMEM_LIMIT),
        name=name,
        cost_estimate=pl.CostEstimate(
            flops=COSTS.get(name, 10**10), bytes_accessed=0, transcendentals=0
        ),
    )(
        *[
            pltpu.with_memory_space_constraint(array, pltpu.HBM) if kind in "ho" else array
            for kind, array in args
        ]
    )


def row8(ref, t):
    return jnp.broadcast_to(ref[pl.ds(t, 1), :], (8, D))


LANES = 128


def put8(part_ref, t, rows, eight):
    for j in range(D // LANES):
        base = pl.multiple_of(j * rows * 8 + t * 8, 8)
        part_ref[pl.ds(base, 8), :] = eight[:, j * LANES : (j + 1) * LANES]


def fold8(part_ref, out_ref, rows):
    def one(g, _):
        at = pl.multiple_of(g * 8, 8)
        for j in range(D // LANES):
            base = pl.multiple_of(j * rows * 8 + g * 64, 64)
            acc = part_ref[pl.ds(base, 8, stride=8), :]
            for k in range(1, 8):
                acc = acc + part_ref[pl.ds(base + k, 8, stride=8), :]
            out_ref[pl.ds(at, 8), j * LANES : (j + 1) * LANES] = acc
        return 0

    lax.fori_loop(0, rows // 8, one, 0)


def norm_kernel(
    rows,
    powers,
    lim_ref,
    x,
    gain,
    alpha,
    delta,
    expand,
    eta,
    wvalue_ref,
    normed_ref,
    masked_ref,
    state_ref,
    a_ref,
    c_ref,
    fade_ref,
    wvalue_out_ref,
    m_ref,
    sem,
):
    copies = bring(((wvalue_ref, wvalue_out_ref),), sem)
    x = x()[...].astype(F32)
    center = jnp.mean(x, axis=1, keepdims=True)
    shifted = x - center
    spread = jnp.mean(shifted * shifted, axis=1, keepdims=True)
    normed = (shifted * lax.rsqrt(spread + 1e-05) * gain()[...]).astype(BF16)
    normed_ref[...] = normed
    place = lax.broadcasted_iota(jnp.int32, (rows, 1), 0)
    masked = jnp.where(place < lim_ref[0], normed.astype(F32), 0.0)
    masked_ref[...] = masked.astype(BF16)
    m_ref[...] = masked
    alpha = sigmoid(alpha()[...])
    decay = 1.0 - alpha * sigmoid(delta()[...])
    a_ref[...] = decay
    c_ref[...] = eta()[...] * alpha * expand()[...]
    log_decay = jnp.log(decay)
    for i, power in enumerate(powers):
        fade_ref[i] = jnp.exp(log_decay * power)
    a = (decay[0:8, :], decay[8:16, :])

    def step(g, carry):
        s, q = carry
        for k in range(8):
            row = row8(m_ref, g * 8 + k)
            grown = tuple(a[i] * s[i] for i in range(2))
            q = tuple(a[i] * q[i] + grown[i] for i in range(2))
            s = tuple(grown[i] + row for i in range(2))
        return s, q

    zero = jnp.zeros((8, D), F32)
    s, q = lax.fori_loop(0, rows // 8, step, ((zero, zero), (zero, zero)))
    state_ref[0:8, :] = s[0].astype(BF16)
    state_ref[8:16, :] = s[1].astype(BF16)
    state_ref[16:24, :] = q[0].astype(BF16)
    state_ref[24:32, :] = q[1].astype(BF16)
    for copy in copies:
        copy.wait()


def bring(pairs, sem):
    copies = []
    for i, (src, dst) in enumerate(pairs):
        copy = pltpu.make_async_copy(src, dst, sem.at[i])
        copy.start()
        copies.append(copy)
    return copies


def local_kernel(rows, masked_ref, a_ref, c_ref, wmix_ref, out_ref, wmix_out_ref, m_ref, part_ref, sem):
    copies = bring(((wmix_ref, wmix_out_ref),), sem)
    m_ref[...] = masked_ref[...].astype(F32)
    a = (a_ref[0:8, :], a_ref[8:16, :])
    c = (c_ref[0:8, :], c_ref[8:16, :])

    def step(g, s):
        for k in range(8):
            t = g * 8 + k
            row = row8(m_ref, t)
            s = tuple(a[i] * s[i] + row for i in range(2))
            put8(part_ref, t, rows, c[0] * s[0] + c[1] * s[1])
        return s

    zero = jnp.zeros((8, D), F32)
    lax.fori_loop(0, rows // 8, step, (zero, zero))
    fold8(part_ref, out_ref, rows)
    for copy in copies:
        copy.wait()


def value_kernel(
    normed_ref, wvalue_ref, wup_ref, wdown_ref, pre_ref, low_ref, wup_out_ref, wdown_out_ref, sem
):
    copies = bring(((wup_ref, wup_out_ref), (wdown_ref, wdown_out_ref)), sem)
    for lo in range(0, V, D):
        pre = dot(normed_ref[...], wvalue_ref[:, lo : lo + D])
        pre_ref[:, lo : lo + D] = pre
        low_ref[:, lo : lo + D] = (pre * sigmoid(pre)).astype(BF16)
    for copy in copies:
        copy.wait()


def inner_kernel(wdown_ref, cot, whid_ref, out_ref, whid_out_ref, sem):
    copies = bring(((whid_ref, whid_out_ref),), sem)
    out_ref[...] = dot_nt(cot()[...], wdown_ref[...])
    for copy in copies:
        copy.wait()


def moved(state, fade, steps):
    if state.shape[0] == H:
        return fade * state
    return jnp.concatenate([fade * state[:H], fade * (state[H:] + steps * state[:H])], axis=0)


def joined(own_len, level, direction, me, group, other, fades):
    late = ((me >> level) & 1) == (1 if direction == 1 else 0)
    first, second = jnp.where(late, other, group), jnp.where(late, group, other)
    return (moved(first, fades[level], float(own_len << level)) + second).astype(BF16)


def join_kernel(own_len, level, me_ref, group_ref, other_ref, fade_ref, out_ref):
    group, other = group_ref[...].astype(F32), other_ref[...].astype(F32)
    out_ref[...] = joined(own_len, level, 1, me_ref[0], group, other, fade_ref)


def carried(own_len, direction, me, others, fades):
    total = None
    for i, other in enumerate(others):
        blocks = me if direction == 1 else ~me
        late = ((me >> i) & 1) == (1 if direction == 1 else 0)
        for j in range(i):
            on = ((blocks >> j) & 1) == 1
            other = jnp.where(on, moved(other, fades[j], float(own_len << j)), other)
        other = jnp.where(late, other, 0.0)
        total = other if total is None else total + other
    return total


def place(slots_ref, dst, side, at, grad):
    rows, cols = grad.shape
    piece = rows // 16
    for g in range(4):
        slot = slots_ref[1 + 4 * side + g]
        for z in range(4):
            tile = at
            for lo in range((g * 4 + z) * piece, (g * 4 + z + 1) * piece, 16):
                for c in range(0, cols, 128):
                    dst[slot, z, tile * 16 : tile * 16 + 16, :] = grad[lo : lo + 16, c : c + 128]
                    tile += 1


def outer(slots_ref, keep_ref, send_ref, at, left_ref, right):
    half = left_ref.shape[1] // 2
    for side, dst in enumerate((keep_ref, send_ref)):
        core = slots_ref[0] ^ side
        left = left_ref[:, pl.ds(pl.multiple_of(core * half, half), half)]
        place(slots_ref, dst, side, at, dot_tn(left, right).astype(BF16))


def forward_kernel(
    rows,
    n_others,
    has_far,
    lim_ref,
    me_ref,
    slots_ref,
    fade_ref,
    masked_ref,
    value_ref,
    a_ref,
    c_ref,
    wmix_ref,
    whid_ref,
    wup_ref,
    local_ref,
    ginner_ref,
    *refs,
):
    others, refs = refs[:n_others], refs[n_others:]
    far, refs = (refs[0], refs[1:]) if has_far else (None, refs)
    (
        omega,
        qk,
        mask,
        x,
        gain,
        cot,
        carry_ref,
        pre_ref,
        mixlow_ref,
        mixed_ref,
        probs_ref,
        att_ref,
        gated_ref,
        candpre_ref,
        resid_ref,
        inner_ref,
        guplow_ref,
        keep_ref,
        send_ref,
        part_ref,
        up_ref,
        ffn_ref,
    ) = refs
    masked = masked_ref[...].astype(F32)
    if n_others == 1:
        carry_ref[...] = others[0][...].astype(F32)
    else:
        states = [ref[...].astype(F32) for ref in others]
        carry_ref[...] = carried(rows, 1, me_ref[0], states, fade_ref)
    a = (a_ref[0:8, :], a_ref[8:16, :])

    def step(g, s):
        for k in range(8):
            s = tuple(a[i] * s[i] for i in range(2))
            put8(part_ref, g * 8 + k, rows, s[0] + s[1])
        return s

    start = tuple(c_ref[i : i + 8, :] * carry_ref[i : i + 8, :] for i in (0, 8))
    lax.fori_loop(0, rows // 8, step, start)
    fold8(part_ref, pre_ref, rows)
    pre = pre_ref[...] + local_ref[...] + omega()[...] * masked
    if has_far:
        pre = pre + far()[...]
    pre_ref[...] = pre
    mix_low = (pre * sigmoid(pre)).astype(BF16)
    mixlow_ref[...] = mix_low
    mixed_ref[...] = dot(mix_low, wmix_ref[...])
    shared_pre = mixed_ref[:, D : D + Z]
    shared = shared_pre * sigmoid(shared_pre)
    qk_ref, mask_ref = qk(), mask()
    query = (shared * qk_ref[0:1, :] + qk_ref[1:2, :]).astype(BF16)
    key = (shared * qk_ref[2:3, :]).astype(BF16)
    places = lax.broadcasted_iota(jnp.int32, (BLOCK, BLOCK), 0)
    others = lax.broadcasted_iota(jnp.int32, (BLOCK, BLOCK), 1)
    for g in range(rows // BLOCK):
        lo = g * BLOCK
        ok = (mask_ref[:, lo : lo + BLOCK] > 0) & (
            lax.broadcasted_iota(jnp.int32, (1, BLOCK), 1) + lo < lim_ref[0]
        )
        ok = jnp.broadcast_to(ok.astype(F32), (BLOCK, BLOCK)) > 0.5
        allowed = (places == others) | ((places > others) & ok)
        scores = dot_nt(query[lo : lo + BLOCK], key[lo : lo + BLOCK]) * (Z**-0.5)
        scores = jnp.where(allowed, scores, -1000000000.0)
        grown = jnp.exp(scores - jnp.max(scores, axis=1, keepdims=True))
        probs = grown / jnp.sum(grown, axis=1, keepdims=True)
        probs_ref[lo : lo + BLOCK, :] = probs
        att_ref[lo : lo + BLOCK, :] = dot(probs.astype(BF16), value_ref[lo : lo + BLOCK, :])
    reset_pre = mixed_ref[:, D + Z : D + Z + V]
    gated = (att_ref[...] * (reset_pre * sigmoid(reset_pre))).astype(BF16)
    gated_ref[...] = gated
    cand_pre = mixed_ref[:, D + Z + V :] + dot(gated, whid_ref[...])
    candpre_ref[...] = cand_pre
    cand = cand_pre * sigmoid(cand_pre)
    x = x()[...].astype(F32)
    resid = x + sigmoid(mixed_ref[:, :D]) * (cand - x)
    resid_ref[...] = resid
    unit, _ = unit_rows(resid)
    ffn_low = (unit * gain()[...]).astype(BF16)
    ffn_ref[...] = ffn_low
    up_ref[...] = dot(ffn_low, wup_ref[...])
    up = up_ref[...]
    sig = sigmoid(up)
    inner = (up * sig).astype(BF16)
    inner_ref[...] = inner
    outer(slots_ref, keep_ref, send_ref, 0, inner_ref, cot()[...])
    gup_low = (ginner_ref[...] * (sig * (1.0 + up * (1.0 - sig)))).astype(BF16)
    guplow_ref[...] = gup_low
    outer(slots_ref, keep_ref, send_ref, 8, ffn_ref, gup_low)


def unit_rows(rows):
    shifted = rows - jnp.mean(rows, axis=1, keepdims=True)
    inv = lax.rsqrt(jnp.mean(shifted * shifted, axis=1, keepdims=True) + 1e-05)
    return shifted * inv, inv


def norm_back(unit, inv, e):
    return inv * (
        e
        - jnp.mean(e, axis=1, keepdims=True)
        - unit * jnp.mean(e * unit, axis=1, keepdims=True)
    )


def output_kernel(resid_ref, inner_ref, wdown, out_ref):
    out_ref[...] = (resid_ref[...] + dot(inner_ref[...], wdown()[...])).astype(BF16)


def slope(v, sig):
    return sig * (1.0 + v * (1.0 - sig))


def resid_kernel(
    slots_ref,
    cot,
    gain,
    resid_ref,
    guplow_ref,
    wup_ref,
    mixed_ref,
    candpre_ref,
    gated_ref,
    keep_ref,
    send_ref,
    gres_ref,
    ggain_ref,
    ghid_ref,
):
    g_ffn = dot_nt(guplow_ref[...], wup_ref[...])
    unit, inv = unit_rows(resid_ref[...])
    ggain_ref[...] = jnp.sum(g_ffn * unit, axis=0, keepdims=True)
    g_resid = cot()[...].astype(F32) + norm_back(unit, inv, g_ffn * gain()[...])
    gres_ref[...] = g_resid
    cand_pre = candpre_ref[...]
    g_cand = g_resid * sigmoid(mixed_ref[:, :D]) * slope(cand_pre, sigmoid(cand_pre))
    g_hid = g_cand.astype(BF16)
    ghid_ref[...] = g_hid
    outer(slots_ref, keep_ref, send_ref, 0, gated_ref, g_hid)


def gates_kernel(
    slots_ref,
    keep_in_ref,
    send_in_ref,
    x,
    whid_ref,
    mixlow_ref,
    mixed_ref,
    att_ref,
    candpre_ref,
    gres_ref,
    ghid_ref,
    keep_ref,
    send_ref,
    gskip_ref,
    gupd_ref,
    greset_ref,
    gatt_ref,
):
    g_hid = ghid_ref[...]
    g_gated = dot_nt(g_hid, whid_ref[...])
    outer(slots_ref, keep_ref, send_ref, 12, mixlow_ref, g_hid)
    g_resid = gres_ref[...]
    update = sigmoid(mixed_ref[:, :D])
    cand_pre = candpre_ref[...]
    g_update = g_resid * update
    gskip_ref[...] = g_resid - g_update
    cand = cand_pre * sigmoid(cand_pre)
    g_upd = (g_update * (1.0 - update) * (cand - x()[...].astype(F32))).astype(BF16)
    gupd_ref[...] = g_upd
    outer(slots_ref, keep_ref, send_ref, 8, mixlow_ref, g_upd)
    reset_pre = mixed_ref[:, D + Z : D + Z + V]
    sig = sigmoid(reset_pre)
    gatt_ref[...] = (g_gated * (reset_pre * sig)).astype(BF16)
    greset_ref[...] = (g_gated * att_ref[...] * slope(reset_pre, sig)).astype(BF16)


def attention_kernel(
    rows,
    slots_ref,
    normed_ref,
    valuepre_ref,
    value_ref,
    mixlow_ref,
    mixed_ref,
    probs_ref,
    gatt_ref,
    greset_ref,
    wvalue_ref,
    qk,
    keep_ref,
    send_ref,
    gqk_ref,
    gshared_ref,
    gnorm_ref,
):
    qk_ref = qk()
    shared_pre = mixed_ref[:, D : D + Z]
    ssig = sigmoid(shared_pre)
    shared = shared_pre * ssig
    query = (shared * qk_ref[0:1, :] + qk_ref[1:2, :]).astype(BF16)
    key = (shared * qk_ref[2:3, :]).astype(BF16)
    g_query, g_key, g_value = [], [], []
    for g in range(rows // BLOCK):
        part = slice(g * BLOCK, (g + 1) * BLOCK)
        probs = probs_ref[part, :]
        g_probs = dot_nt(gatt_ref[part, :], value_ref[part, :])
        g_value.append(dot_tn(probs.astype(BF16), gatt_ref[part, :]))
        inner = jnp.sum(g_probs * probs, axis=1, keepdims=True)
        g_scores = (probs * (g_probs - inner) * (Z**-0.5)).astype(BF16)
        g_query.append(dot(g_scores, key[part]))
        g_key.append(dot_tn(g_scores, query[part]))
    g_query = jnp.concatenate(g_query, axis=0)
    g_key = jnp.concatenate(g_key, axis=0)
    g_value = jnp.concatenate(g_value, axis=0)
    gqk_ref[0:1, :] = jnp.sum(g_query * shared, axis=0, keepdims=True)
    gqk_ref[1:2, :] = jnp.sum(g_query, axis=0, keepdims=True)
    gqk_ref[2:3, :] = jnp.sum(g_key * shared, axis=0, keepdims=True)
    g_shared = g_query * qk_ref[0:1, :] + g_key * qk_ref[2:3, :]
    g_shared = (g_shared * slope(shared_pre, ssig)).astype(BF16)
    gshared_ref[...] = g_shared
    outer(slots_ref, keep_ref, send_ref, 8, mixlow_ref, g_shared)
    value_pre = valuepre_ref[...]
    vsig = sigmoid(value_pre)
    g_vpre = (g_value * slope(value_pre, vsig)).astype(BF16)
    outer(slots_ref, keep_ref, send_ref, 0, normed_ref, g_vpre)
    outer(slots_ref, keep_ref, send_ref, 9, mixlow_ref, greset_ref[...])
    gnorm_ref[...] = dot_nt(g_vpre, wvalue_ref[...])


SMALL = 4 * H + 4


def tables_kernel(
    rows,
    has_far,
    slots_ref,
    keep_in_ref,
    send_in_ref,
    masked_ref,
    normed_ref,
    pre_ref,
    gupd_ref,
    gshared_ref,
    greset_ref,
    ghid_ref,
    gnorm_ref,
    gqk_ref,
    gffn_ref,
    carry_ref,
    a_ref,
    c_ref,
    wmix_ref,
    *refs,
):
    far, refs = (refs[0], refs[1:]) if has_far else (None, refs)
    expand, alpha, delta, eta, gain, *refs = refs
    keep_ref, send_ref, gpre_ref, adj_ref, m_ref, small_ref = refs
    m_ref[...] = masked_ref[...].astype(F32)
    pre = pre_ref[...]
    psig = sigmoid(pre)
    g_mix_low = dot_nt(gupd_ref[...], wmix_ref[:, :D])
    g_mix_low += dot_nt(gshared_ref[...], wmix_ref[:, D : D + Z])
    g_mix_low += dot_nt(greset_ref[...], wmix_ref[:, D + Z : D + Z + V])
    g_mix_low += dot_nt(ghid_ref[...], wmix_ref[:, D + Z + V :])
    g_pre = g_mix_low * slope(pre, psig)
    gpre_ref[...] = g_pre
    a = (a_ref[0:8, :], a_ref[8:16, :])

    def step(g, carry):
        s, q, dc, dq, m = carry
        for k in range(8):
            t = g * 8 + k
            row = row8(m_ref, t)
            grad = row8(gpre_ref, t)
            late = row8(gpre_ref, rows - 1 - t)
            grown = tuple(a[i] * s[i] for i in range(2))
            q = tuple(a[i] * q[i] + grown[i] for i in range(2))
            s = tuple(grown[i] + row for i in range(2))
            dc = tuple(dc[i] + grad * s[i] for i in range(2))
            dq = tuple(dq[i] + grad * q[i] for i in range(2))
            m = tuple(a[i] * (m[i] + late) for i in range(2))
        return s, q, dc, dq, m

    zero = jnp.zeros((8, D), F32)
    _, _, dc, dq, m = lax.fori_loop(
        0,
        rows // 8,
        step,
        (
            (carry_ref[0:8, :], carry_ref[8:16, :]),
            (carry_ref[16:24, :], carry_ref[24:32, :]),
            (zero, zero),
            (zero, zero),
            (zero, zero),
        ),
    )
    adj_ref[0:8, :] = m[0].astype(BF16)
    adj_ref[8:16, :] = m[1].astype(BF16)
    g_coeff = jnp.concatenate(dc, axis=0)
    g_log = c_ref[...] * jnp.concatenate(dq, axis=0)
    if has_far:
        far_ref = far()
        g_coeff, g_log = g_coeff + far_ref[0:H, :], g_log + far_ref[H:, :]
    expand, eta = expand()[...], eta()[...]
    alpha, delta = sigmoid(alpha()[...]), sigmoid(delta()[...])
    g_log = g_log / a_ref[...]
    g_expand = g_coeff * (eta * alpha)
    g_eta = g_coeff * (alpha * expand)
    g_alpha = (g_coeff * (eta * expand) - g_log * delta) * (alpha * (1.0 - alpha))
    g_delta = -(g_log * alpha) * (delta * (1.0 - delta))
    small_ref[...] = jnp.zeros_like(small_ref)
    for i, part in enumerate((g_expand, g_alpha, g_delta, g_eta)):
        for j in range(D // LANES):
            at = (i * 4 + j) * H
            small_ref[at : at + H, :] = part[:, j * LANES : (j + 1) * LANES]
    g_gain = jnp.sum(
        g_pre * pre + normed_ref[...].astype(F32) * gnorm_ref[...], axis=0, keepdims=True
    ) / gain()[...]
    g_omega = jnp.sum(g_pre * m_ref[...], axis=0, keepdims=True)
    for i, part in enumerate((g_gain, g_omega, gffn_ref[...])):
        for j in range(D // LANES):
            at = 16 * H + j * H + i
            small_ref[at : at + 1, :] = part[:, j * LANES : (j + 1) * LANES]
    for j in range(3):
        at = 16 * H + j * H + 3
        small_ref[at : at + 1, :] = gqk_ref[j : j + 1, :]
    for side, dst in enumerate((keep_ref, send_ref)):
        row = pl.multiple_of((slots_ref[0] ^ side) * 256, 256)
        place(slots_ref, dst, side, 17, small_ref[pl.ds(row, 256), :].astype(BF16))


def input_kernel(
    rows,
    n_others,
    has_far,
    lim_ref,
    me_ref,
    fade_ref,
    gpre_ref,
    gskip_ref,
    gnorm_ref,
    a_ref,
    c_ref,
    *refs,
):
    others, refs = refs[:n_others], refs[n_others:]
    far, refs = (refs[0], refs[1:]) if has_far else (None, refs)
    x, omega, gain, din_ref, part_ref, gx_ref = refs
    if n_others == 1:
        adjoint = others[0][...].astype(F32)
    else:
        adjoint = carried(rows, -1, me_ref[0], [state_in(ref) for ref in others], fade_ref)
    a = (a_ref[0:8, :], a_ref[8:16, :])
    c = (c_ref[0:8, :], c_ref[8:16, :])

    def back(g, m):
        for k in range(8):
            t = rows - 1 - (g * 8 + k)
            row = row8(gpre_ref, t)
            lam = tuple(m[i] + row for i in range(2))
            put8(part_ref, t, rows, c[0] * lam[0] + c[1] * lam[1])
            m = tuple(a[i] * lam[i] for i in range(2))
        return m

    lax.fori_loop(0, rows // 8, back, (adjoint[0:8, :], adjoint[8:16, :]))
    fold8(part_ref, gx_ref, rows)
    g_masked = gx_ref[...] + omega()[...] * gpre_ref[...]
    if has_far:
        g_masked = g_masked + far()[...]
    place = lax.broadcasted_iota(jnp.int32, (rows, 1), 0)
    e = jnp.where(place < lim_ref[0], g_masked, 0.0) + gnorm_ref[...]
    x = x()[...].astype(F32)
    shifted = x - jnp.mean(x, axis=1, keepdims=True)
    inv = lax.rsqrt(jnp.mean(shifted * shifted, axis=1, keepdims=True) + 1e-05)
    unit = shifted * inv
    e = e * gain()[...]
    g_in = inv * (
        e
        - jnp.mean(e, axis=1, keepdims=True)
        - unit * jnp.mean(e * unit, axis=1, keepdims=True)
    )
    din_ref[...] = (g_in + gskip_ref[...]).astype(BF16)


def unpack(slots_ref, sources, first, segments, sem):
    copies = []
    for at, rows, cols, buffer_ref, out_ref, col in segments:
        group, piece = rows // 8, rows // 32
        for side, src in sources:
            for slot in range(2):
                block = len(copies) % 4
                for z in range(4):
                    tile = at
                    for lo in range(z * piece, (z + 1) * piece, 16):
                        for c in range(0, cols, 128):
                            buffer_ref[block, lo : lo + 16, c : c + 128] = src[
                                slot, z, tile * 16 : tile * 16 + 16, :
                            ].astype(F32)
                            tile += 1
                place_of = slots_ref[9 + 4 * side + first + slot]
                row = pl.multiple_of(
                    (slots_ref[0] ^ side) * (rows // 2) + place_of * group, group
                )
                copy = pltpu.make_async_copy(
                    buffer_ref.at[block],
                    out_ref.at[pl.ds(row, group), pl.ds(col, cols)],
                    sem.at[len(copies)],
                )
                copy.start()
                copies.append(copy)
    return copies


def ffn_segments(down_buf, up_buf, down_ref, up_ref):
    return [(0, FF, D, down_buf, down_ref, 0), (8, D, FF, up_buf, up_ref, 0)]


def gates_segments(hid_buf, upd_buf, in_buf, hid_ref, mix_ref):
    return [
        (0, V, D, hid_buf, hid_ref, 0),
        (8, D, D, upd_buf, mix_ref, 0),
        (12, D, D, in_buf, mix_ref, D + Z + V),
    ]


def rest_segments(value_buf, shared_buf, reset_buf, mix_ref, value_ref):
    return [
        (0, D, V, value_buf, value_ref, 0),
        (8, D, Z, shared_buf, mix_ref, D),
        (9, D, V, reset_buf, mix_ref, D + Z),
    ]


def unpack_kernel(segments, n_out, n_given, first, slots_ref, mine_ref, twin_ref, *refs):
    refs = refs[n_given:]
    outs, refs = refs[:n_out], refs[n_out:]
    parts = segments(*refs[:-1], *outs)
    for copy in unpack(slots_ref, ((0, mine_ref), (1, twin_ref)), first, parts, refs[-1]):
        copy.wait()


def unpack_rest_kernel(
    slots_ref,
    mine_ref,
    twin_ref,
    early_ref,
    twin_early_ref,
    mix_in_ref,
    value_in_ref,
    mix_ref,
    value_ref,
    expand_ref,
    alpha_ref,
    delta_ref,
    eta_ref,
    gain_ref,
    omega_ref,
    ffn_ref,
    qk_ref,
    value_buf,
    shared_buf,
    reset_buf,
    small_ref,
    sem,
):
    parts = rest_segments(value_buf, shared_buf, reset_buf, mix_ref, value_ref)
    copies = unpack(slots_ref, ((0, mine_ref), (1, twin_ref)), 2, parts, sem)
    for side, pair in enumerate(((early_ref, mine_ref), (twin_early_ref, twin_ref))):
        for slot in range(4):
            place_of = slots_ref[9 + 4 * side + slot]
            row = pl.multiple_of((slots_ref[0] ^ side) * 256 + place_of * 64, 64)
            for z in range(4):
                small_ref[pl.ds(row + z * 16, 16), :] = pair[slot // 2][
                    slot % 2, z, 17 * 16 : 18 * 16, :
                ].astype(F32)
    for i, out_ref in enumerate((expand_ref, alpha_ref, delta_ref, eta_ref)):
        for j in range(D // LANES):
            at = (i * 4 + j) * H
            out_ref[:, j * LANES : (j + 1) * LANES] = small_ref[at : at + H, :]
    for i, out_ref in enumerate((gain_ref, omega_ref, ffn_ref)):
        for j in range(D // LANES):
            at = 16 * H + j * H + i
            out_ref[:, j * LANES : (j + 1) * LANES] = small_ref[at : at + 1, :]
    for j in range(3):
        at = 16 * H + j * H + 3
        qk_ref[j : j + 1, :] = small_ref[at : at + 1, :]
    for copy in copies:
        copy.wait()


def added(left, right):
    return (left.astype(F32) + right.astype(F32)).astype(BF16)


def plain_halve_kernel(level, me_ref, keep_ref, came_ref, send_ref, kept_ref):
    if level < 3:
        half = keep_ref.shape[0] // 2
        send_ref[...] = added(keep_ref[half:], came_ref[half:])
        kept_ref[...] = added(keep_ref[:half], came_ref[:half])
        return
    half = keep_ref.shape[1] // 2
    mine = (me_ref[0] >> 1) & 1
    other = pl.ds((1 - mine) * half, half)
    send_ref[0] = added(keep_ref[0, other], came_ref[0, other])
    own = pl.ds(mine * half, half)
    kept_ref[0] = added(keep_ref[0, own], came_ref[0, own])


def add_kernel(left_ref, right_ref, out_ref):
    out_ref[...] = added(left_ref[...], right_ref[...])


def add_start_kernel(left_ref, right_ref, out_ref):
    pieces, rows = out_ref.shape[1:3]
    for i in range(pieces):
        part = slice(i * rows, (i + 1) * rows)
        out_ref[0, i] = added(left_ref[part, :], right_ref[part, :])


def pair_kernel(me_ref, now_ref, came_ref, out_ref):
    half = now_ref.shape[1]
    mine = (me_ref[0] >> 1) & 1
    out_ref[0, pl.ds(mine * half, half)] = now_ref[0]
    out_ref[0, pl.ds((1 - mine) * half, half)] = came_ref[0]


def stack_kernel(now_ref, came_ref, out_ref):
    out_ref[0] = now_ref[0]
    out_ref[1] = came_ref[0]


STATE = 4 * H


def state_in(ref):
    if ref.shape[1] == D:
        return ref[...].astype(F32)
    base = ref.shape[0] - STATE
    return jnp.concatenate([ref[base + j * H : base + (j + 1) * H, :] for j in range(4)], axis=1).astype(F32)


def put_state(ref, state):
    base = ref.shape[0] - STATE
    for j in range(4):
        ref[base + j * H : base + (j + 1) * H, :] = state[:, j * LANES : (j + 1) * LANES].astype(BF16)


def halve_kernel(level, own_len, me_ref, core_ref, fade_ref, adj_ref, keep_ref, came_ref, *refs):
    groups, pieces, rows, _ = keep_ref.shape
    size = pieces * rows

    def sums(g, z0, zn):
        keep = keep_ref[g, pl.ds(z0, zn)].reshape(zn * rows, 128)
        if len(came_ref.shape) == 4:
            came = came_ref[g, pl.ds(z0, zn)].reshape(zn * rows, 128)
        else:
            start = g * size + z0 * rows
            came = came_ref[pl.ds(pl.multiple_of(start, 16), zn * rows), :]
        return added(keep, came)

    if level < 3:
        send_ref, kept_ref = refs
        put_state(send_ref, adj_ref[...].astype(F32))
        half = groups // 2
        for g in range(half):
            send_ref[g * size : (g + 1) * size, :] = sums(half + g, 0, pieces)
        for g in range(half):
            kept_ref[g] = sums(g, 0, pieces).reshape(pieces, rows, 128)
        return
    first_ref, send_ref, kept_ref, other_ref, group_ref = refs
    me = me_ref[0]
    mine = (me >> 1) & 1
    other = jnp.where(core_ref[0] == 1, state_in(first_ref), state_in(came_ref))
    other_ref[...] = other.astype(BF16)
    group = joined(own_len, 0, -1, me, adj_ref[...].astype(F32), other, fade_ref)
    group_ref[...] = group
    put_state(send_ref, group.astype(F32))
    half = pieces // 2
    send_ref[: half * rows, :] = sums(0, (1 - mine) * half, half)
    kept_ref[0] = sums(0, mine * half, half).reshape(half, rows, 128)


def exchange_kernel(own_len, me_ref, fade_ref, group_ref, keep_ref, came_ref, now_ref):
    _, pieces, rows, _ = keep_ref.shape
    keep = keep_ref[0].reshape(pieces * rows, 128)
    now_ref[: pieces * rows, :] = added(keep, came_ref[: pieces * rows, :])
    group, other = group_ref[...].astype(F32), state_in(came_ref)
    put_state(now_ref, joined(own_len, 1, -1, me_ref[0], group, other, fade_ref).astype(F32))


def exchanges(batches, seqs):
    def pairs(turn):
        out = []
        for b in range(batches):
            for s in range(seqs):
                nb, ns = turn(b, s)
                out.append((b * seqs + s, nb * seqs + ns))
        return out

    halving = [
        pairs(lambda b, s: (b ^ 1, s)),
        pairs(lambda b, s: (b, s ^ 1) if b & 1 else (b ^ 2, s)),
        pairs(lambda b, s: (b ^ 2, s) if b & 1 else (b, s ^ 1)),
        pairs(lambda b, s: (b, s ^ 2)),
    ]
    whole = []
    bit = 4
    while bit < seqs:
        whole.append(pairs(lambda b, s, bit=bit: (b, s ^ bit)))
        bit *= 2
    return halving, whole


def slot_table():
    b, s = lax.axis_index("batch"), lax.axis_index("seq")
    core, here = b & 1, ((b >> 1) & 1) * 2 + (s & 1)
    at = jnp.arange(17, dtype=jnp.int32)
    part, four = (at - 1) >> 2, (at - 1) & 3

    def swapped(v):
        return (v >> 1) | ((v & 1) << 1)

    turned = (core ^ (part & 1)) == 1
    slot = jnp.where(turned, swapped(four ^ here), four ^ here)
    group = jnp.where(turned, swapped(four) ^ here, four ^ here)
    return jnp.where(at == 0, core, jnp.where(part < 2, slot, group))


def tied(token, *arrays):
    return lax.optimization_barrier((token,) + arrays)[1:]


class Summed:
    def __init__(self, keep, send, halving, whole):
        self.keep, self.send, self.halving, self.whole = keep, send, halving, whole
        self.me = jnp.full((1,), lax.axis_index("seq"), jnp.int32)

    def first(self, token):
        (send,) = tied(token, self.send)
        self.came = lax.ppermute(send, AXES, self.halving[0])
        return send

    def halve(self, level, token):
        keep, came = tied(token, self.keep, self.came)
        groups, pieces, rows, _ = keep.shape
        shape = (groups // 2, pieces, rows, 128) if level < 3 else (1, pieces // 2, rows, 128)
        self.send, self.keep = call(
            functools.partial(plain_halve_kernel, level),
            [("v", shape, BF16)] * 2,
            [("s", self.me), ("v", keep), ("v", came)],
        )
        self.came = lax.ppermute(self.send, AXES, self.halving[level])
        return self.send

    def exchange(self, token):
        now = self.sum(self.keep, self.came, token)
        for stage in self.whole[:-1]:
            now = self.sum(now, lax.ppermute(now, AXES, stage), token)
        self.came = lax.ppermute(now, AXES, self.whole[-1])
        self.now = now
        return now

    def turn(self, token):
        self.now = self.sum(self.now, self.came, token)
        self.came = lax.ppermute(self.now, AXES, self.halving[-1])
        return self.now

    def sum(self, left, right, token):
        left, right = tied(token, left, right)
        return call(add_kernel, [("v", left.shape, BF16)], [("v", left), ("v", right)])[0]

    def double(self, level, token):
        now, came = tied(token, self.now, self.came)
        groups, pieces, rows, _ = now.shape
        if level == 2:
            (self.now,) = call(
                pair_kernel,
                [("v", (1, 2 * pieces, rows, 128), BF16)],
                [("s", self.me), ("v", now), ("v", came)],
            )
        else:
            (self.now,) = call(
                stack_kernel,
                [("v", (2, pieces, rows, 128), BF16)],
                [("v", now), ("v", came)],
            )
            self.twin = lax.ppermute(self.now, AXES, self.halving[0])
        self.came = lax.ppermute(self.now, AXES, self.halving[level])
        return self.now

    def last(self, token):
        (self.late,) = tied(token, self.came)
        self.late_twin = lax.ppermute(self.late, AXES, self.halving[0])
        return self.late


class SummedWithStates(Summed):
    def __init__(self, keep, send, halving, whole, adjoint, fades, own_len):
        super().__init__(keep, send, halving, whole)
        self.adjoint, self.fades, self.own_len = adjoint, fades, own_len
        self.core = jnp.full((1,), lax.axis_index("batch") & 1, jnp.int32)
        self.earlier = None

    def halve(self, level, token):
        keep, came = tied(token, self.keep, self.came)
        groups, pieces, rows, _ = keep.shape
        args = [("s", self.me), ("s", self.core)]
        args += [("v", t) for t in (self.fades, self.adjoint, keep, came)]
        if level < 3:
            kept = (groups // 2, pieces, rows, 128)
            extra = []
        else:
            kept = (1, pieces // 2, rows, 128)
            args.append(("v", self.earlier))
            extra = [("v", (H, D), BF16)] * 2
        sent = (kept[0] * kept[1] * rows + STATE, 128)
        self.send, self.keep, *states = call(
            functools.partial(halve_kernel, level, self.own_len),
            [("v", sent, BF16), ("v", kept, BF16)] + extra,
            args,
        )
        if states:
            self.others = [states[0]]
            self.group = states[1]
        self.earlier = came
        self.came = lax.ppermute(self.send, AXES, self.halving[level])
        return self.send

    def exchange(self, token):
        keep, came = tied(token, self.keep, self.came)
        self.others.append(came)
        _, pieces, rows, _ = keep.shape
        self.shape = keep.shape
        (self.now,) = call(
            functools.partial(exchange_kernel, self.own_len),
            [("v", (pieces * rows + STATE, 128), BF16)],
            [("s", self.me)] + [("v", t) for t in (self.fades, self.group, keep, came)],
        )
        self.came = lax.ppermute(self.now, AXES, self.whole[-1])
        return self.now

    def turn(self, token):
        now, came = tied(token, self.now, self.came)
        self.others.append(came)
        (self.now,) = call(
            add_start_kernel, [("v", self.shape, BF16)], [("v", now), ("v", came)]
        )
        self.came = lax.ppermute(self.now, AXES, self.halving[-1])
        return self.now


def shifted_pairs(seqs, by):
    return [(i, i + by) for i in range(seqs) if 0 <= i + by < seqs]


def state_powers(seqs, own_len):
    reach = WINDOW // own_len
    if by_levels(own_len):
        return [float(own_len << i) for i in range(seqs.bit_length() - 1)]
    return [float(own_len * i) for i in range(min(seqs, reach))]


def by_levels(own_len):
    return lax.axis_size("seq") == 8 and 8 <= WINDOW // own_len


def states_before(state, fades, me, own_len, beside):
    if not by_levels(own_len):
        for run in beside:
            run(state)
        return [direct_states(state, fades, own_len, 1)]
    seqs = lax.axis_size("seq")
    group, others = state, []
    levels = seqs.bit_length() - 1
    for i in range(levels):
        others.append(lax.ppermute(group, "seq", [(j, j ^ (1 << i)) for j in range(seqs)]))
        token = beside[i](group)
        if i < levels - 1:
            (other,) = tied(token, others[-1])
            (group,) = call(
                functools.partial(join_kernel, own_len, i),
                [("v", state.shape, BF16)],
                [("s", me), ("v", group), ("v", other), ("v", fades)],
            )
    return others


def direct_states(state, fades, own_len, direction):
    seqs = lax.axis_size("seq")
    total = jnp.zeros(state.shape, F32)
    for k in range(1, min(seqs, WINDOW // own_len)):
        far = lax.ppermute(state, "seq", shifted_pairs(seqs, k * direction))
        total = total + moved(far.astype(F32), fades[k - 1], float((k - 1) * own_len))
    return total


def far_part(signal, log_decay, coeff):
    own_len = signal.shape[0]
    steps = jnp.arange(own_len).astype(F32)[:, None, None]
    held = jnp.exp(log_decay[None] * (WINDOW - 1.0 - steps)) * signal[:, None, :]
    after = lax.cumsum(held, axis=0, reverse=True) - held
    return jnp.sum(coeff[None] * jnp.exp(log_decay[None] * (steps + 1.0)) * after, axis=1)


def start_unpack(who, slots, chunk, results):
    segments, outs, scratch = PLANS[who]
    given = [("s", slots), ("v", chunk.now), ("v", chunk.twin)]
    alias = {}
    if who != "A" and "mix" in results:
        alias = {len(given): outs.index(MIX_OUT)}
        given.append(("o", results["mix"]))
    return call(
        functools.partial(unpack_kernel, segments, len(outs), len(alias), 0),
        outs,
        given,
        scratch(),
        alias=alias,
    )


def end_unpack(who, slots, chunk, results):
    given = [("s", slots), ("v", chunk.late), ("v", chunk.late_twin)]
    if who == "C":
        return call(
            unpack_rest_kernel,
            PLANS[who][1]
            + [("v", (H, D), F32)] * 4
            + [("v", (1, D), F32)] * 3
            + [("v", (3, Z), F32)],
            given
            + [("v", chunk.now), ("v", chunk.twin)]
            + [("o", results["mix"]), ("o", results["C"][1])],
            rest_buffers()[:-1] + [pltpu.VMEM((512, 128), F32), pltpu.SemaphoreType.DMA((12,))],
            alias={5: 0, 6: 1},
        )
    segments, outs, scratch = PLANS[who]
    before = list(results[who])
    if who != "A":
        before[outs.index(MIX_OUT)] = results["mix"]
    return call(
        functools.partial(unpack_kernel, segments, len(outs), len(outs), 2),
        outs,
        given + [("o", t) for t in before],
        scratch(),
        alias={3 + i: i for i in range(len(outs))},
    )


def wide(*shapes):
    buffers = [pltpu.VMEM((4, rows // 8, cols), F32) for rows, cols in shapes]
    return buffers + [pltpu.SemaphoreType.DMA((4 * len(shapes),))]


def rest_buffers():
    return wide((D, V), (D, Z), (D, V))


MIX_OUT = ("o", (D, MIX), F32)
PLANS = {
    "A": (
        ffn_segments,
        [("o", (FF, D), F32), ("o", (D, FF), F32)],
        lambda: wide((FF, D), (D, FF)),
    ),
    "B": (
        gates_segments,
        [("o", (V, D), F32), MIX_OUT],
        lambda: wide((V, D), (D, D), (D, D)),
    ),
    "C": (rest_segments, [MIX_OUT, ("o", (D, V), F32)], rest_buffers),
}


ORDER = (
    "Ac", "F", "Ah1", "G", "Bc", "T", "Bh1", "E", "Cc", "Ah2", "O", "Bh2", "Ah3", "Ch1", "Bh3",
    "Ax", "Ch2", "At", "Bx", "Ad2", "Ch3", "Bt", "Ad1", "Cx", "Bd2", "Aa", "Ct", "Bd1", "K",
    "Ad0", "Cd2", "Ba", "Bd0", "Cd1", "Au", "Ca", "Bu", "Cd0", "Cu",
)


def advance(chunk, who, what, token, slots, results):
    if what == "c":
        return chunk.first(token)
    if what == "x":
        return chunk.exchange(token)
    if what == "t":
        return chunk.turn(token)
    if what[0] == "h":
        return chunk.halve(int(what[1:]), token)
    if what == "d0":
        return chunk.last(token)
    if what[0] == "d":
        return chunk.double(int(what[1:]), token)
    if what == "a":
        chunk.now, chunk.twin = tied(token, chunk.now, chunk.twin)
        results[who] = list(start_unpack(who, slots, chunk, results))
    else:
        chunk.late, chunk.late_twin = tied(token, chunk.late, chunk.late_twin)
        results[who] = list(end_unpack(who, slots, chunk, results))
    if who != "A":
        results["mix"] = results[who][1 if who == "B" else 0]
    return results[who][0]


def on_device(
    inputs,
    lengths,
    key_mask,
    norm_gain,
    ema_expand,
    ema_alpha,
    ema_delta,
    ema_eta,
    ema_omega,
    w_value,
    w_mix,
    qk_affine,
    w_hidden,
    ffn_gain,
    w_up,
    w_down,
    cotangent,
):
    _, rows, _ = inputs.shape
    seqs = lax.axis_size("seq")
    reach = WINDOW // rows
    halving, whole = exchanges(lax.axis_size("batch"), seqs)
    slots = slot_table()
    limit = lengths - lax.axis_index("seq") * rows
    x = inputs.reshape(rows, D)
    cot = cotangent.reshape(rows, D)
    expand, alpha, delta, eta = ema_expand.T, ema_alpha.T, ema_delta.T, ema_eta.T
    omega = ema_omega.reshape(1, D)
    gain1 = norm_gain.reshape(1, D)
    gain2 = ffn_gain.reshape(1, D)
    powers = state_powers(seqs, rows)
    me = jnp.full((1,), lax.axis_index("seq"), jnp.int32)

    def buffers(tiles):
        return [("v", (4, 4, tiles * 16, 128), BF16)] * 2

    tall = rows * 8 * (D // LANES)
    normed, masked, state, decay, coeff, fades, w_value_near = call(
        functools.partial(norm_kernel, rows, powers),
        [
            ("v", (rows, D), BF16),
            ("v", (rows, D), BF16),
            ("v", (2 * H, D), BF16),
            ("v", (H, D), F32),
            ("v", (H, D), F32),
            ("v", (len(powers), H, D), F32),
            ("v", (D, V), BF16),
        ],
        [("s", limit), ("h", x), ("h", gain1)]
        + [("h", t) for t in (alpha, delta, expand, eta)]
        + [("o", w_value)],
        [pltpu.VMEM((rows, D), F32), pltpu.SemaphoreType.DMA((1,))],
    )
    early = {}

    def own_ema(token):
        (signal,) = tied(token, masked)
        early["local"], early["mix"] = call(
            functools.partial(local_kernel, rows),
            [("v", (rows, D), F32), ("v", (D, MIX), BF16)],
            [("v", signal), ("v", decay), ("v", coeff), ("o", w_mix)],
            [
                pltpu.VMEM((rows, D), F32),
                pltpu.VMEM((tall, LANES), F32),
                pltpu.SemaphoreType.DMA((1,)),
            ],
        )
        return early["local"]

    def own_values(token):
        (rows_in,) = tied(token, normed)
        early["value_pre"], early["value_low"], early["up"], early["down"] = call(
            value_kernel,
            [
                ("v", (rows, V), F32),
                ("v", (rows, V), BF16),
                ("v", (D, FF), BF16),
                ("v", (FF, D), BF16),
            ],
            [("v", rows_in), ("v", w_value_near), ("o", w_up), ("o", w_down)],
            [pltpu.SemaphoreType.DMA((2,))],
        )
        return early["value_low"]

    def own_inner(token):
        (down,) = tied(token, early["down"])
        early["inner"], early["hidden"] = call(
            inner_kernel,
            [("v", (rows, FF), F32), ("v", (V, D), BF16)],
            [("v", down), ("h", cot), ("o", w_hidden)],
            [pltpu.SemaphoreType.DMA((1,))],
        )
        return early["inner"]

    others = states_before(state, fades, me, rows, (own_ema, own_values, own_inner))
    w_mix_near, w_hidden_near = early["mix"], early["hidden"]
    value_pre, value_low = early["value_pre"], early["value_low"]
    far_here = seqs > reach
    far, far_back, far_tables = [], [], []
    if far_here:
        behind = lax.ppermute(masked, "seq", shifted_pairs(seqs, reach)).astype(F32)
        edge, far_pull = jax.vjp(far_part, behind, jnp.log(decay), coeff)
        far = [("h", edge)]
    (
        carry,
        pre,
        mix_low,
        mixed,
        probs,
        attended,
        gated,
        cand_pre,
        resid,
        inner_low,
        g_up_low,
        keep1,
        send1,
    ) = call(
        functools.partial(forward_kernel, rows, len(others), far_here),
        [
            ("v", (2 * H, D), F32),
            ("v", (rows, D), F32),
            ("v", (rows, D), BF16),
            ("v", (rows, MIX), F32),
            ("v", (rows, BLOCK), F32),
            ("v", (rows, V), F32),
            ("v", (rows, V), BF16),
            ("v", (rows, D), F32),
            ("v", (rows, D), F32),
            ("v", (rows, FF), BF16),
            ("v", (rows, FF), BF16),
        ]
        + buffers(16),
        [("s", limit), ("s", me), ("s", slots)]
        + [("v", t) for t in (fades, masked, value_low, decay, coeff)]
        + [("v", t) for t in (w_mix_near, w_hidden_near, early["up"])]
        + [("v", t) for t in (early["local"], early["inner"], *others)]
        + far
        + [("h", t) for t in (omega, qk_affine, key_mask, x, gain2, cot)],
        [
            pltpu.VMEM((tall, LANES), F32),
            pltpu.VMEM((rows, FF), F32),
            pltpu.VMEM((rows, D), BF16),
        ],
    )
    token = resid
    chunks = {"A": Summed(keep1, send1, halving, whole)}
    results = {}
    for step in ORDER:
        who, what = step[0], step[1:]
        if step == "F":
            (g_up_low,) = tied(token, g_up_low)
            keep2, send2, g_resid, g_ffn_gain, g_hid = call(
                resid_kernel,
                buffers(16)
                + [("v", (rows, D), F32), ("v", (1, D), F32), ("v", (rows, D), BF16)],
                [("s", slots), ("h", cot), ("h", gain2)]
                + [("v", t) for t in (resid, g_up_low, early["up"], mixed, cand_pre, gated)],
            )
            token = g_resid
        elif step == "O":
            (inner_low,) = tied(token, inner_low)
            (out,) = call(
                output_kernel,
                [("v", (rows, D), BF16)],
                [("v", resid), ("v", inner_low), ("h", w_down)],
            )
            token = out
        elif step == "G":
            (g_resid,) = tied(token, g_resid)
            keep2, send2, g_skip, g_upd, g_reset, g_att = call(
                gates_kernel,
                buffers(16)
                + [
                    ("v", (rows, D), F32),
                    ("v", (rows, D), BF16),
                    ("v", (rows, V), BF16),
                    ("v", (rows, V), BF16),
                ],
                [("s", slots), ("v", keep2), ("v", send2), ("h", x), ("v", w_hidden_near)]
                + [("v", t) for t in (mix_low, mixed, attended, cand_pre, g_resid, g_hid)],
                alias={1: 0, 2: 1},
            )
            chunks["B"] = Summed(keep2, send2, halving, whole)
            token = g_skip
        elif step == "T":
            (g_att,) = tied(token, g_att)
            keep3, send3, g_qk, g_shared, g_normed = call(
                functools.partial(attention_kernel, rows),
                buffers(18) + [("v", (3, Z), F32), ("v", (rows, Z), BF16), ("v", (rows, D), F32)],
                [("s", slots)]
                + [
                    ("v", t)
                    for t in (
                        normed,
                        value_pre,
                        value_low,
                        mix_low,
                        mixed,
                        probs,
                        g_att,
                        g_reset,
                        w_value_near,
                    )
                ]
                + [("h", qk_affine)],
            )
            token = g_normed
        elif step == "E":
            (g_upd,) = tied(token, g_upd)
            if far_here:
                g_mixed = jnp.concatenate([g_upd, g_shared, g_reset, g_hid], axis=1)
                g_early = lax.dot_general(
                    g_mixed, w_mix, (((1,), (1,)), ((), ())), preferred_element_type=F32
                )
                sig = jax.nn.sigmoid(pre)
                g_behind, far_log, far_coeff = far_pull(g_early * (sig * (1.0 + pre * (1.0 - sig))))
                far_tables = [("h", jnp.concatenate([far_coeff, far_log], axis=0))]
                g_far = lax.ppermute(g_behind.astype(BF16), "seq", shifted_pairs(seqs, -reach))
                far_back = [("h", g_far.astype(F32))]
            keep3, send3, g_pre, adjoint = call(
                functools.partial(tables_kernel, rows, far_here),
                buffers(18) + [("v", (rows, D), F32), ("v", (H, D), BF16)],
                [("s", slots)]
                + [
                    ("v", t)
                    for t in (
                        keep3,
                        send3,
                        masked,
                        normed,
                        pre,
                        g_upd,
                        g_shared,
                        g_reset,
                        g_hid,
                        g_normed,
                        g_qk,
                        g_ffn_gain,
                        carry,
                        decay,
                        coeff,
                        w_mix_near,
                    )
                ]
                + far_tables
                + [("h", t) for t in (expand, alpha, delta, eta, gain1)],
                [pltpu.VMEM((rows, D), F32), pltpu.VMEM((512, 128), F32)],
                alias={1: 0, 2: 1},
            )
            if by_levels(rows):
                chunks["C"] = SummedWithStates(
                    keep3, send3, halving, whole, adjoint, fades, rows
                )
            else:
                chunks["C"] = Summed(keep3, send3, halving, whole)
                chunks["C"].others = [direct_states(adjoint, fades, rows, -1)]
            token = g_pre
        elif step == "K":
            others = chunks["C"].others
            (g_pre,) = tied(token, g_pre)
            (d_input,) = call(
                functools.partial(input_kernel, rows, len(others), far_here),
                [("v", (rows, D), BF16)],
                [("s", limit), ("s", me)]
                + [("v", t) for t in (fades, g_pre, g_skip, g_normed, decay, coeff)]
                + [("v", t) for t in others]
                + far_back
                + [("h", t) for t in (x, omega, gain1)],
                [pltpu.VMEM((tall, LANES), F32), pltpu.VMEM((rows, D), F32)],
            )
            token = d_input
        else:
            token = advance(chunks[who], who, what, token, slots, results)
    grad_down, grad_up = results["A"]
    grad_hidden, _ = results["B"]
    grad_mix = results["mix"]
    (
        _,
        grad_value,
        g_expand,
        g_alpha,
        g_delta,
        g_eta,
        g_norm_gain,
        g_omega,
        g_ffn_gain,
        g_qk,
    ) = results["C"]
    return (
        out.reshape(inputs.shape),
        d_input.reshape(inputs.shape),
        g_norm_gain.reshape(D),
        g_expand.T,
        g_alpha.T,
        g_delta.T,
        g_eta.T,
        g_omega.reshape(D),
        grad_value,
        grad_mix,
        g_qk,
        grad_hidden,
        g_ffn_gain.reshape(D),
        grad_up,
        grad_down,
    )


def solution(mesh):
    row = P("batch", "seq", None)
    return jax.shard_map(
        on_device,
        mesh=mesh,
        in_specs=(row, P("batch"), P("batch", "seq")) + (P(),) * 13 + (row,),
        out_specs=(row, row) + (P(),) * 13,
        check_vma=False,
    )
```

```python
import functools

import jax
import jax.numpy as jnp
from jax import lax
from jax.experimental import pallas as pl
from jax.experimental.pallas import tpu as pltpu
from jax.sharding import PartitionSpec as P

D = 512
Z = 128
V = 1024
H = 16
FF = 1024
BLOCK = 128
WINDOW = 4096
MIX = 2 * D + Z + V
AXES = ("batch", "seq")
F32 = jnp.float32
BF16 = jnp.bfloat16
COSTS = {
    "norm_kernel": 10**9,
    "join_kernel": 10**9,
    "local_kernel": 10**9,
    "value_kernel": 10**9,
    "inner_kernel": 10**9,
    "forward_kernel": 10**9,
    "resid_kernel": 10**9,
    "gates_kernel": 10**9,
    "output_kernel": 10**9,
    "attention_kernel": 12 * 10**9,
    "tables_kernel": 10**9,
    "local_back_kernel": 10**9,
    "input_kernel": 10**9,
}
VMEM_LIMIT = 24 * 2**20


def sigmoid(v):
    return 1.0 / (1.0 + jnp.exp(-v))


def dot(a, b):
    return lax.dot_general(a, b, (((1,), (0,)), ((), ())), preferred_element_type=F32)


def dot_nt(a, b):
    return lax.dot_general(a, b, (((1,), (1,)), ((), ())), preferred_element_type=F32)


def dot_tn(a, b):
    return lax.dot_general(a, b, (((0,), (0,)), ((), ())), preferred_element_type=F32)


class Late:
    def __init__(self, copy, ref):
        self.copy, self.ref, self.waited = copy, ref, False

    def __call__(self):
        if not self.waited:
            self.copy.wait()
            self.waited = True
        return self.ref


SPACES = {"s": pltpu.SMEM, "v": pltpu.VMEM, "h": pltpu.HBM, "o": pltpu.HBM}


def call(body, outs, args, scratch=(), alias=None):
    late = [i for i, (kind, _) in enumerate(args) if kind == "h"]
    n_in, n_out = len(args), len(outs)

    def run(*refs):
        ins = list(refs[:n_in])
        mine = refs[n_in : n_in + n_out + len(scratch)]
        if late:
            rest = refs[n_in + n_out + len(scratch) :]
            for k, i in enumerate(late):
                copy = pltpu.make_async_copy(ins[i], rest[k], rest[-1].at[k])
                copy.start()
                ins[i] = Late(copy, rest[k])
        body(*ins, *mine)
        for i in late:
            ins[i]()

    name = getattr(body, "func", body).__name__
    buffers = [pltpu.VMEM(args[i][1].shape, args[i][1].dtype) for i in late]
    if late:
        buffers.append(pltpu.SemaphoreType.DMA((len(late),)))
    return pl.pallas_call(
        run,
        out_shape=[jax.ShapeDtypeStruct(shape, dtype) for _, shape, dtype in outs],
        in_specs=[pl.BlockSpec(memory_space=SPACES[kind]) for kind, _ in args],
        out_specs=[pl.BlockSpec(memory_space=SPACES[kind]) for kind, _, _ in outs],
        scratch_shapes=list(scratch) + buffers,
        input_output_aliases=alias or {},
        compiler_params=pltpu.CompilerParams(vmem_limit_bytes=VMEM_LIMIT),
        name=name,
        cost_estimate=pl.CostEstimate(
            flops=COSTS.get(name, 10**10), bytes_accessed=0, transcendentals=0
        ),
    )(
        *[
            pltpu.with_memory_space_constraint(array, pltpu.HBM) if kind in "ho" else array
            for kind, array in args
        ]
    )


def row8(ref, t):
    return jnp.broadcast_to(ref[pl.ds(t, 1), :], (8, D))


LANES = 128


def put8(part_ref, t, rows, eight):
    for j in range(D // LANES):
        base = pl.multiple_of(j * rows * 8 + t * 8, 8)
        part_ref[pl.ds(base, 8), :] = eight[:, j * LANES : (j + 1) * LANES]


def fold8(part_ref, out_ref, rows):
    def one(g, _):
        at = pl.multiple_of(g * 8, 8)
        for j in range(D // LANES):
            base = pl.multiple_of(j * rows * 8 + g * 64, 64)
            acc = part_ref[pl.ds(base, 8, stride=8), :]
            for k in range(1, 8):
                acc = acc + part_ref[pl.ds(base + k, 8, stride=8), :]
            out_ref[pl.ds(at, 8), j * LANES : (j + 1) * LANES] = acc
        return 0

    lax.fori_loop(0, rows // 8, one, 0)


def norm_kernel(
    rows,
    powers,
    lim_ref,
    x,
    gain,
    alpha,
    delta,
    expand,
    eta,
    wvalue_ref,
    normed_ref,
    masked_ref,
    state_ref,
    a_ref,
    c_ref,
    fade_ref,
    wvalue_out_ref,
    m_ref,
    sem,
):
    copies = bring(((wvalue_ref, wvalue_out_ref),), sem)
    x = x()[...].astype(F32)
    center = jnp.mean(x, axis=1, keepdims=True)
    shifted = x - center
    spread = jnp.mean(shifted * shifted, axis=1, keepdims=True)
    normed = (shifted * lax.rsqrt(spread + 1e-05) * gain()[...]).astype(BF16)
    normed_ref[...] = normed
    place = lax.broadcasted_iota(jnp.int32, (rows, 1), 0)
    masked = jnp.where(place < lim_ref[0], normed.astype(F32), 0.0)
    masked_ref[...] = masked.astype(BF16)
    m_ref[...] = masked
    alpha = sigmoid(alpha()[...])
    decay = 1.0 - alpha * sigmoid(delta()[...])
    a_ref[...] = decay
    c_ref[...] = eta()[...] * alpha * expand()[...]
    log_decay = jnp.log(decay)
    for i, power in enumerate(powers):
        fade_ref[i] = jnp.exp(log_decay * power)
    a = (decay[0:8, :], decay[8:16, :])

    def step(g, carry):
        s, q = carry
        for k in range(8):
            row = row8(m_ref, g * 8 + k)
            grown = tuple(a[i] * s[i] for i in range(2))
            q = tuple(a[i] * q[i] + grown[i] for i in range(2))
            s = tuple(grown[i] + row for i in range(2))
        return s, q

    zero = jnp.zeros((8, D), F32)
    s, q = lax.fori_loop(0, rows // 8, step, ((zero, zero), (zero, zero)))
    state_ref[0:8, :] = s[0].astype(BF16)
    state_ref[8:16, :] = s[1].astype(BF16)
    state_ref[16:24, :] = q[0].astype(BF16)
    state_ref[24:32, :] = q[1].astype(BF16)
    for copy in copies:
        copy.wait()


def bring(pairs, sem):
    copies = []
    for i, (src, dst) in enumerate(pairs):
        copy = pltpu.make_async_copy(src, dst, sem.at[i])
        copy.start()
        copies.append(copy)
    return copies


def local_kernel(rows, masked_ref, a_ref, c_ref, wmix_ref, out_ref, wmix_out_ref, m_ref, part_ref, sem):
    copies = bring(((wmix_ref, wmix_out_ref),), sem)
    m_ref[...] = masked_ref[...].astype(F32)
    a = (a_ref[0:8, :], a_ref[8:16, :])
    c = (c_ref[0:8, :], c_ref[8:16, :])

    def step(g, s):
        for k in range(8):
            t = g * 8 + k
            row = row8(m_ref, t)
            s = tuple(a[i] * s[i] + row for i in range(2))
            put8(part_ref, t, rows, c[0] * s[0] + c[1] * s[1])
        return s

    zero = jnp.zeros((8, D), F32)
    lax.fori_loop(0, rows // 8, step, (zero, zero))
    fold8(part_ref, out_ref, rows)
    for copy in copies:
        copy.wait()


def value_kernel(
    normed_ref, wvalue_ref, wup_ref, wdown_ref, pre_ref, low_ref, wup_out_ref, wdown_out_ref, sem
):
    copies = bring(((wup_ref, wup_out_ref), (wdown_ref, wdown_out_ref)), sem)
    for lo in range(0, V, D):
        pre = dot(normed_ref[...], wvalue_ref[:, lo : lo + D])
        pre_ref[:, lo : lo + D] = pre
        low_ref[:, lo : lo + D] = (pre * sigmoid(pre)).astype(BF16)
    for copy in copies:
        copy.wait()


def inner_kernel(wdown_ref, cot, whid_ref, out_ref, whid_out_ref, sem):
    copies = bring(((whid_ref, whid_out_ref),), sem)
    out_ref[...] = dot_nt(cot()[...], wdown_ref[...])
    for copy in copies:
        copy.wait()


def moved(state, fade, steps):
    if state.shape[0] == H:
        return fade * state
    return jnp.concatenate([fade * state[:H], fade * (state[H:] + steps * state[:H])], axis=0)


def joined(own_len, level, direction, me, group, other, fades):
    late = ((me >> level) & 1) == (1 if direction == 1 else 0)
    first, second = jnp.where(late, other, group), jnp.where(late, group, other)
    return (moved(first, fades[level], float(own_len << level)) + second).astype(BF16)


def join_kernel(own_len, level, me_ref, group_ref, other_ref, fade_ref, out_ref):
    group, other = group_ref[...].astype(F32), other_ref[...].astype(F32)
    out_ref[...] = joined(own_len, level, 1, me_ref[0], group, other, fade_ref)


def carried(own_len, direction, me, others, fades):
    total = None
    for i, other in enumerate(others):
        blocks = me if direction == 1 else ~me
        late = ((me >> i) & 1) == (1 if direction == 1 else 0)
        for j in range(i):
            on = ((blocks >> j) & 1) == 1
            other = jnp.where(on, moved(other, fades[j], float(own_len << j)), other)
        other = jnp.where(late, other, 0.0)
        total = other if total is None else total + other
    return total


def place(slots_ref, dst, side, at, grad):
    rows, cols = grad.shape
    piece = rows // 16
    for g in range(4):
        slot = slots_ref[1 + 4 * side + g]
        for z in range(4):
            tile = at
            for lo in range((g * 4 + z) * piece, (g * 4 + z + 1) * piece, 16):
                for c in range(0, cols, 128):
                    dst[slot, z, tile * 16 : tile * 16 + 16, :] = grad[lo : lo + 16, c : c + 128]
                    tile += 1


def outer(slots_ref, keep_ref, send_ref, at, left_ref, right):
    half = left_ref.shape[1] // 2
    for side, dst in enumerate((keep_ref, send_ref)):
        core = slots_ref[0] ^ side
        left = left_ref[:, pl.ds(pl.multiple_of(core * half, half), half)]
        place(slots_ref, dst, side, at, dot_tn(left, right).astype(BF16))


def forward_kernel(
    rows,
    n_others,
    has_far,
    lim_ref,
    me_ref,
    slots_ref,
    fade_ref,
    masked_ref,
    value_ref,
    a_ref,
    c_ref,
    wmix_ref,
    whid_ref,
    wup_ref,
    local_ref,
    ginner_ref,
    *refs,
):
    others, refs = refs[:n_others], refs[n_others:]
    far, refs = (refs[0], refs[1:]) if has_far else (None, refs)
    (
        omega,
        qk,
        mask,
        x,
        gain,
        cot,
        carry_ref,
        pre_ref,
        mixlow_ref,
        mixed_ref,
        probs_ref,
        att_ref,
        gated_ref,
        candpre_ref,
        resid_ref,
        inner_ref,
        guplow_ref,
        keep_ref,
        send_ref,
        part_ref,
        up_ref,
        ffn_ref,
    ) = refs
    masked = masked_ref[...].astype(F32)
    if n_others == 1:
        carry_ref[...] = others[0][...].astype(F32)
    else:
        states = [ref[...].astype(F32) for ref in others]
        carry_ref[...] = carried(rows, 1, me_ref[0], states, fade_ref)
    a = (a_ref[0:8, :], a_ref[8:16, :])

    def step(g, s):
        for k in range(8):
            s = tuple(a[i] * s[i] for i in range(2))
            put8(part_ref, g * 8 + k, rows, s[0] + s[1])
        return s

    start = tuple(c_ref[i : i + 8, :] * carry_ref[i : i + 8, :] for i in (0, 8))
    lax.fori_loop(0, rows // 8, step, start)
    fold8(part_ref, pre_ref, rows)
    pre = pre_ref[...] + local_ref[...] + omega()[...] * masked
    if has_far:
        pre = pre + far()[...]
    pre_ref[...] = pre
    mix_low = (pre * sigmoid(pre)).astype(BF16)
    mixlow_ref[...] = mix_low
    shared_pre = dot(mix_low, wmix_ref[:, D : D + Z])
    mixed_ref[:, D : D + Z] = shared_pre
    shared = shared_pre * sigmoid(shared_pre)
    qk_ref, mask_ref = qk(), mask()
    query = (shared * qk_ref[0:1, :] + qk_ref[1:2, :]).astype(BF16)
    key = (shared * qk_ref[2:3, :]).astype(BF16)
    places = lax.broadcasted_iota(jnp.int32, (BLOCK, BLOCK), 0)
    others = lax.broadcasted_iota(jnp.int32, (BLOCK, BLOCK), 1)
    for g in range(rows // BLOCK):
        lo = g * BLOCK
        ok = (mask_ref[:, lo : lo + BLOCK] > 0) & (
            lax.broadcasted_iota(jnp.int32, (1, BLOCK), 1) + lo < lim_ref[0]
        )
        ok = jnp.broadcast_to(ok.astype(F32), (BLOCK, BLOCK)) > 0.5
        allowed = (places == others) | ((places > others) & ok)
        scores = dot_nt(query[lo : lo + BLOCK], key[lo : lo + BLOCK]) * (Z**-0.5)
        scores = jnp.where(allowed, scores, -1000000000.0)
        grown = jnp.exp(scores - jnp.max(scores, axis=1, keepdims=True))
        probs = grown / jnp.sum(grown, axis=1, keepdims=True)
        probs_ref[lo : lo + BLOCK, :] = probs
        att_ref[lo : lo + BLOCK, :] = dot(probs.astype(BF16), value_ref[lo : lo + BLOCK, :])
    for lo in range(0, V, 512):
        reset_pre = dot(mix_low, wmix_ref[:, D + Z + lo : D + Z + lo + 512])
        mixed_ref[:, D + Z + lo : D + Z + lo + 512] = reset_pre
        gate = reset_pre * sigmoid(reset_pre)
        gated_ref[:, lo : lo + 512] = (att_ref[:, lo : lo + 512] * gate).astype(BF16)
    gated = gated_ref[...]
    hidden_in = dot(mix_low, wmix_ref[:, D + Z + V :])
    mixed_ref[:, D + Z + V :] = hidden_in
    update_pre = dot(mix_low, wmix_ref[:, :D])
    mixed_ref[:, :D] = update_pre
    cand_pre = hidden_in + dot(gated, whid_ref[...])
    candpre_ref[...] = cand_pre
    cand = cand_pre * sigmoid(cand_pre)
    x = x()[...].astype(F32)
    resid = x + sigmoid(update_pre) * (cand - x)
    resid_ref[...] = resid
    unit, _ = unit_rows(resid)
    ffn_low = (unit * gain()[...]).astype(BF16)
    ffn_ref[...] = ffn_low
    up_ref[...] = dot(ffn_low, wup_ref[...])
    up = up_ref[...]
    sig = sigmoid(up)
    inner = (up * sig).astype(BF16)
    inner_ref[...] = inner
    outer(slots_ref, keep_ref, send_ref, 0, inner_ref, cot()[...])
    gup_low = (ginner_ref[...] * (sig * (1.0 + up * (1.0 - sig)))).astype(BF16)
    guplow_ref[...] = gup_low
    outer(slots_ref, keep_ref, send_ref, 8, ffn_ref, gup_low)


def unit_rows(rows):
    shifted = rows - jnp.mean(rows, axis=1, keepdims=True)
    inv = lax.rsqrt(jnp.mean(shifted * shifted, axis=1, keepdims=True) + 1e-05)
    return shifted * inv, inv


def norm_back(unit, inv, e):
    return inv * (
        e
        - jnp.mean(e, axis=1, keepdims=True)
        - unit * jnp.mean(e * unit, axis=1, keepdims=True)
    )


def output_kernel(resid_ref, inner_ref, wdown, out_ref):
    out_ref[...] = (resid_ref[...] + dot(inner_ref[...], wdown()[...])).astype(BF16)


def slope(v, sig):
    return sig * (1.0 + v * (1.0 - sig))


def resid_kernel(
    slots_ref,
    cot,
    gain,
    resid_ref,
    guplow_ref,
    wup_ref,
    mixed_ref,
    candpre_ref,
    gated_ref,
    keep_ref,
    send_ref,
    gres_ref,
    ggain_ref,
    ghid_ref,
):
    g_ffn = dot_nt(guplow_ref[...], wup_ref[...])
    unit, inv = unit_rows(resid_ref[...])
    ggain_ref[...] = jnp.sum(g_ffn * unit, axis=0, keepdims=True)
    g_resid = cot()[...].astype(F32) + norm_back(unit, inv, g_ffn * gain()[...])
    gres_ref[...] = g_resid
    cand_pre = candpre_ref[...]
    g_cand = g_resid * sigmoid(mixed_ref[:, :D]) * slope(cand_pre, sigmoid(cand_pre))
    g_hid = g_cand.astype(BF16)
    ghid_ref[...] = g_hid
    outer(slots_ref, keep_ref, send_ref, 0, gated_ref, g_hid)


def gates_kernel(
    slots_ref,
    keep_in_ref,
    send_in_ref,
    x,
    whid_ref,
    mixlow_ref,
    mixed_ref,
    att_ref,
    candpre_ref,
    gres_ref,
    ghid_ref,
    keep_ref,
    send_ref,
    gskip_ref,
    gupd_ref,
    greset_ref,
    gatt_ref,
):
    g_hid = ghid_ref[...]
    g_gated = dot_nt(g_hid, whid_ref[...])
    outer(slots_ref, keep_ref, send_ref, 12, mixlow_ref, g_hid)
    g_resid = gres_ref[...]
    update = sigmoid(mixed_ref[:, :D])
    cand_pre = candpre_ref[...]
    g_update = g_resid * update
    gskip_ref[...] = g_resid - g_update
    cand = cand_pre * sigmoid(cand_pre)
    g_upd = (g_update * (1.0 - update) * (cand - x()[...].astype(F32))).astype(BF16)
    gupd_ref[...] = g_upd
    outer(slots_ref, keep_ref, send_ref, 8, mixlow_ref, g_upd)
    reset_pre = mixed_ref[:, D + Z : D + Z + V]
    sig = sigmoid(reset_pre)
    gatt_ref[...] = (g_gated * (reset_pre * sig)).astype(BF16)
    greset_ref[...] = (g_gated * att_ref[...] * slope(reset_pre, sig)).astype(BF16)


def attention_kernel(
    rows,
    slots_ref,
    normed_ref,
    valuepre_ref,
    value_ref,
    mixlow_ref,
    mixed_ref,
    probs_ref,
    gatt_ref,
    greset_ref,
    wvalue_ref,
    qk,
    keep_ref,
    send_ref,
    gqk_ref,
    gshared_ref,
    gnorm_ref,
):
    qk_ref = qk()
    shared_pre = mixed_ref[:, D : D + Z]
    ssig = sigmoid(shared_pre)
    shared = shared_pre * ssig
    query = (shared * qk_ref[0:1, :] + qk_ref[1:2, :]).astype(BF16)
    key = (shared * qk_ref[2:3, :]).astype(BF16)
    g_query, g_key, g_value = [], [], []
    for g in range(rows // BLOCK):
        part = slice(g * BLOCK, (g + 1) * BLOCK)
        probs = probs_ref[part, :]
        g_probs = dot_nt(gatt_ref[part, :], value_ref[part, :])
        g_value.append(dot_tn(probs.astype(BF16), gatt_ref[part, :]))
        inner = jnp.sum(g_probs * probs, axis=1, keepdims=True)
        g_scores = (probs * (g_probs - inner) * (Z**-0.5)).astype(BF16)
        g_query.append(dot(g_scores, key[part]))
        g_key.append(dot_tn(g_scores, query[part]))
    g_query = jnp.concatenate(g_query, axis=0)
    g_key = jnp.concatenate(g_key, axis=0)
    g_value = jnp.concatenate(g_value, axis=0)
    gqk_ref[0:1, :] = jnp.sum(g_query * shared, axis=0, keepdims=True)
    gqk_ref[1:2, :] = jnp.sum(g_query, axis=0, keepdims=True)
    gqk_ref[2:3, :] = jnp.sum(g_key * shared, axis=0, keepdims=True)
    g_shared = g_query * qk_ref[0:1, :] + g_key * qk_ref[2:3, :]
    g_shared = (g_shared * slope(shared_pre, ssig)).astype(BF16)
    gshared_ref[...] = g_shared
    outer(slots_ref, keep_ref, send_ref, 8, mixlow_ref, g_shared)
    value_pre = valuepre_ref[...]
    vsig = sigmoid(value_pre)
    g_vpre = (g_value * slope(value_pre, vsig)).astype(BF16)
    outer(slots_ref, keep_ref, send_ref, 0, normed_ref, g_vpre)
    outer(slots_ref, keep_ref, send_ref, 9, mixlow_ref, greset_ref[...])
    gnorm_ref[...] = dot_nt(g_vpre, wvalue_ref[...])


SMALL = 4 * H + 4


def tables_kernel(
    rows,
    has_far,
    slots_ref,
    keep_in_ref,
    send_in_ref,
    masked_ref,
    normed_ref,
    pre_ref,
    gupd_ref,
    gshared_ref,
    greset_ref,
    ghid_ref,
    gnorm_ref,
    gqk_ref,
    gffn_ref,
    carry_ref,
    a_ref,
    c_ref,
    wmix_ref,
    *refs,
):
    far, refs = (refs[0], refs[1:]) if has_far else (None, refs)
    expand, alpha, delta, eta, gain, *refs = refs
    keep_ref, send_ref, gpre_ref, adj_ref, m_ref, small_ref = refs
    m_ref[...] = masked_ref[...].astype(F32)
    pre = pre_ref[...]
    psig = sigmoid(pre)
    g_mix_low = dot_nt(gupd_ref[...], wmix_ref[:, :D])
    g_mix_low += dot_nt(gshared_ref[...], wmix_ref[:, D : D + Z])
    g_mix_low += dot_nt(greset_ref[...], wmix_ref[:, D + Z : D + Z + V])
    g_mix_low += dot_nt(ghid_ref[...], wmix_ref[:, D + Z + V :])
    g_pre = g_mix_low * slope(pre, psig)
    gpre_ref[...] = g_pre
    a = (a_ref[0:8, :], a_ref[8:16, :])

    def step(g, carry):
        s, q, dc, dq, m = carry
        for k in range(8):
            t = g * 8 + k
            row = row8(m_ref, t)
            grad = row8(gpre_ref, t)
            late = row8(gpre_ref, rows - 1 - t)
            grown = tuple(a[i] * s[i] for i in range(2))
            q = tuple(a[i] * q[i] + grown[i] for i in range(2))
            s = tuple(grown[i] + row for i in range(2))
            dc = tuple(dc[i] + grad * s[i] for i in range(2))
            dq = tuple(dq[i] + grad * q[i] for i in range(2))
            m = tuple(a[i] * (m[i] + late) for i in range(2))
        return s, q, dc, dq, m

    zero = jnp.zeros((8, D), F32)
    _, _, dc, dq, m = lax.fori_loop(
        0,
        rows // 8,
        step,
        (
            (carry_ref[0:8, :], carry_ref[8:16, :]),
            (carry_ref[16:24, :], carry_ref[24:32, :]),
            (zero, zero),
            (zero, zero),
            (zero, zero),
        ),
    )
    adj_ref[0:8, :] = m[0].astype(BF16)
    adj_ref[8:16, :] = m[1].astype(BF16)
    g_coeff = jnp.concatenate(dc, axis=0)
    g_log = c_ref[...] * jnp.concatenate(dq, axis=0)
    if has_far:
        far_ref = far()
        g_coeff, g_log = g_coeff + far_ref[0:H, :], g_log + far_ref[H:, :]
    expand, eta = expand()[...], eta()[...]
    alpha, delta = sigmoid(alpha()[...]), sigmoid(delta()[...])
    g_log = g_log / a_ref[...]
    g_expand = g_coeff * (eta * alpha)
    g_eta = g_coeff * (alpha * expand)
    g_alpha = (g_coeff * (eta * expand) - g_log * delta) * (alpha * (1.0 - alpha))
    g_delta = -(g_log * alpha) * (delta * (1.0 - delta))
    small_ref[...] = jnp.zeros_like(small_ref)
    for i, part in enumerate((g_expand, g_alpha, g_delta, g_eta)):
        for j in range(D // LANES):
            at = (i * 4 + j) * H
            small_ref[at : at + H, :] = part[:, j * LANES : (j + 1) * LANES]
    g_gain = jnp.sum(
        g_pre * pre + normed_ref[...].astype(F32) * gnorm_ref[...], axis=0, keepdims=True
    ) / gain()[...]
    g_omega = jnp.sum(g_pre * m_ref[...], axis=0, keepdims=True)
    for i, part in enumerate((g_gain, g_omega, gffn_ref[...])):
        for j in range(D // LANES):
            at = 16 * H + j * H + i
            small_ref[at : at + 1, :] = part[:, j * LANES : (j + 1) * LANES]
    for j in range(3):
        at = 16 * H + j * H + 3
        small_ref[at : at + 1, :] = gqk_ref[j : j + 1, :]
    for side, dst in enumerate((keep_ref, send_ref)):
        row = pl.multiple_of((slots_ref[0] ^ side) * 256, 256)
        place(slots_ref, dst, side, 17, small_ref[pl.ds(row, 256), :].astype(BF16))


def local_back_kernel(rows, gpre_ref, a_ref, c_ref, gx_ref, part_ref):
    a = (a_ref[0:8, :], a_ref[8:16, :])
    c = (c_ref[0:8, :], c_ref[8:16, :])

    def back(g, m):
        for k in range(8):
            t = rows - 1 - (g * 8 + k)
            row = row8(gpre_ref, t)
            lam = tuple(m[i] + row for i in range(2))
            put8(part_ref, t, rows, c[0] * lam[0] + c[1] * lam[1])
            m = tuple(a[i] * lam[i] for i in range(2))
        return m

    zero = jnp.zeros((8, D), F32)
    lax.fori_loop(0, rows // 8, back, (zero, zero))
    fold8(part_ref, gx_ref, rows)


def input_kernel(
    rows,
    n_others,
    has_far,
    lim_ref,
    me_ref,
    fade_ref,
    gpre_ref,
    glocal_ref,
    gskip_ref,
    gnorm_ref,
    a_ref,
    c_ref,
    *refs,
):
    others, refs = refs[:n_others], refs[n_others:]
    far, refs = (refs[0], refs[1:]) if has_far else (None, refs)
    x, omega, gain, din_ref, part_ref, gx_ref = refs
    if n_others == 1:
        adjoint = others[0][...].astype(F32)
    else:
        adjoint = carried(rows, -1, me_ref[0], [state_in(ref) for ref in others], fade_ref)
    a = (a_ref[0:8, :], a_ref[8:16, :])

    def back(g, m):
        for k in range(8):
            put8(part_ref, rows - 1 - (g * 8 + k), rows, m[0] + m[1])
            m = tuple(a[i] * m[i] for i in range(2))
        return m

    start = tuple(c_ref[i : i + 8, :] * adjoint[i : i + 8, :] for i in (0, 8))
    lax.fori_loop(0, rows // 8, back, start)
    fold8(part_ref, gx_ref, rows)
    g_masked = gx_ref[...] + glocal_ref[...] + omega()[...] * gpre_ref[...]
    if has_far:
        g_masked = g_masked + far()[...]
    place = lax.broadcasted_iota(jnp.int32, (rows, 1), 0)
    e = jnp.where(place < lim_ref[0], g_masked, 0.0) + gnorm_ref[...]
    x = x()[...].astype(F32)
    shifted = x - jnp.mean(x, axis=1, keepdims=True)
    inv = lax.rsqrt(jnp.mean(shifted * shifted, axis=1, keepdims=True) + 1e-05)
    unit = shifted * inv
    e = e * gain()[...]
    g_in = inv * (
        e
        - jnp.mean(e, axis=1, keepdims=True)
        - unit * jnp.mean(e * unit, axis=1, keepdims=True)
    )
    din_ref[...] = (g_in + gskip_ref[...]).astype(BF16)


def unpack(slots_ref, sources, first, segments, sem):
    copies = []
    for at, rows, cols, buffer_ref, out_ref, col in segments:
        group, piece = rows // 8, rows // 32
        for side, src in sources:
            for slot in range(2):
                block = len(copies) % 4
                for z in range(4):
                    tile = at
                    for lo in range(z * piece, (z + 1) * piece, 16):
                        for c in range(0, cols, 128):
                            buffer_ref[block, lo : lo + 16, c : c + 128] = src[
                                slot, z, tile * 16 : tile * 16 + 16, :
                            ].astype(F32)
                            tile += 1
                place_of = slots_ref[9 + 4 * side + first + slot]
                row = pl.multiple_of(
                    (slots_ref[0] ^ side) * (rows // 2) + place_of * group, group
                )
                copy = pltpu.make_async_copy(
                    buffer_ref.at[block],
                    out_ref.at[pl.ds(row, group), pl.ds(col, cols)],
                    sem.at[len(copies)],
                )
                copy.start()
                copies.append(copy)
    return copies


def ffn_segments(down_buf, up_buf, down_ref, up_ref):
    return [(0, FF, D, down_buf, down_ref, 0), (8, D, FF, up_buf, up_ref, 0)]


def gates_segments(hid_buf, upd_buf, in_buf, hid_ref, mix_ref):
    return [
        (0, V, D, hid_buf, hid_ref, 0),
        (8, D, D, upd_buf, mix_ref, 0),
        (12, D, D, in_buf, mix_ref, D + Z + V),
    ]


def rest_segments(value_buf, shared_buf, reset_buf, mix_ref, value_ref):
    return [
        (0, D, V, value_buf, value_ref, 0),
        (8, D, Z, shared_buf, mix_ref, D),
        (9, D, V, reset_buf, mix_ref, D + Z),
    ]


def unpack_kernel(segments, n_out, n_given, first, slots_ref, mine_ref, twin_ref, *refs):
    refs = refs[n_given:]
    outs, refs = refs[:n_out], refs[n_out:]
    parts = segments(*refs[:-1], *outs)
    for copy in unpack(slots_ref, ((0, mine_ref), (1, twin_ref)), first, parts, refs[-1]):
        copy.wait()


def unpack_own_kernel(
    slots_ref, mine_ref, mix_in_ref, value_in_ref, mix_ref, value_ref, *refs
):
    parts = rest_segments(*refs[:-1], mix_ref, value_ref)
    for copy in unpack(slots_ref, ((0, mine_ref),), 2, parts, refs[-1]):
        copy.wait()


def unpack_rest_kernel(
    slots_ref,
    mine_ref,
    twin_ref,
    early_ref,
    twin_early_ref,
    mix_in_ref,
    value_in_ref,
    mix_ref,
    value_ref,
    expand_ref,
    alpha_ref,
    delta_ref,
    eta_ref,
    gain_ref,
    omega_ref,
    ffn_ref,
    qk_ref,
    value_buf,
    shared_buf,
    reset_buf,
    small_ref,
    sem,
):
    parts = rest_segments(value_buf, shared_buf, reset_buf, mix_ref, value_ref)
    copies = unpack(slots_ref, ((1, twin_ref),), 2, parts, sem)
    for side, pair in enumerate(((early_ref, mine_ref), (twin_early_ref, twin_ref))):
        for slot in range(4):
            place_of = slots_ref[9 + 4 * side + slot]
            row = pl.multiple_of((slots_ref[0] ^ side) * 256 + place_of * 64, 64)
            for z in range(4):
                small_ref[pl.ds(row + z * 16, 16), :] = pair[slot // 2][
                    slot % 2, z, 17 * 16 : 18 * 16, :
                ].astype(F32)
    for i, out_ref in enumerate((expand_ref, alpha_ref, delta_ref, eta_ref)):
        for j in range(D // LANES):
            at = (i * 4 + j) * H
            out_ref[:, j * LANES : (j + 1) * LANES] = small_ref[at : at + H, :]
    for i, out_ref in enumerate((gain_ref, omega_ref, ffn_ref)):
        for j in range(D // LANES):
            at = 16 * H + j * H + i
            out_ref[:, j * LANES : (j + 1) * LANES] = small_ref[at : at + 1, :]
    for j in range(3):
        at = 16 * H + j * H + 3
        qk_ref[j : j + 1, :] = small_ref[at : at + 1, :]
    for copy in copies:
        copy.wait()


def added(left, right):
    return (left.astype(F32) + right.astype(F32)).astype(BF16)


def plain_halve_kernel(level, me_ref, keep_ref, came_ref, send_ref, kept_ref):
    if level < 3:
        half = keep_ref.shape[0] // 2
        send_ref[...] = added(keep_ref[half:], came_ref[half:])
        kept_ref[...] = added(keep_ref[:half], came_ref[:half])
        return
    half = keep_ref.shape[1] // 2
    mine = (me_ref[0] >> 1) & 1
    other = pl.ds((1 - mine) * half, half)
    send_ref[0] = added(keep_ref[0, other], came_ref[0, other])
    own = pl.ds(mine * half, half)
    kept_ref[0] = added(keep_ref[0, own], came_ref[0, own])


def add_kernel(left_ref, right_ref, out_ref):
    out_ref[...] = added(left_ref[...], right_ref[...])


def add_start_kernel(left_ref, right_ref, out_ref):
    pieces, rows = out_ref.shape[1:3]
    for i in range(pieces):
        part = slice(i * rows, (i + 1) * rows)
        out_ref[0, i] = added(left_ref[part, :], right_ref[part, :])


def pair_kernel(me_ref, now_ref, came_ref, out_ref):
    half = now_ref.shape[1]
    mine = (me_ref[0] >> 1) & 1
    out_ref[0, pl.ds(mine * half, half)] = now_ref[0]
    out_ref[0, pl.ds((1 - mine) * half, half)] = came_ref[0]


def stack_kernel(now_ref, came_ref, out_ref):
    out_ref[0] = now_ref[0]
    out_ref[1] = came_ref[0]


STATE = 4 * H


def state_in(ref):
    if ref.shape[1] == D:
        return ref[...].astype(F32)
    base = ref.shape[0] - STATE
    return jnp.concatenate([ref[base + j * H : base + (j + 1) * H, :] for j in range(4)], axis=1).astype(F32)


def put_state(ref, state):
    base = ref.shape[0] - STATE
    for j in range(4):
        ref[base + j * H : base + (j + 1) * H, :] = state[:, j * LANES : (j + 1) * LANES].astype(BF16)


def halve_kernel(level, own_len, me_ref, core_ref, fade_ref, adj_ref, keep_ref, came_ref, *refs):
    groups, pieces, rows, _ = keep_ref.shape
    size = pieces * rows

    def sums(g, z0, zn):
        keep = keep_ref[g, pl.ds(z0, zn)].reshape(zn * rows, 128)
        if len(came_ref.shape) == 4:
            came = came_ref[g, pl.ds(z0, zn)].reshape(zn * rows, 128)
        else:
            start = g * size + z0 * rows
            came = came_ref[pl.ds(pl.multiple_of(start, 16), zn * rows), :]
        return added(keep, came)

    if level < 3:
        send_ref, kept_ref = refs
        put_state(send_ref, adj_ref[...].astype(F32))
        half = groups // 2
        for g in range(half):
            send_ref[g * size : (g + 1) * size, :] = sums(half + g, 0, pieces)
        for g in range(half):
            kept_ref[g] = sums(g, 0, pieces).reshape(pieces, rows, 128)
        return
    first_ref, send_ref, kept_ref, other_ref, group_ref = refs
    me = me_ref[0]
    mine = (me >> 1) & 1
    other = jnp.where(core_ref[0] == 1, state_in(first_ref), state_in(came_ref))
    other_ref[...] = other.astype(BF16)
    group = joined(own_len, 0, -1, me, adj_ref[...].astype(F32), other, fade_ref)
    group_ref[...] = group
    put_state(send_ref, group.astype(F32))
    half = pieces // 2
    send_ref[: half * rows, :] = sums(0, (1 - mine) * half, half)
    kept_ref[0] = sums(0, mine * half, half).reshape(half, rows, 128)


def exchange_kernel(own_len, me_ref, fade_ref, group_ref, keep_ref, came_ref, now_ref):
    _, pieces, rows, _ = keep_ref.shape
    keep = keep_ref[0].reshape(pieces * rows, 128)
    now_ref[: pieces * rows, :] = added(keep, came_ref[: pieces * rows, :])
    group, other = group_ref[...].astype(F32), state_in(came_ref)
    put_state(now_ref, joined(own_len, 1, -1, me_ref[0], group, other, fade_ref).astype(F32))


def exchanges(batches, seqs):
    def pairs(turn):
        out = []
        for b in range(batches):
            for s in range(seqs):
                nb, ns = turn(b, s)
                out.append((b * seqs + s, nb * seqs + ns))
        return out

    halving = [
        pairs(lambda b, s: (b ^ 1, s)),
        pairs(lambda b, s: (b, s ^ 1) if b & 1 else (b ^ 2, s)),
        pairs(lambda b, s: (b ^ 2, s) if b & 1 else (b, s ^ 1)),
        pairs(lambda b, s: (b, s ^ 2)),
    ]
    whole = []
    bit = 4
    while bit < seqs:
        whole.append(pairs(lambda b, s, bit=bit: (b, s ^ bit)))
        bit *= 2
    return halving, whole


def slot_table():
    b, s = lax.axis_index("batch"), lax.axis_index("seq")
    core, here = b & 1, ((b >> 1) & 1) * 2 + (s & 1)
    at = jnp.arange(17, dtype=jnp.int32)
    part, four = (at - 1) >> 2, (at - 1) & 3

    def swapped(v):
        return (v >> 1) | ((v & 1) << 1)

    turned = (core ^ (part & 1)) == 1
    slot = jnp.where(turned, swapped(four ^ here), four ^ here)
    group = jnp.where(turned, swapped(four) ^ here, four ^ here)
    return jnp.where(at == 0, core, jnp.where(part < 2, slot, group))


def tied(token, *arrays):
    return lax.optimization_barrier((token,) + arrays)[1:]


class Summed:
    def __init__(self, keep, send, halving, whole):
        self.keep, self.send, self.halving, self.whole = keep, send, halving, whole
        self.me = jnp.full((1,), lax.axis_index("seq"), jnp.int32)

    def first(self, token):
        (send,) = tied(token, self.send)
        self.came = lax.ppermute(send, AXES, self.halving[0])
        return send

    def halve(self, level, token):
        keep, came = tied(token, self.keep, self.came)
        groups, pieces, rows, _ = keep.shape
        shape = (groups // 2, pieces, rows, 128) if level < 3 else (1, pieces // 2, rows, 128)
        self.send, self.keep = call(
            functools.partial(plain_halve_kernel, level),
            [("v", shape, BF16)] * 2,
            [("s", self.me), ("v", keep), ("v", came)],
        )
        self.came = lax.ppermute(self.send, AXES, self.halving[level])
        return self.send

    def exchange(self, token):
        now = self.sum(self.keep, self.came, token)
        for stage in self.whole[:-1]:
            now = self.sum(now, lax.ppermute(now, AXES, stage), token)
        self.came = lax.ppermute(now, AXES, self.whole[-1])
        self.now = now
        return now

    def turn(self, token):
        self.now = self.sum(self.now, self.came, token)
        self.came = lax.ppermute(self.now, AXES, self.halving[-1])
        return self.now

    def sum(self, left, right, token):
        left, right = tied(token, left, right)
        return call(add_kernel, [("v", left.shape, BF16)], [("v", left), ("v", right)])[0]

    def double(self, level, token):
        now, came = tied(token, self.now, self.came)
        groups, pieces, rows, _ = now.shape
        if level == 2:
            (self.now,) = call(
                pair_kernel,
                [("v", (1, 2 * pieces, rows, 128), BF16)],
                [("s", self.me), ("v", now), ("v", came)],
            )
        else:
            (self.now,) = call(
                stack_kernel,
                [("v", (2, pieces, rows, 128), BF16)],
                [("v", now), ("v", came)],
            )
            self.twin = lax.ppermute(self.now, AXES, self.halving[0])
        self.came = lax.ppermute(self.now, AXES, self.halving[level])
        return self.now

    def last(self, token):
        (self.late,) = tied(token, self.came)
        self.late_twin = lax.ppermute(self.late, AXES, self.halving[0])
        return self.late


class SummedWithStates(Summed):
    def __init__(self, keep, send, halving, whole, adjoint, fades, own_len):
        super().__init__(keep, send, halving, whole)
        self.adjoint, self.fades, self.own_len = adjoint, fades, own_len
        self.core = jnp.full((1,), lax.axis_index("batch") & 1, jnp.int32)
        self.earlier = None

    def halve(self, level, token):
        keep, came = tied(token, self.keep, self.came)
        groups, pieces, rows, _ = keep.shape
        args = [("s", self.me), ("s", self.core)]
        args += [("v", t) for t in (self.fades, self.adjoint, keep, came)]
        if level < 3:
            kept = (groups // 2, pieces, rows, 128)
            extra = []
        else:
            kept = (1, pieces // 2, rows, 128)
            args.append(("v", self.earlier))
            extra = [("v", (H, D), BF16)] * 2
        sent = (kept[0] * kept[1] * rows + STATE, 128)
        self.send, self.keep, *states = call(
            functools.partial(halve_kernel, level, self.own_len),
            [("v", sent, BF16), ("v", kept, BF16)] + extra,
            args,
        )
        if states:
            self.others = [states[0]]
            self.group = states[1]
        self.earlier = came
        self.came = lax.ppermute(self.send, AXES, self.halving[level])
        return self.send

    def exchange(self, token):
        keep, came = tied(token, self.keep, self.came)
        self.others.append(came)
        _, pieces, rows, _ = keep.shape
        self.shape = keep.shape
        (self.now,) = call(
            functools.partial(exchange_kernel, self.own_len),
            [("v", (pieces * rows + STATE, 128), BF16)],
            [("s", self.me)] + [("v", t) for t in (self.fades, self.group, keep, came)],
        )
        self.came = lax.ppermute(self.now, AXES, self.whole[-1])
        return self.now

    def turn(self, token):
        now, came = tied(token, self.now, self.came)
        self.others.append(came)
        (self.now,) = call(
            add_start_kernel, [("v", self.shape, BF16)], [("v", now), ("v", came)]
        )
        self.came = lax.ppermute(self.now, AXES, self.halving[-1])
        return self.now


def shifted_pairs(seqs, by):
    return [(i, i + by) for i in range(seqs) if 0 <= i + by < seqs]


def state_powers(seqs, own_len):
    reach = WINDOW // own_len
    if by_levels(own_len):
        return [float(own_len << i) for i in range(seqs.bit_length() - 1)]
    return [float(own_len * i) for i in range(min(seqs, reach))]


def by_levels(own_len):
    return lax.axis_size("seq") == 8 and 8 <= WINDOW // own_len


def states_before(state, fades, me, own_len, beside):
    if not by_levels(own_len):
        for run in beside:
            run(state)
        return [direct_states(state, fades, own_len, 1)]
    seqs = lax.axis_size("seq")
    group, others = state, []
    levels = seqs.bit_length() - 1
    for i in range(levels):
        others.append(lax.ppermute(group, "seq", [(j, j ^ (1 << i)) for j in range(seqs)]))
        token = beside[i](group)
        if i < levels - 1:
            (other,) = tied(token, others[-1])
            (group,) = call(
                functools.partial(join_kernel, own_len, i),
                [("v", state.shape, BF16)],
                [("s", me), ("v", group), ("v", other), ("v", fades)],
            )
    return others


def direct_states(state, fades, own_len, direction):
    seqs = lax.axis_size("seq")
    total = jnp.zeros(state.shape, F32)
    for k in range(1, min(seqs, WINDOW // own_len)):
        far = lax.ppermute(state, "seq", shifted_pairs(seqs, k * direction))
        total = total + moved(far.astype(F32), fades[k - 1], float((k - 1) * own_len))
    return total


def far_part(signal, log_decay, coeff):
    own_len = signal.shape[0]
    steps = jnp.arange(own_len).astype(F32)[:, None, None]
    held = jnp.exp(log_decay[None] * (WINDOW - 1.0 - steps)) * signal[:, None, :]
    after = lax.cumsum(held, axis=0, reverse=True) - held
    return jnp.sum(coeff[None] * jnp.exp(log_decay[None] * (steps + 1.0)) * after, axis=1)


def start_unpack(who, slots, chunk, results):
    segments, outs, scratch = PLANS[who]
    given = [("s", slots), ("v", chunk.now), ("v", chunk.twin)]
    alias = {}
    if who != "A" and "mix" in results:
        alias = {len(given): outs.index(MIX_OUT)}
        given.append(("o", results["mix"]))
    return call(
        functools.partial(unpack_kernel, segments, len(outs), len(alias), 0),
        outs,
        given,
        scratch(),
        alias=alias,
    )


def own_unpack(slots, chunk, results):
    segments, outs, scratch = PLANS["C"]
    return call(
        unpack_own_kernel,
        outs,
        [("s", slots), ("v", chunk.late), ("o", results["mix"]), ("o", results["C"][1])],
        scratch(),
        alias={2: 0, 3: 1},
    )


def end_unpack(who, slots, chunk, results):
    given = [("s", slots), ("v", chunk.late), ("v", chunk.late_twin)]
    if who == "C":
        return call(
            unpack_rest_kernel,
            PLANS[who][1]
            + [("v", (H, D), F32)] * 4
            + [("v", (1, D), F32)] * 3
            + [("v", (3, Z), F32)],
            given
            + [("v", chunk.now), ("v", chunk.twin)]
            + [("o", results["mix"]), ("o", results["C"][1])],
            rest_buffers()[:-1] + [pltpu.VMEM((512, 128), F32), pltpu.SemaphoreType.DMA((12,))],
            alias={5: 0, 6: 1},
        )
    segments, outs, scratch = PLANS[who]
    before = list(results[who])
    if who != "A":
        before[outs.index(MIX_OUT)] = results["mix"]
    return call(
        functools.partial(unpack_kernel, segments, len(outs), len(outs), 2),
        outs,
        given + [("o", t) for t in before],
        scratch(),
        alias={3 + i: i for i in range(len(outs))},
    )


def wide(*shapes):
    buffers = [pltpu.VMEM((4, rows // 8, cols), F32) for rows, cols in shapes]
    return buffers + [pltpu.SemaphoreType.DMA((4 * len(shapes),))]


def rest_buffers():
    return wide((D, V), (D, Z), (D, V))


MIX_OUT = ("o", (D, MIX), F32)
PLANS = {
    "A": (
        ffn_segments,
        [("o", (FF, D), F32), ("o", (D, FF), F32)],
        lambda: wide((FF, D), (D, FF)),
    ),
    "B": (
        gates_segments,
        [("o", (V, D), F32), MIX_OUT],
        lambda: wide((V, D), (D, D), (D, D)),
    ),
    "C": (rest_segments, [MIX_OUT, ("o", (D, V), F32)], rest_buffers),
}


ORDER = (
    "Ac", "F", "Ah1", "G", "Bc", "T", "Bh1", "E", "Cc", "Ah2", "O", "Bh2", "Ah3", "Ch1", "Bh3",
    "Ax", "L", "Ch2", "At", "Bx", "Ad2", "Ch3", "Bt", "Ad1", "Cx", "Bd2", "Aa", "Ct", "Bd1",
    "Ad0", "K", "Cd2", "Ba", "Bd0", "Cd1", "Au", "Ca", "Bu", "Cd0", "Cb", "Cu",
)


def advance(chunk, who, what, token, slots, results):
    if what == "c":
        return chunk.first(token)
    if what == "x":
        return chunk.exchange(token)
    if what == "t":
        return chunk.turn(token)
    if what[0] == "h":
        return chunk.halve(int(what[1:]), token)
    if what == "d0":
        return chunk.last(token)
    if what[0] == "d":
        return chunk.double(int(what[1:]), token)
    if what == "a":
        chunk.now, chunk.twin = tied(token, chunk.now, chunk.twin)
        results[who] = list(start_unpack(who, slots, chunk, results))
    elif what == "b":
        (chunk.late,) = tied(token, chunk.late)
        results[who] = list(own_unpack(slots, chunk, results))
    else:
        chunk.late, chunk.late_twin = tied(token, chunk.late, chunk.late_twin)
        results[who] = list(end_unpack(who, slots, chunk, results))
    if who != "A":
        results["mix"] = results[who][1 if who == "B" else 0]
    return results[who][0]


def on_device(
    inputs,
    lengths,
    key_mask,
    norm_gain,
    ema_expand,
    ema_alpha,
    ema_delta,
    ema_eta,
    ema_omega,
    w_value,
    w_mix,
    qk_affine,
    w_hidden,
    ffn_gain,
    w_up,
    w_down,
    cotangent,
):
    _, rows, _ = inputs.shape
    seqs = lax.axis_size("seq")
    reach = WINDOW // rows
    halving, whole = exchanges(lax.axis_size("batch"), seqs)
    slots = slot_table()
    limit = lengths - lax.axis_index("seq") * rows
    x = inputs.reshape(rows, D)
    cot = cotangent.reshape(rows, D)
    expand, alpha, delta, eta = ema_expand.T, ema_alpha.T, ema_delta.T, ema_eta.T
    omega = ema_omega.reshape(1, D)
    gain1 = norm_gain.reshape(1, D)
    gain2 = ffn_gain.reshape(1, D)
    powers = state_powers(seqs, rows)
    me = jnp.full((1,), lax.axis_index("seq"), jnp.int32)

    def buffers(tiles):
        return [("v", (4, 4, tiles * 16, 128), BF16)] * 2

    tall = rows * 8 * (D // LANES)
    normed, masked, state, decay, coeff, fades, w_value_near = call(
        functools.partial(norm_kernel, rows, powers),
        [
            ("v", (rows, D), BF16),
            ("v", (rows, D), BF16),
            ("v", (2 * H, D), BF16),
            ("v", (H, D), F32),
            ("v", (H, D), F32),
            ("v", (len(powers), H, D), F32),
            ("v", (D, V), BF16),
        ],
        [("s", limit), ("h", x), ("h", gain1)]
        + [("h", t) for t in (alpha, delta, expand, eta)]
        + [("o", w_value)],
        [pltpu.VMEM((rows, D), F32), pltpu.SemaphoreType.DMA((1,))],
    )
    early = {}

    def own_ema(token):
        (signal,) = tied(token, masked)
        early["local"], early["mix"] = call(
            functools.partial(local_kernel, rows),
            [("v", (rows, D), F32), ("v", (D, MIX), BF16)],
            [("v", signal), ("v", decay), ("v", coeff), ("o", w_mix)],
            [
                pltpu.VMEM((rows, D), F32),
                pltpu.VMEM((tall, LANES), F32),
                pltpu.SemaphoreType.DMA((1,)),
            ],
        )
        return early["local"]

    def own_values(token):
        (rows_in,) = tied(token, normed)
        early["value_pre"], early["value_low"], early["up"], early["down"] = call(
            value_kernel,
            [
                ("v", (rows, V), F32),
                ("v", (rows, V), BF16),
                ("v", (D, FF), BF16),
                ("v", (FF, D), BF16),
            ],
            [("v", rows_in), ("v", w_value_near), ("o", w_up), ("o", w_down)],
            [pltpu.SemaphoreType.DMA((2,))],
        )
        return early["value_low"]

    def own_inner(token):
        (down,) = tied(token, early["down"])
        early["inner"], early["hidden"] = call(
            inner_kernel,
            [("v", (rows, FF), F32), ("v", (V, D), BF16)],
            [("v", down), ("h", cot), ("o", w_hidden)],
            [pltpu.SemaphoreType.DMA((1,))],
        )
        return early["inner"]

    others = states_before(state, fades, me, rows, (own_ema, own_values, own_inner))
    w_mix_near, w_hidden_near = early["mix"], early["hidden"]
    value_pre, value_low = early["value_pre"], early["value_low"]
    far_here = seqs > reach
    far, far_back, far_tables = [], [], []
    if far_here:
        behind = lax.ppermute(masked, "seq", shifted_pairs(seqs, reach)).astype(F32)
        edge, far_pull = jax.vjp(far_part, behind, jnp.log(decay), coeff)
        far = [("h", edge)]
    (
        carry,
        pre,
        mix_low,
        mixed,
        probs,
        attended,
        gated,
        cand_pre,
        resid,
        inner_low,
        g_up_low,
        keep1,
        send1,
    ) = call(
        functools.partial(forward_kernel, rows, len(others), far_here),
        [
            ("v", (2 * H, D), F32),
            ("v", (rows, D), F32),
            ("v", (rows, D), BF16),
            ("v", (rows, MIX), F32),
            ("v", (rows, BLOCK), F32),
            ("v", (rows, V), F32),
            ("v", (rows, V), BF16),
            ("v", (rows, D), F32),
            ("v", (rows, D), F32),
            ("v", (rows, FF), BF16),
            ("v", (rows, FF), BF16),
        ]
        + buffers(16),
        [("s", limit), ("s", me), ("s", slots)]
        + [("v", t) for t in (fades, masked, value_low, decay, coeff)]
        + [("v", t) for t in (w_mix_near, w_hidden_near, early["up"])]
        + [("v", t) for t in (early["local"], early["inner"], *others)]
        + far
        + [("h", t) for t in (omega, qk_affine, key_mask, x, gain2, cot)],
        [
            pltpu.VMEM((tall, LANES), F32),
            pltpu.VMEM((rows, FF), F32),
            pltpu.VMEM((rows, D), BF16),
        ],
    )
    token = resid
    chunks = {"A": Summed(keep1, send1, halving, whole)}
    results = {}
    for step in ORDER:
        who, what = step[0], step[1:]
        if step == "F":
            (g_up_low,) = tied(token, g_up_low)
            keep2, send2, g_resid, g_ffn_gain, g_hid = call(
                resid_kernel,
                buffers(16)
                + [("v", (rows, D), F32), ("v", (1, D), F32), ("v", (rows, D), BF16)],
                [("s", slots), ("h", cot), ("h", gain2)]
                + [("v", t) for t in (resid, g_up_low, early["up"], mixed, cand_pre, gated)],
            )
            token = g_resid
        elif step == "O":
            (inner_low,) = tied(token, inner_low)
            (out,) = call(
                output_kernel,
                [("v", (rows, D), BF16)],
                [("v", resid), ("v", inner_low), ("h", w_down)],
            )
            token = out
        elif step == "G":
            (g_resid,) = tied(token, g_resid)
            keep2, send2, g_skip, g_upd, g_reset, g_att = call(
                gates_kernel,
                buffers(16)
                + [
                    ("v", (rows, D), F32),
                    ("v", (rows, D), BF16),
                    ("v", (rows, V), BF16),
                    ("v", (rows, V), BF16),
                ],
                [("s", slots), ("v", keep2), ("v", send2), ("h", x), ("v", w_hidden_near)]
                + [("v", t) for t in (mix_low, mixed, attended, cand_pre, g_resid, g_hid)],
                alias={1: 0, 2: 1},
            )
            chunks["B"] = Summed(keep2, send2, halving, whole)
            token = g_skip
        elif step == "T":
            (g_att,) = tied(token, g_att)
            keep3, send3, g_qk, g_shared, g_normed = call(
                functools.partial(attention_kernel, rows),
                buffers(18) + [("v", (3, Z), F32), ("v", (rows, Z), BF16), ("v", (rows, D), F32)],
                [("s", slots)]
                + [
                    ("v", t)
                    for t in (
                        normed,
                        value_pre,
                        value_low,
                        mix_low,
                        mixed,
                        probs,
                        g_att,
                        g_reset,
                        w_value_near,
                    )
                ]
                + [("h", qk_affine)],
            )
            token = g_normed
        elif step == "E":
            (g_upd,) = tied(token, g_upd)
            if far_here:
                g_mixed = jnp.concatenate([g_upd, g_shared, g_reset, g_hid], axis=1)
                g_early = lax.dot_general(
                    g_mixed, w_mix, (((1,), (1,)), ((), ())), preferred_element_type=F32
                )
                sig = jax.nn.sigmoid(pre)
                g_behind, far_log, far_coeff = far_pull(g_early * (sig * (1.0 + pre * (1.0 - sig))))
                far_tables = [("h", jnp.concatenate([far_coeff, far_log], axis=0))]
                g_far = lax.ppermute(g_behind.astype(BF16), "seq", shifted_pairs(seqs, -reach))
                far_back = [("h", g_far.astype(F32))]
            keep3, send3, g_pre, adjoint = call(
                functools.partial(tables_kernel, rows, far_here),
                buffers(18) + [("v", (rows, D), F32), ("v", (H, D), BF16)],
                [("s", slots)]
                + [
                    ("v", t)
                    for t in (
                        keep3,
                        send3,
                        masked,
                        normed,
                        pre,
                        g_upd,
                        g_shared,
                        g_reset,
                        g_hid,
                        g_normed,
                        g_qk,
                        g_ffn_gain,
                        carry,
                        decay,
                        coeff,
                        w_mix_near,
                    )
                ]
                + far_tables
                + [("h", t) for t in (expand, alpha, delta, eta, gain1)],
                [pltpu.VMEM((rows, D), F32), pltpu.VMEM((512, 128), F32)],
                alias={1: 0, 2: 1},
            )
            if by_levels(rows):
                chunks["C"] = SummedWithStates(
                    keep3, send3, halving, whole, adjoint, fades, rows
                )
            else:
                chunks["C"] = Summed(keep3, send3, halving, whole)
                chunks["C"].others = [direct_states(adjoint, fades, rows, -1)]
            token = g_pre
        elif step == "L":
            (g_pre,) = tied(token, g_pre)
            (g_local,) = call(
                functools.partial(local_back_kernel, rows),
                [("v", (rows, D), F32)],
                [("v", t) for t in (g_pre, decay, coeff)],
                [pltpu.VMEM((tall, LANES), F32)],
            )
            token = g_local
        elif step == "K":
            others = chunks["C"].others
            (g_pre,) = tied(token, g_pre)
            (d_input,) = call(
                functools.partial(input_kernel, rows, len(others), far_here),
                [("v", (rows, D), BF16)],
                [("s", limit), ("s", me)]
                + [("v", t) for t in (fades, g_pre, g_local, g_skip, g_normed, decay, coeff)]
                + [("v", t) for t in others]
                + far_back
                + [("h", t) for t in (x, omega, gain1)],
                [pltpu.VMEM((tall, LANES), F32), pltpu.VMEM((rows, D), F32)],
            )
            token = d_input
        else:
            token = advance(chunks[who], who, what, token, slots, results)
    grad_down, grad_up = results["A"]
    grad_hidden, _ = results["B"]
    grad_mix = results["mix"]
    (
        _,
        grad_value,
        g_expand,
        g_alpha,
        g_delta,
        g_eta,
        g_norm_gain,
        g_omega,
        g_ffn_gain,
        g_qk,
    ) = results["C"]
    return (
        out.reshape(inputs.shape),
        d_input.reshape(inputs.shape),
        g_norm_gain.reshape(D),
        g_expand.T,
        g_alpha.T,
        g_delta.T,
        g_eta.T,
        g_omega.reshape(D),
        grad_value,
        grad_mix,
        g_qk,
        grad_hidden,
        g_ffn_gain.reshape(D),
        grad_up,
        grad_down,
    )


def solution(mesh):
    row = P("batch", "seq", None)
    return jax.shard_map(
        on_device,
        mesh=mesh,
        in_specs=(row, P("batch"), P("batch", "seq")) + (P(),) * 13 + (row,),
        out_specs=(row, row) + (P(),) * 13,
        check_vma=False,
    )
```

```python
import functools

import jax
import jax.numpy as jnp
from jax import lax
from jax.experimental import pallas as pl
from jax.experimental.pallas import tpu as pltpu
from jax.sharding import PartitionSpec as P

D = 512
Z = 128
V = 1024
H = 16
FF = 1024
BLOCK = 128
WINDOW = 4096
MIX = 2 * D + Z + V
AXES = ("batch", "seq")
F32 = jnp.float32
BF16 = jnp.bfloat16
COSTS = {
    "norm_kernel": 10**9,
    "join_kernel": 10**9,
    "local_kernel": 10**9,
    "value_kernel": 10**9,
    "inner_kernel": 10**9,
    "forward_kernel": 10**9,
    "resid_kernel": 10**9,
    "gates_kernel": 10**9,
    "output_kernel": 10**9,
    "attention_kernel": 12 * 10**9,
    "tables_kernel": 10**9,
    "local_back_kernel": 10**9,
    "input_kernel": 10**9,
}
VMEM_LIMIT = 24 * 2**20


def sigmoid(v):
    return 1.0 / (1.0 + jnp.exp(-v))


def dot(a, b):
    return lax.dot_general(a, b, (((1,), (0,)), ((), ())), preferred_element_type=F32)


def dot_nt(a, b):
    return lax.dot_general(a, b, (((1,), (1,)), ((), ())), preferred_element_type=F32)


def dot_tn(a, b):
    return lax.dot_general(a, b, (((0,), (0,)), ((), ())), preferred_element_type=F32)


class Late:
    def __init__(self, copy, ref):
        self.copy, self.ref, self.waited = copy, ref, False

    def __call__(self):
        if not self.waited:
            self.copy.wait()
            self.waited = True
        return self.ref


SPACES = {"s": pltpu.SMEM, "v": pltpu.VMEM, "h": pltpu.HBM, "o": pltpu.HBM}


def call(body, outs, args, scratch=(), alias=None):
    late = [i for i, (kind, _) in enumerate(args) if kind == "h"]
    n_in, n_out = len(args), len(outs)

    def run(*refs):
        ins = list(refs[:n_in])
        mine = refs[n_in : n_in + n_out + len(scratch)]
        if late:
            rest = refs[n_in + n_out + len(scratch) :]
            for k, i in enumerate(late):
                copy = pltpu.make_async_copy(ins[i], rest[k], rest[-1].at[k])
                copy.start()
                ins[i] = Late(copy, rest[k])
        body(*ins, *mine)
        for i in late:
            ins[i]()

    name = getattr(body, "func", body).__name__
    buffers = [pltpu.VMEM(args[i][1].shape, args[i][1].dtype) for i in late]
    if late:
        buffers.append(pltpu.SemaphoreType.DMA((len(late),)))
    return pl.pallas_call(
        run,
        out_shape=[jax.ShapeDtypeStruct(shape, dtype) for _, shape, dtype in outs],
        in_specs=[pl.BlockSpec(memory_space=SPACES[kind]) for kind, _ in args],
        out_specs=[pl.BlockSpec(memory_space=SPACES[kind]) for kind, _, _ in outs],
        scratch_shapes=list(scratch) + buffers,
        input_output_aliases=alias or {},
        compiler_params=pltpu.CompilerParams(vmem_limit_bytes=VMEM_LIMIT),
        name=name,
        cost_estimate=pl.CostEstimate(
            flops=COSTS.get(name, 10**10), bytes_accessed=0, transcendentals=0
        ),
    )(
        *[
            pltpu.with_memory_space_constraint(array, pltpu.HBM) if kind in "ho" else array
            for kind, array in args
        ]
    )


def row8(ref, t):
    return jnp.broadcast_to(ref[pl.ds(t, 1), :], (8, D))


LANES = 128


def put8(part_ref, t, rows, eight):
    for j in range(D // LANES):
        base = pl.multiple_of(j * rows * 8 + t * 8, 8)
        part_ref[pl.ds(base, 8), :] = eight[:, j * LANES : (j + 1) * LANES]


def fold8(part_ref, out_ref, rows):
    def one(g, _):
        at = pl.multiple_of(g * 8, 8)
        for j in range(D // LANES):
            base = pl.multiple_of(j * rows * 8 + g * 64, 64)
            acc = part_ref[pl.ds(base, 8, stride=8), :]
            for k in range(1, 8):
                acc = acc + part_ref[pl.ds(base + k, 8, stride=8), :]
            out_ref[pl.ds(at, 8), j * LANES : (j + 1) * LANES] = acc
        return 0

    lax.fori_loop(0, rows // 8, one, 0)


def norm_kernel(
    rows,
    powers,
    lim_ref,
    x,
    gain,
    alpha,
    delta,
    expand,
    eta,
    normed_ref,
    masked_ref,
    state_ref,
    a_ref,
    c_ref,
    fade_ref,
    m_ref,
):
    x = x()[...].astype(F32)
    center = jnp.mean(x, axis=1, keepdims=True)
    shifted = x - center
    spread = jnp.mean(shifted * shifted, axis=1, keepdims=True)
    normed = (shifted * lax.rsqrt(spread + 1e-05) * gain()[...]).astype(BF16)
    normed_ref[...] = normed
    place = lax.broadcasted_iota(jnp.int32, (rows, 1), 0)
    masked = jnp.where(place < lim_ref[0], normed.astype(F32), 0.0)
    masked_ref[...] = masked.astype(BF16)
    m_ref[...] = masked
    alpha = sigmoid(alpha()[...])
    decay = 1.0 - alpha * sigmoid(delta()[...])
    a_ref[...] = decay
    c_ref[...] = eta()[...] * alpha * expand()[...]
    log_decay = jnp.log(decay)
    for i, power in enumerate(powers):
        fade_ref[i] = jnp.exp(log_decay * power)
    a = (decay[0:8, :], decay[8:16, :])

    def step(g, carry):
        s, q = carry
        for k in range(8):
            row = row8(m_ref, g * 8 + k)
            grown = tuple(a[i] * s[i] for i in range(2))
            q = tuple(a[i] * q[i] + grown[i] for i in range(2))
            s = tuple(grown[i] + row for i in range(2))
        return s, q

    zero = jnp.zeros((8, D), F32)
    s, q = lax.fori_loop(0, rows // 8, step, ((zero, zero), (zero, zero)))
    state_ref[0:8, :] = s[0].astype(BF16)
    state_ref[8:16, :] = s[1].astype(BF16)
    state_ref[16:24, :] = q[0].astype(BF16)
    state_ref[24:32, :] = q[1].astype(BF16)


def bring(pairs, sem):
    copies = []
    for i, (src, dst) in enumerate(pairs):
        copy = pltpu.make_async_copy(src, dst, sem.at[i])
        copy.start()
        copies.append(copy)
    return copies


def local_kernel(
    rows,
    masked_ref,
    a_ref,
    c_ref,
    wvalue_ref,
    wmix_ref,
    out_ref,
    wvalue_out_ref,
    wmix_out_ref,
    m_ref,
    part_ref,
    sem,
):
    copies = bring(((wvalue_ref, wvalue_out_ref), (wmix_ref, wmix_out_ref)), sem)
    m_ref[...] = masked_ref[...].astype(F32)
    a = (a_ref[0:8, :], a_ref[8:16, :])
    c = (c_ref[0:8, :], c_ref[8:16, :])

    def step(g, s):
        for k in range(8):
            t = g * 8 + k
            row = row8(m_ref, t)
            s = tuple(a[i] * s[i] + row for i in range(2))
            put8(part_ref, t, rows, c[0] * s[0] + c[1] * s[1])
        return s

    zero = jnp.zeros((8, D), F32)
    lax.fori_loop(0, rows // 8, step, (zero, zero))
    fold8(part_ref, out_ref, rows)
    for copy in copies:
        copy.wait()


def value_kernel(
    normed_ref, wvalue_ref, wup_ref, wdown_ref, pre_ref, low_ref, wup_out_ref, wdown_out_ref, sem
):
    copies = bring(((wup_ref, wup_out_ref), (wdown_ref, wdown_out_ref)), sem)
    for lo in range(0, V, D):
        pre = dot(normed_ref[...], wvalue_ref[:, lo : lo + D])
        pre_ref[:, lo : lo + D] = pre
        low_ref[:, lo : lo + D] = (pre * sigmoid(pre)).astype(BF16)
    for copy in copies:
        copy.wait()


def inner_kernel(wdown_ref, cot, whid_ref, out_ref, whid_out_ref, sem):
    copies = bring(((whid_ref, whid_out_ref),), sem)
    out_ref[...] = dot_nt(cot()[...], wdown_ref[...])
    for copy in copies:
        copy.wait()


def moved(state, fade, steps):
    if state.shape[0] == H:
        return fade * state
    return jnp.concatenate([fade * state[:H], fade * (state[H:] + steps * state[:H])], axis=0)


def joined(own_len, level, direction, me, group, other, fades):
    late = ((me >> level) & 1) == (1 if direction == 1 else 0)
    first, second = jnp.where(late, other, group), jnp.where(late, group, other)
    return (moved(first, fades[level], float(own_len << level)) + second).astype(BF16)


def join_kernel(own_len, level, me_ref, group_ref, other_ref, fade_ref, out_ref):
    group, other = group_ref[...].astype(F32), other_ref[...].astype(F32)
    out_ref[...] = joined(own_len, level, 1, me_ref[0], group, other, fade_ref)


def carried(own_len, direction, me, others, fades):
    total = None
    for i, other in enumerate(others):
        blocks = me if direction == 1 else ~me
        late = ((me >> i) & 1) == (1 if direction == 1 else 0)
        for j in range(i):
            on = ((blocks >> j) & 1) == 1
            other = jnp.where(on, moved(other, fades[j], float(own_len << j)), other)
        other = jnp.where(late, other, 0.0)
        total = other if total is None else total + other
    return total


def place(slots_ref, dst, side, at, grad):
    rows, cols = grad.shape
    piece = rows // 16
    for g in range(4):
        slot = slots_ref[1 + 4 * side + g]
        for z in range(4):
            tile = at
            for lo in range((g * 4 + z) * piece, (g * 4 + z + 1) * piece, 16):
                for c in range(0, cols, 128):
                    dst[slot, z, tile * 16 : tile * 16 + 16, :] = grad[lo : lo + 16, c : c + 128]
                    tile += 1


def outer(slots_ref, keep_ref, send_ref, at, left_ref, right):
    half = left_ref.shape[1] // 2
    for side, dst in enumerate((keep_ref, send_ref)):
        core = slots_ref[0] ^ side
        left = left_ref[:, pl.ds(pl.multiple_of(core * half, half), half)]
        place(slots_ref, dst, side, at, dot_tn(left, right).astype(BF16))


def forward_kernel(
    rows,
    n_others,
    has_far,
    lim_ref,
    me_ref,
    slots_ref,
    fade_ref,
    masked_ref,
    value_ref,
    a_ref,
    c_ref,
    wmix_ref,
    whid_ref,
    wup_ref,
    local_ref,
    ginner_ref,
    *refs,
):
    others, refs = refs[:n_others], refs[n_others:]
    far, refs = (refs[0], refs[1:]) if has_far else (None, refs)
    (
        omega,
        qk,
        mask,
        x,
        gain,
        cot,
        carry_ref,
        pre_ref,
        mixlow_ref,
        mixed_ref,
        probs_ref,
        att_ref,
        gated_ref,
        candpre_ref,
        resid_ref,
        inner_ref,
        guplow_ref,
        keep_ref,
        send_ref,
        part_ref,
        up_ref,
        ffn_ref,
    ) = refs
    masked = masked_ref[...].astype(F32)
    if n_others == 1:
        carry_ref[...] = others[0][...].astype(F32)
    else:
        states = [ref[...].astype(F32) for ref in others]
        carry_ref[...] = carried(rows, 1, me_ref[0], states, fade_ref)
    a = (a_ref[0:8, :], a_ref[8:16, :])

    def step(g, s):
        for k in range(8):
            s = tuple(a[i] * s[i] for i in range(2))
            put8(part_ref, g * 8 + k, rows, s[0] + s[1])
        return s

    start = tuple(c_ref[i : i + 8, :] * carry_ref[i : i + 8, :] for i in (0, 8))
    lax.fori_loop(0, rows // 8, step, start)
    fold8(part_ref, pre_ref, rows)
    pre = pre_ref[...] + local_ref[...] + omega()[...] * masked
    if has_far:
        pre = pre + far()[...]
    pre_ref[...] = pre
    mix_low = (pre * sigmoid(pre)).astype(BF16)
    mixlow_ref[...] = mix_low
    shared_pre = dot(mix_low, wmix_ref[:, D : D + Z])
    mixed_ref[:, D : D + Z] = shared_pre
    shared = shared_pre * sigmoid(shared_pre)
    qk_ref, mask_ref = qk(), mask()
    query = (shared * qk_ref[0:1, :] + qk_ref[1:2, :]).astype(BF16)
    key = (shared * qk_ref[2:3, :]).astype(BF16)
    places = lax.broadcasted_iota(jnp.int32, (BLOCK, BLOCK), 0)
    others = lax.broadcasted_iota(jnp.int32, (BLOCK, BLOCK), 1)
    for g in range(rows // BLOCK):
        lo = g * BLOCK
        ok = (mask_ref[:, lo : lo + BLOCK] > 0) & (
            lax.broadcasted_iota(jnp.int32, (1, BLOCK), 1) + lo < lim_ref[0]
        )
        ok = jnp.broadcast_to(ok.astype(F32), (BLOCK, BLOCK)) > 0.5
        allowed = (places == others) | ((places > others) & ok)
        scores = dot_nt(query[lo : lo + BLOCK], key[lo : lo + BLOCK]) * (Z**-0.5)
        scores = jnp.where(allowed, scores, -1000000000.0)
        grown = jnp.exp(scores - jnp.max(scores, axis=1, keepdims=True))
        probs = grown / jnp.sum(grown, axis=1, keepdims=True)
        probs_ref[lo : lo + BLOCK, :] = probs
        att_ref[lo : lo + BLOCK, :] = dot(probs.astype(BF16), value_ref[lo : lo + BLOCK, :])
    for lo in range(0, V, 512):
        reset_pre = dot(mix_low, wmix_ref[:, D + Z + lo : D + Z + lo + 512])
        mixed_ref[:, D + Z + lo : D + Z + lo + 512] = reset_pre
        gate = reset_pre * sigmoid(reset_pre)
        gated_ref[:, lo : lo + 512] = (att_ref[:, lo : lo + 512] * gate).astype(BF16)
    gated = gated_ref[...]
    hidden_in = dot(mix_low, wmix_ref[:, D + Z + V :])
    mixed_ref[:, D + Z + V :] = hidden_in
    update_pre = dot(mix_low, wmix_ref[:, :D])
    mixed_ref[:, :D] = update_pre
    cand_pre = hidden_in + dot(gated, whid_ref[...])
    candpre_ref[...] = cand_pre
    cand = cand_pre * sigmoid(cand_pre)
    x = x()[...].astype(F32)
    resid = x + sigmoid(update_pre) * (cand - x)
    resid_ref[...] = resid
    unit, _ = unit_rows(resid)
    ffn_low = (unit * gain()[...]).astype(BF16)
    ffn_ref[...] = ffn_low
    up_ref[...] = dot(ffn_low, wup_ref[...])
    up = up_ref[...]
    sig = sigmoid(up)
    inner = (up * sig).astype(BF16)
    inner_ref[...] = inner
    outer(slots_ref, keep_ref, send_ref, 0, inner_ref, cot()[...])
    gup_low = (ginner_ref[...] * (sig * (1.0 + up * (1.0 - sig)))).astype(BF16)
    guplow_ref[...] = gup_low
    outer(slots_ref, keep_ref, send_ref, 8, ffn_ref, gup_low)


def unit_rows(rows):
    shifted = rows - jnp.mean(rows, axis=1, keepdims=True)
    inv = lax.rsqrt(jnp.mean(shifted * shifted, axis=1, keepdims=True) + 1e-05)
    return shifted * inv, inv


def norm_back(unit, inv, e):
    return inv * (
        e
        - jnp.mean(e, axis=1, keepdims=True)
        - unit * jnp.mean(e * unit, axis=1, keepdims=True)
    )


def output_kernel(resid_ref, inner_ref, wdown, out_ref):
    out_ref[...] = (resid_ref[...] + dot(inner_ref[...], wdown()[...])).astype(BF16)


def slope(v, sig):
    return sig * (1.0 + v * (1.0 - sig))


def resid_kernel(
    slots_ref,
    cot,
    gain,
    resid_ref,
    guplow_ref,
    wup_ref,
    mixed_ref,
    candpre_ref,
    gated_ref,
    keep_ref,
    send_ref,
    gres_ref,
    ggain_ref,
    ghid_ref,
):
    g_ffn = dot_nt(guplow_ref[...], wup_ref[...])
    unit, inv = unit_rows(resid_ref[...])
    ggain_ref[...] = jnp.sum(g_ffn * unit, axis=0, keepdims=True)
    g_resid = cot()[...].astype(F32) + norm_back(unit, inv, g_ffn * gain()[...])
    gres_ref[...] = g_resid
    cand_pre = candpre_ref[...]
    g_cand = g_resid * sigmoid(mixed_ref[:, :D]) * slope(cand_pre, sigmoid(cand_pre))
    g_hid = g_cand.astype(BF16)
    ghid_ref[...] = g_hid
    outer(slots_ref, keep_ref, send_ref, 0, gated_ref, g_hid)


def gates_kernel(
    slots_ref,
    keep_in_ref,
    send_in_ref,
    x,
    whid_ref,
    mixlow_ref,
    mixed_ref,
    att_ref,
    candpre_ref,
    gres_ref,
    ghid_ref,
    keep_ref,
    send_ref,
    gskip_ref,
    gupd_ref,
    greset_ref,
    gatt_ref,
):
    g_hid = ghid_ref[...]
    g_gated = dot_nt(g_hid, whid_ref[...])
    outer(slots_ref, keep_ref, send_ref, 12, mixlow_ref, g_hid)
    g_resid = gres_ref[...]
    update = sigmoid(mixed_ref[:, :D])
    cand_pre = candpre_ref[...]
    g_update = g_resid * update
    gskip_ref[...] = g_resid - g_update
    cand = cand_pre * sigmoid(cand_pre)
    g_upd = (g_update * (1.0 - update) * (cand - x()[...].astype(F32))).astype(BF16)
    gupd_ref[...] = g_upd
    outer(slots_ref, keep_ref, send_ref, 8, mixlow_ref, g_upd)
    reset_pre = mixed_ref[:, D + Z : D + Z + V]
    sig = sigmoid(reset_pre)
    gatt_ref[...] = (g_gated * (reset_pre * sig)).astype(BF16)
    greset_ref[...] = (g_gated * att_ref[...] * slope(reset_pre, sig)).astype(BF16)


def attention_kernel(
    rows,
    slots_ref,
    normed_ref,
    valuepre_ref,
    value_ref,
    mixlow_ref,
    mixed_ref,
    probs_ref,
    gatt_ref,
    greset_ref,
    wvalue_ref,
    qk,
    keep_ref,
    send_ref,
    gqk_ref,
    gshared_ref,
    gnorm_ref,
):
    qk_ref = qk()
    shared_pre = mixed_ref[:, D : D + Z]
    ssig = sigmoid(shared_pre)
    shared = shared_pre * ssig
    query = (shared * qk_ref[0:1, :] + qk_ref[1:2, :]).astype(BF16)
    key = (shared * qk_ref[2:3, :]).astype(BF16)
    g_query, g_key, g_value = [], [], []
    for g in range(rows // BLOCK):
        part = slice(g * BLOCK, (g + 1) * BLOCK)
        probs = probs_ref[part, :]
        g_probs = dot_nt(gatt_ref[part, :], value_ref[part, :])
        g_value.append(dot_tn(probs.astype(BF16), gatt_ref[part, :]))
        inner = jnp.sum(g_probs * probs, axis=1, keepdims=True)
        g_scores = (probs * (g_probs - inner) * (Z**-0.5)).astype(BF16)
        g_query.append(dot(g_scores, key[part]))
        g_key.append(dot_tn(g_scores, query[part]))
    g_query = jnp.concatenate(g_query, axis=0)
    g_key = jnp.concatenate(g_key, axis=0)
    g_value = jnp.concatenate(g_value, axis=0)
    gqk_ref[0:1, :] = jnp.sum(g_query * shared, axis=0, keepdims=True)
    gqk_ref[1:2, :] = jnp.sum(g_query, axis=0, keepdims=True)
    gqk_ref[2:3, :] = jnp.sum(g_key * shared, axis=0, keepdims=True)
    g_shared = g_query * qk_ref[0:1, :] + g_key * qk_ref[2:3, :]
    g_shared = (g_shared * slope(shared_pre, ssig)).astype(BF16)
    gshared_ref[...] = g_shared
    outer(slots_ref, keep_ref, send_ref, 8, mixlow_ref, g_shared)
    value_pre = valuepre_ref[...]
    vsig = sigmoid(value_pre)
    g_vpre = (g_value * slope(value_pre, vsig)).astype(BF16)
    outer(slots_ref, keep_ref, send_ref, 0, normed_ref, g_vpre)
    outer(slots_ref, keep_ref, send_ref, 9, mixlow_ref, greset_ref[...])
    gnorm_ref[...] = dot_nt(g_vpre, wvalue_ref[...])


SMALL = 4 * H + 4


def tables_kernel(
    rows,
    has_far,
    slots_ref,
    keep_in_ref,
    send_in_ref,
    masked_ref,
    normed_ref,
    pre_ref,
    gupd_ref,
    gshared_ref,
    greset_ref,
    ghid_ref,
    gnorm_ref,
    gqk_ref,
    gffn_ref,
    carry_ref,
    a_ref,
    c_ref,
    wmix_ref,
    *refs,
):
    far, refs = (refs[0], refs[1:]) if has_far else (None, refs)
    expand, alpha, delta, eta, gain, *refs = refs
    keep_ref, send_ref, gpre_ref, adj_ref, m_ref, small_ref = refs
    m_ref[...] = masked_ref[...].astype(F32)
    pre = pre_ref[...]
    psig = sigmoid(pre)
    g_mix_low = dot_nt(gupd_ref[...], wmix_ref[:, :D])
    g_mix_low += dot_nt(gshared_ref[...], wmix_ref[:, D : D + Z])
    g_mix_low += dot_nt(greset_ref[...], wmix_ref[:, D + Z : D + Z + V])
    g_mix_low += dot_nt(ghid_ref[...], wmix_ref[:, D + Z + V :])
    g_pre = g_mix_low * slope(pre, psig)
    gpre_ref[...] = g_pre
    a = (a_ref[0:8, :], a_ref[8:16, :])

    def step(g, carry):
        s, q, dc, dq, m = carry
        for k in range(8):
            t = g * 8 + k
            row = row8(m_ref, t)
            grad = row8(gpre_ref, t)
            late = row8(gpre_ref, rows - 1 - t)
            grown = tuple(a[i] * s[i] for i in range(2))
            q = tuple(a[i] * q[i] + grown[i] for i in range(2))
            s = tuple(grown[i] + row for i in range(2))
            dc = tuple(dc[i] + grad * s[i] for i in range(2))
            dq = tuple(dq[i] + grad * q[i] for i in range(2))
            m = tuple(a[i] * (m[i] + late) for i in range(2))
        return s, q, dc, dq, m

    zero = jnp.zeros((8, D), F32)
    _, _, dc, dq, m = lax.fori_loop(
        0,
        rows // 8,
        step,
        (
            (carry_ref[0:8, :], carry_ref[8:16, :]),
            (carry_ref[16:24, :], carry_ref[24:32, :]),
            (zero, zero),
            (zero, zero),
            (zero, zero),
        ),
    )
    adj_ref[0:8, :] = m[0].astype(BF16)
    adj_ref[8:16, :] = m[1].astype(BF16)
    g_coeff = jnp.concatenate(dc, axis=0)
    g_log = c_ref[...] * jnp.concatenate(dq, axis=0)
    if has_far:
        far_ref = far()
        g_coeff, g_log = g_coeff + far_ref[0:H, :], g_log + far_ref[H:, :]
    expand, eta = expand()[...], eta()[...]
    alpha, delta = sigmoid(alpha()[...]), sigmoid(delta()[...])
    g_log = g_log / a_ref[...]
    g_expand = g_coeff * (eta * alpha)
    g_eta = g_coeff * (alpha * expand)
    g_alpha = (g_coeff * (eta * expand) - g_log * delta) * (alpha * (1.0 - alpha))
    g_delta = -(g_log * alpha) * (delta * (1.0 - delta))
    small_ref[...] = jnp.zeros_like(small_ref)
    for i, part in enumerate((g_expand, g_alpha, g_delta, g_eta)):
        for j in range(D // LANES):
            at = (i * 4 + j) * H
            small_ref[at : at + H, :] = part[:, j * LANES : (j + 1) * LANES]
    g_gain = jnp.sum(
        g_pre * pre + normed_ref[...].astype(F32) * gnorm_ref[...], axis=0, keepdims=True
    ) / gain()[...]
    g_omega = jnp.sum(g_pre * m_ref[...], axis=0, keepdims=True)
    for i, part in enumerate((g_gain, g_omega, gffn_ref[...])):
        for j in range(D // LANES):
            at = 16 * H + j * H + i
            small_ref[at : at + 1, :] = part[:, j * LANES : (j + 1) * LANES]
    for j in range(3):
        at = 16 * H + j * H + 3
        small_ref[at : at + 1, :] = gqk_ref[j : j + 1, :]
    for side, dst in enumerate((keep_ref, send_ref)):
        row = pl.multiple_of((slots_ref[0] ^ side) * 256, 256)
        place(slots_ref, dst, side, 17, small_ref[pl.ds(row, 256), :].astype(BF16))


def local_back_kernel(rows, gpre_ref, a_ref, c_ref, gx_ref, part_ref):
    a = (a_ref[0:8, :], a_ref[8:16, :])
    c = (c_ref[0:8, :], c_ref[8:16, :])

    def back(g, m):
        for k in range(8):
            t = rows - 1 - (g * 8 + k)
            row = row8(gpre_ref, t)
            lam = tuple(m[i] + row for i in range(2))
            put8(part_ref, t, rows, c[0] * lam[0] + c[1] * lam[1])
            m = tuple(a[i] * lam[i] for i in range(2))
        return m

    zero = jnp.zeros((8, D), F32)
    lax.fori_loop(0, rows // 8, back, (zero, zero))
    fold8(part_ref, gx_ref, rows)


def input_kernel(
    rows,
    n_others,
    has_far,
    lim_ref,
    me_ref,
    fade_ref,
    gpre_ref,
    glocal_ref,
    gskip_ref,
    gnorm_ref,
    a_ref,
    c_ref,
    *refs,
):
    others, refs = refs[:n_others], refs[n_others:]
    far, refs = (refs[0], refs[1:]) if has_far else (None, refs)
    x, omega, gain, din_ref, part_ref, gx_ref = refs
    if n_others == 1:
        adjoint = others[0][...].astype(F32)
    else:
        adjoint = carried(rows, -1, me_ref[0], [state_in(ref) for ref in others], fade_ref)
    a = (a_ref[0:8, :], a_ref[8:16, :])

    def back(g, m):
        for k in range(8):
            put8(part_ref, rows - 1 - (g * 8 + k), rows, m[0] + m[1])
            m = tuple(a[i] * m[i] for i in range(2))
        return m

    start = tuple(c_ref[i : i + 8, :] * adjoint[i : i + 8, :] for i in (0, 8))
    lax.fori_loop(0, rows // 8, back, start)
    fold8(part_ref, gx_ref, rows)
    g_masked = gx_ref[...] + glocal_ref[...] + omega()[...] * gpre_ref[...]
    if has_far:
        g_masked = g_masked + far()[...]
    place = lax.broadcasted_iota(jnp.int32, (rows, 1), 0)
    e = jnp.where(place < lim_ref[0], g_masked, 0.0) + gnorm_ref[...]
    x = x()[...].astype(F32)
    shifted = x - jnp.mean(x, axis=1, keepdims=True)
    inv = lax.rsqrt(jnp.mean(shifted * shifted, axis=1, keepdims=True) + 1e-05)
    unit = shifted * inv
    e = e * gain()[...]
    g_in = inv * (
        e
        - jnp.mean(e, axis=1, keepdims=True)
        - unit * jnp.mean(e * unit, axis=1, keepdims=True)
    )
    din_ref[...] = (g_in + gskip_ref[...]).astype(BF16)


def unpack(slots_ref, sources, first, segments, sem):
    copies = []
    for at, rows, cols, buffer_ref, out_ref, col in segments:
        group, piece = rows // 8, rows // 32
        for side, src in sources:
            for slot in range(2):
                block = len(copies) % 4
                for z in range(4):
                    tile = at
                    for lo in range(z * piece, (z + 1) * piece, 16):
                        for c in range(0, cols, 128):
                            buffer_ref[block, lo : lo + 16, c : c + 128] = src[
                                slot, z, tile * 16 : tile * 16 + 16, :
                            ].astype(F32)
                            tile += 1
                place_of = slots_ref[9 + 4 * side + first + slot]
                row = pl.multiple_of(
                    (slots_ref[0] ^ side) * (rows // 2) + place_of * group, group
                )
                copy = pltpu.make_async_copy(
                    buffer_ref.at[block],
                    out_ref.at[pl.ds(row, group), pl.ds(col, cols)],
                    sem.at[len(copies)],
                )
                copy.start()
                copies.append(copy)
    return copies


def ffn_segments(down_buf, up_buf, down_ref, up_ref):
    return [(0, FF, D, down_buf, down_ref, 0), (8, D, FF, up_buf, up_ref, 0)]


def gates_segments(hid_buf, upd_buf, in_buf, hid_ref, mix_ref):
    return [
        (0, V, D, hid_buf, hid_ref, 0),
        (8, D, D, upd_buf, mix_ref, 0),
        (12, D, D, in_buf, mix_ref, D + Z + V),
    ]


def rest_segments(value_buf, shared_buf, reset_buf, mix_ref, value_ref):
    return [
        (0, D, V, value_buf, value_ref, 0),
        (9, D, V, reset_buf, mix_ref, D + Z),
        (8, D, Z, shared_buf, mix_ref, D),
    ]


def unpack_kernel(segments, n_out, n_given, first, slots_ref, mine_ref, twin_ref, *refs):
    refs = refs[n_given:]
    outs, refs = refs[:n_out], refs[n_out:]
    parts = segments(*refs[:-1], *outs)
    for copy in unpack(slots_ref, ((0, mine_ref), (1, twin_ref)), first, parts, refs[-1]):
        copy.wait()


def unpack_own_kernel(
    slots_ref, mine_ref, mix_in_ref, value_in_ref, mix_ref, value_ref, *refs
):
    parts = rest_segments(*refs[:-1], mix_ref, value_ref)
    for copy in unpack(slots_ref, ((0, mine_ref),), 2, parts, refs[-1]):
        copy.wait()


def unpack_rest_kernel(
    slots_ref,
    mine_ref,
    twin_ref,
    early_ref,
    twin_early_ref,
    mix_in_ref,
    value_in_ref,
    mix_ref,
    value_ref,
    expand_ref,
    alpha_ref,
    delta_ref,
    eta_ref,
    gain_ref,
    omega_ref,
    ffn_ref,
    qk_ref,
    value_buf,
    shared_buf,
    reset_buf,
    small_ref,
    sem,
):
    parts = rest_segments(value_buf, shared_buf, reset_buf, mix_ref, value_ref)
    copies = unpack(slots_ref, ((1, twin_ref),), 2, parts, sem)
    for side, pair in enumerate(((early_ref, mine_ref), (twin_early_ref, twin_ref))):
        for slot in range(4):
            place_of = slots_ref[9 + 4 * side + slot]
            row = pl.multiple_of((slots_ref[0] ^ side) * 256 + place_of * 64, 64)
            for z in range(4):
                small_ref[pl.ds(row + z * 16, 16), :] = pair[slot // 2][
                    slot % 2, z, 17 * 16 : 18 * 16, :
                ].astype(F32)
    for i, out_ref in enumerate((expand_ref, alpha_ref, delta_ref, eta_ref)):
        for j in range(D // LANES):
            at = (i * 4 + j) * H
            out_ref[:, j * LANES : (j + 1) * LANES] = small_ref[at : at + H, :]
    for i, out_ref in enumerate((gain_ref, omega_ref, ffn_ref)):
        for j in range(D // LANES):
            at = 16 * H + j * H + i
            out_ref[:, j * LANES : (j + 1) * LANES] = small_ref[at : at + 1, :]
    for j in range(3):
        at = 16 * H + j * H + 3
        qk_ref[j : j + 1, :] = small_ref[at : at + 1, :]
    for copy in copies:
        copy.wait()


def added(left, right):
    return (left.astype(F32) + right.astype(F32)).astype(BF16)


def plain_halve_kernel(level, me_ref, keep_ref, came_ref, send_ref, kept_ref):
    if level < 3:
        half = keep_ref.shape[0] // 2
        send_ref[...] = added(keep_ref[half:], came_ref[half:])
        kept_ref[...] = added(keep_ref[:half], came_ref[:half])
        return
    half = keep_ref.shape[1] // 2
    mine = (me_ref[0] >> 1) & 1
    other = pl.ds((1 - mine) * half, half)
    send_ref[0] = added(keep_ref[0, other], came_ref[0, other])
    own = pl.ds(mine * half, half)
    kept_ref[0] = added(keep_ref[0, own], came_ref[0, own])


def add_kernel(left_ref, right_ref, out_ref):
    out_ref[...] = added(left_ref[...], right_ref[...])


def add_start_kernel(left_ref, right_ref, out_ref):
    pieces, rows = out_ref.shape[1:3]
    for i in range(pieces):
        part = slice(i * rows, (i + 1) * rows)
        out_ref[0, i] = added(left_ref[part, :], right_ref[part, :])


def pair_kernel(me_ref, now_ref, came_ref, out_ref):
    half = now_ref.shape[1]
    mine = (me_ref[0] >> 1) & 1
    out_ref[0, pl.ds(mine * half, half)] = now_ref[0]
    out_ref[0, pl.ds((1 - mine) * half, half)] = came_ref[0]


def stack_kernel(now_ref, came_ref, out_ref):
    out_ref[0] = now_ref[0]
    out_ref[1] = came_ref[0]


STATE = 4 * H


def state_in(ref):
    if ref.shape[1] == D:
        return ref[...].astype(F32)
    base = ref.shape[0] - STATE
    return jnp.concatenate([ref[base + j * H : base + (j + 1) * H, :] for j in range(4)], axis=1).astype(F32)


def put_state(ref, state):
    base = ref.shape[0] - STATE
    for j in range(4):
        ref[base + j * H : base + (j + 1) * H, :] = state[:, j * LANES : (j + 1) * LANES].astype(BF16)


def halve_kernel(level, own_len, me_ref, core_ref, fade_ref, adj_ref, keep_ref, came_ref, *refs):
    groups, pieces, rows, _ = keep_ref.shape
    size = pieces * rows

    def sums(g, z0, zn):
        keep = keep_ref[g, pl.ds(z0, zn)].reshape(zn * rows, 128)
        if len(came_ref.shape) == 4:
            came = came_ref[g, pl.ds(z0, zn)].reshape(zn * rows, 128)
        else:
            start = g * size + z0 * rows
            came = came_ref[pl.ds(pl.multiple_of(start, 16), zn * rows), :]
        return added(keep, came)

    if level < 3:
        send_ref, kept_ref = refs
        put_state(send_ref, adj_ref[...].astype(F32))
        half = groups // 2
        for g in range(half):
            send_ref[g * size : (g + 1) * size, :] = sums(half + g, 0, pieces)
        for g in range(half):
            kept_ref[g] = sums(g, 0, pieces).reshape(pieces, rows, 128)
        return
    first_ref, send_ref, kept_ref, other_ref, group_ref = refs
    me = me_ref[0]
    mine = (me >> 1) & 1
    other = jnp.where(core_ref[0] == 1, state_in(first_ref), state_in(came_ref))
    other_ref[...] = other.astype(BF16)
    group = joined(own_len, 0, -1, me, adj_ref[...].astype(F32), other, fade_ref)
    group_ref[...] = group
    put_state(send_ref, group.astype(F32))
    half = pieces // 2
    send_ref[: half * rows, :] = sums(0, (1 - mine) * half, half)
    kept_ref[0] = sums(0, mine * half, half).reshape(half, rows, 128)


def exchange_kernel(own_len, me_ref, fade_ref, group_ref, keep_ref, came_ref, now_ref):
    _, pieces, rows, _ = keep_ref.shape
    keep = keep_ref[0].reshape(pieces * rows, 128)
    now_ref[: pieces * rows, :] = added(keep, came_ref[: pieces * rows, :])
    group, other = group_ref[...].astype(F32), state_in(came_ref)
    put_state(now_ref, joined(own_len, 1, -1, me_ref[0], group, other, fade_ref).astype(F32))


def exchanges(batches, seqs):
    def pairs(turn):
        out = []
        for b in range(batches):
            for s in range(seqs):
                nb, ns = turn(b, s)
                out.append((b * seqs + s, nb * seqs + ns))
        return out

    halving = [
        pairs(lambda b, s: (b ^ 1, s)),
        pairs(lambda b, s: (b, s ^ 1) if b & 1 else (b ^ 2, s)),
        pairs(lambda b, s: (b ^ 2, s) if b & 1 else (b, s ^ 1)),
        pairs(lambda b, s: (b, s ^ 2)),
    ]
    whole = []
    bit = 4
    while bit < seqs:
        whole.append(pairs(lambda b, s, bit=bit: (b, s ^ bit)))
        bit *= 2
    return halving, whole


def slot_table():
    b, s = lax.axis_index("batch"), lax.axis_index("seq")
    core, here = b & 1, ((b >> 1) & 1) * 2 + (s & 1)
    at = jnp.arange(17, dtype=jnp.int32)
    part, four = (at - 1) >> 2, (at - 1) & 3

    def swapped(v):
        return (v >> 1) | ((v & 1) << 1)

    turned = (core ^ (part & 1)) == 1
    slot = jnp.where(turned, swapped(four ^ here), four ^ here)
    group = jnp.where(turned, swapped(four) ^ here, four ^ here)
    return jnp.where(at == 0, core, jnp.where(part < 2, slot, group))


def tied(token, *arrays):
    return lax.optimization_barrier((token,) + arrays)[1:]


class Summed:
    def __init__(self, keep, send, halving, whole):
        self.keep, self.send, self.halving, self.whole = keep, send, halving, whole
        self.me = jnp.full((1,), lax.axis_index("seq"), jnp.int32)

    def first(self, token):
        (send,) = tied(token, self.send)
        self.came = lax.ppermute(send, AXES, self.halving[0])
        return send

    def halve(self, level, token):
        keep, came = tied(token, self.keep, self.came)
        groups, pieces, rows, _ = keep.shape
        shape = (groups // 2, pieces, rows, 128) if level < 3 else (1, pieces // 2, rows, 128)
        self.send, self.keep = call(
            functools.partial(plain_halve_kernel, level),
            [("v", shape, BF16)] * 2,
            [("s", self.me), ("v", keep), ("v", came)],
        )
        self.came = lax.ppermute(self.send, AXES, self.halving[level])
        return self.send

    def exchange(self, token):
        now = self.sum(self.keep, self.came, token)
        for stage in self.whole[:-1]:
            now = self.sum(now, lax.ppermute(now, AXES, stage), token)
        self.came = lax.ppermute(now, AXES, self.whole[-1])
        self.now = now
        return now

    def turn(self, token):
        self.now = self.sum(self.now, self.came, token)
        self.came = lax.ppermute(self.now, AXES, self.halving[-1])
        return self.now

    def sum(self, left, right, token):
        left, right = tied(token, left, right)
        return call(add_kernel, [("v", left.shape, BF16)], [("v", left), ("v", right)])[0]

    def double(self, level, token):
        now, came = tied(token, self.now, self.came)
        groups, pieces, rows, _ = now.shape
        if level == 2:
            (self.now,) = call(
                pair_kernel,
                [("v", (1, 2 * pieces, rows, 128), BF16)],
                [("s", self.me), ("v", now), ("v", came)],
            )
        else:
            (self.now,) = call(
                stack_kernel,
                [("v", (2, pieces, rows, 128), BF16)],
                [("v", now), ("v", came)],
            )
            self.twin = lax.ppermute(self.now, AXES, self.halving[0])
        self.came = lax.ppermute(self.now, AXES, self.halving[level])
        return self.now

    def last(self, token):
        (self.late,) = tied(token, self.came)
        self.late_twin = lax.ppermute(self.late, AXES, self.halving[0])
        return self.late


class SummedWithStates(Summed):
    def __init__(self, keep, send, halving, whole, adjoint, fades, own_len):
        super().__init__(keep, send, halving, whole)
        self.adjoint, self.fades, self.own_len = adjoint, fades, own_len
        self.core = jnp.full((1,), lax.axis_index("batch") & 1, jnp.int32)
        self.earlier = None

    def halve(self, level, token):
        keep, came = tied(token, self.keep, self.came)
        groups, pieces, rows, _ = keep.shape
        args = [("s", self.me), ("s", self.core)]
        args += [("v", t) for t in (self.fades, self.adjoint, keep, came)]
        if level < 3:
            kept = (groups // 2, pieces, rows, 128)
            extra = []
        else:
            kept = (1, pieces // 2, rows, 128)
            args.append(("v", self.earlier))
            extra = [("v", (H, D), BF16)] * 2
        sent = (kept[0] * kept[1] * rows + STATE, 128)
        self.send, self.keep, *states = call(
            functools.partial(halve_kernel, level, self.own_len),
            [("v", sent, BF16), ("v", kept, BF16)] + extra,
            args,
        )
        if states:
            self.others = [states[0]]
            self.group = states[1]
        self.earlier = came
        self.came = lax.ppermute(self.send, AXES, self.halving[level])
        return self.send

    def exchange(self, token):
        keep, came = tied(token, self.keep, self.came)
        self.others.append(came)
        _, pieces, rows, _ = keep.shape
        self.shape = keep.shape
        (self.now,) = call(
            functools.partial(exchange_kernel, self.own_len),
            [("v", (pieces * rows + STATE, 128), BF16)],
            [("s", self.me)] + [("v", t) for t in (self.fades, self.group, keep, came)],
        )
        self.came = lax.ppermute(self.now, AXES, self.whole[-1])
        return self.now

    def turn(self, token):
        now, came = tied(token, self.now, self.came)
        self.others.append(came)
        (self.now,) = call(
            add_start_kernel, [("v", self.shape, BF16)], [("v", now), ("v", came)]
        )
        self.came = lax.ppermute(self.now, AXES, self.halving[-1])
        return self.now


def shifted_pairs(seqs, by):
    return [(i, i + by) for i in range(seqs) if 0 <= i + by < seqs]


def state_powers(seqs, own_len):
    reach = WINDOW // own_len
    if by_levels(own_len):
        return [float(own_len << i) for i in range(seqs.bit_length() - 1)]
    return [float(own_len * i) for i in range(min(seqs, reach))]


def by_levels(own_len):
    return lax.axis_size("seq") == 8 and 8 <= WINDOW // own_len


def states_before(state, fades, me, own_len, beside):
    if not by_levels(own_len):
        for run in beside:
            run(state)
        return [direct_states(state, fades, own_len, 1)]
    seqs = lax.axis_size("seq")
    group, others = state, []
    levels = seqs.bit_length() - 1
    for i in range(levels):
        others.append(lax.ppermute(group, "seq", [(j, j ^ (1 << i)) for j in range(seqs)]))
        token = beside[i](group)
        if i < levels - 1:
            (other,) = tied(token, others[-1])
            (group,) = call(
                functools.partial(join_kernel, own_len, i),
                [("v", state.shape, BF16)],
                [("s", me), ("v", group), ("v", other), ("v", fades)],
            )
    return others


def direct_states(state, fades, own_len, direction):
    seqs = lax.axis_size("seq")
    total = jnp.zeros(state.shape, F32)
    for k in range(1, min(seqs, WINDOW // own_len)):
        far = lax.ppermute(state, "seq", shifted_pairs(seqs, k * direction))
        total = total + moved(far.astype(F32), fades[k - 1], float((k - 1) * own_len))
    return total


def far_part(signal, log_decay, coeff):
    own_len = signal.shape[0]
    steps = jnp.arange(own_len).astype(F32)[:, None, None]
    held = jnp.exp(log_decay[None] * (WINDOW - 1.0 - steps)) * signal[:, None, :]
    after = lax.cumsum(held, axis=0, reverse=True) - held
    return jnp.sum(coeff[None] * jnp.exp(log_decay[None] * (steps + 1.0)) * after, axis=1)


def start_unpack(who, slots, chunk, results):
    segments, outs, scratch = PLANS[who]
    given = [("s", slots), ("v", chunk.now), ("v", chunk.twin)]
    alias = {}
    if who != "A" and "mix" in results:
        alias = {len(given): outs.index(MIX_OUT)}
        given.append(("o", results["mix"]))
    return call(
        functools.partial(unpack_kernel, segments, len(outs), len(alias), 0),
        outs,
        given,
        scratch(),
        alias=alias,
    )


def own_unpack(slots, chunk, results):
    segments, outs, scratch = PLANS["C"]
    return call(
        unpack_own_kernel,
        outs,
        [("s", slots), ("v", chunk.late), ("o", results["mix"]), ("o", results["C"][1])],
        scratch(),
        alias={2: 0, 3: 1},
    )


def end_unpack(who, slots, chunk, results):
    given = [("s", slots), ("v", chunk.late), ("v", chunk.late_twin)]
    if who == "C":
        return call(
            unpack_rest_kernel,
            PLANS[who][1]
            + [("v", (H, D), F32)] * 4
            + [("v", (1, D), F32)] * 3
            + [("v", (3, Z), F32)],
            given
            + [("v", chunk.now), ("v", chunk.twin)]
            + [("o", results["mix"]), ("o", results["C"][1])],
            rest_buffers()[:-1] + [pltpu.VMEM((512, 128), F32), pltpu.SemaphoreType.DMA((12,))],
            alias={5: 0, 6: 1},
        )
    segments, outs, scratch = PLANS[who]
    before = list(results[who])
    if who != "A":
        before[outs.index(MIX_OUT)] = results["mix"]
    return call(
        functools.partial(unpack_kernel, segments, len(outs), len(outs), 2),
        outs,
        given + [("o", t) for t in before],
        scratch(),
        alias={3 + i: i for i in range(len(outs))},
    )


def wide(*shapes):
    buffers = [pltpu.VMEM((4, rows // 8, cols), F32) for rows, cols in shapes]
    return buffers + [pltpu.SemaphoreType.DMA((4 * len(shapes),))]


def rest_buffers():
    return wide((D, V), (D, Z), (D, V))


MIX_OUT = ("o", (D, MIX), F32)
PLANS = {
    "A": (
        ffn_segments,
        [("o", (FF, D), F32), ("o", (D, FF), F32)],
        lambda: wide((FF, D), (D, FF)),
    ),
    "B": (
        gates_segments,
        [("o", (V, D), F32), MIX_OUT],
        lambda: wide((V, D), (D, D), (D, D)),
    ),
    "C": (rest_segments, [MIX_OUT, ("o", (D, V), F32)], rest_buffers),
}


ORDER = (
    "Ac", "F", "Ah1", "G", "Bc", "T", "Bh1", "E", "Cc", "Ah2", "O", "Bh2", "Ah3", "Ch1", "Bh3",
    "Ax", "L", "Ch2", "At", "Bx", "Ad2", "Ch3", "Bt", "Ad1", "Cx", "Bd2", "Aa", "Ct", "Bd1",
    "Ad0", "K", "Cd2", "Ba", "Bd0", "Cd1", "Au", "Ca", "Bu", "Cd0", "Cb", "Cu",
)


def advance(chunk, who, what, token, slots, results):
    if what == "c":
        return chunk.first(token)
    if what == "x":
        return chunk.exchange(token)
    if what == "t":
        return chunk.turn(token)
    if what[0] == "h":
        return chunk.halve(int(what[1:]), token)
    if what == "d0":
        return chunk.last(token)
    if what[0] == "d":
        return chunk.double(int(what[1:]), token)
    if what == "a":
        chunk.now, chunk.twin = tied(token, chunk.now, chunk.twin)
        results[who] = list(start_unpack(who, slots, chunk, results))
    elif what == "b":
        (chunk.late,) = tied(token, chunk.late)
        results[who] = list(own_unpack(slots, chunk, results))
    else:
        chunk.late, chunk.late_twin = tied(token, chunk.late, chunk.late_twin)
        results[who] = list(end_unpack(who, slots, chunk, results))
    if who != "A":
        results["mix"] = results[who][1 if who == "B" else 0]
    return results[who][0]


def on_device(
    inputs,
    lengths,
    key_mask,
    norm_gain,
    ema_expand,
    ema_alpha,
    ema_delta,
    ema_eta,
    ema_omega,
    w_value,
    w_mix,
    qk_affine,
    w_hidden,
    ffn_gain,
    w_up,
    w_down,
    cotangent,
):
    _, rows, _ = inputs.shape
    seqs = lax.axis_size("seq")
    reach = WINDOW // rows
    halving, whole = exchanges(lax.axis_size("batch"), seqs)
    slots = slot_table()
    limit = lengths - lax.axis_index("seq") * rows
    x = inputs.reshape(rows, D)
    cot = cotangent.reshape(rows, D)
    expand, alpha, delta, eta = ema_expand.T, ema_alpha.T, ema_delta.T, ema_eta.T
    omega = ema_omega.reshape(1, D)
    gain1 = norm_gain.reshape(1, D)
    gain2 = ffn_gain.reshape(1, D)
    powers = state_powers(seqs, rows)
    me = jnp.full((1,), lax.axis_index("seq"), jnp.int32)

    def buffers(tiles):
        return [("v", (4, 4, tiles * 16, 128), BF16)] * 2

    tall = rows * 8 * (D // LANES)
    normed, masked, state, decay, coeff, fades = call(
        functools.partial(norm_kernel, rows, powers),
        [
            ("v", (rows, D), BF16),
            ("v", (rows, D), BF16),
            ("v", (2 * H, D), BF16),
            ("v", (H, D), F32),
            ("v", (H, D), F32),
            ("v", (len(powers), H, D), F32),
        ],
        [("s", limit), ("h", x), ("h", gain1)]
        + [("h", t) for t in (alpha, delta, expand, eta)],
        [pltpu.VMEM((rows, D), F32)],
    )
    early = {}

    def own_ema(token):
        (signal,) = tied(token, masked)
        early["local"], early["value"], early["mix"] = call(
            functools.partial(local_kernel, rows),
            [("v", (rows, D), F32), ("v", (D, V), BF16), ("v", (D, MIX), BF16)],
            [("v", signal), ("v", decay), ("v", coeff), ("o", w_value), ("o", w_mix)],
            [
                pltpu.VMEM((rows, D), F32),
                pltpu.VMEM((tall, LANES), F32),
                pltpu.SemaphoreType.DMA((2,)),
            ],
        )
        return early["local"]

    def own_values(token):
        (rows_in,) = tied(token, normed)
        early["value_pre"], early["value_low"], early["up"], early["down"] = call(
            value_kernel,
            [
                ("v", (rows, V), F32),
                ("v", (rows, V), BF16),
                ("v", (D, FF), BF16),
                ("v", (FF, D), BF16),
            ],
            [("v", rows_in), ("v", early["value"]), ("o", w_up), ("o", w_down)],
            [pltpu.SemaphoreType.DMA((2,))],
        )
        return early["value_low"]

    def own_inner(token):
        (down,) = tied(token, early["down"])
        early["inner"], early["hidden"] = call(
            inner_kernel,
            [("v", (rows, FF), F32), ("v", (V, D), BF16)],
            [("v", down), ("h", cot), ("o", w_hidden)],
            [pltpu.SemaphoreType.DMA((1,))],
        )
        return early["inner"]

    others = states_before(state, fades, me, rows, (own_ema, own_values, own_inner))
    w_value_near, w_mix_near, w_hidden_near = early["value"], early["mix"], early["hidden"]
    value_pre, value_low = early["value_pre"], early["value_low"]
    far_here = seqs > reach
    far, far_back, far_tables = [], [], []
    if far_here:
        behind = lax.ppermute(masked, "seq", shifted_pairs(seqs, reach)).astype(F32)
        edge, far_pull = jax.vjp(far_part, behind, jnp.log(decay), coeff)
        far = [("h", edge)]
    (
        carry,
        pre,
        mix_low,
        mixed,
        probs,
        attended,
        gated,
        cand_pre,
        resid,
        inner_low,
        g_up_low,
        keep1,
        send1,
    ) = call(
        functools.partial(forward_kernel, rows, len(others), far_here),
        [
            ("v", (2 * H, D), F32),
            ("v", (rows, D), F32),
            ("v", (rows, D), BF16),
            ("v", (rows, MIX), F32),
            ("v", (rows, BLOCK), F32),
            ("v", (rows, V), F32),
            ("v", (rows, V), BF16),
            ("v", (rows, D), F32),
            ("v", (rows, D), F32),
            ("v", (rows, FF), BF16),
            ("v", (rows, FF), BF16),
        ]
        + buffers(16),
        [("s", limit), ("s", me), ("s", slots)]
        + [("v", t) for t in (fades, masked, value_low, decay, coeff)]
        + [("v", t) for t in (w_mix_near, w_hidden_near, early["up"])]
        + [("v", t) for t in (early["local"], early["inner"], *others)]
        + far
        + [("h", t) for t in (omega, qk_affine, key_mask, x, gain2, cot)],
        [
            pltpu.VMEM((tall, LANES), F32),
            pltpu.VMEM((rows, FF), F32),
            pltpu.VMEM((rows, D), BF16),
        ],
    )
    token = resid
    chunks = {"A": Summed(keep1, send1, halving, whole)}
    results = {}
    for step in ORDER:
        who, what = step[0], step[1:]
        if step == "F":
            (g_up_low,) = tied(token, g_up_low)
            keep2, send2, g_resid, g_ffn_gain, g_hid = call(
                resid_kernel,
                buffers(16)
                + [("v", (rows, D), F32), ("v", (1, D), F32), ("v", (rows, D), BF16)],
                [("s", slots), ("h", cot), ("h", gain2)]
                + [("v", t) for t in (resid, g_up_low, early["up"], mixed, cand_pre, gated)],
            )
            token = g_resid
        elif step == "O":
            (inner_low,) = tied(token, inner_low)
            (out,) = call(
                output_kernel,
                [("v", (rows, D), BF16)],
                [("v", resid), ("v", inner_low), ("h", w_down)],
            )
            token = out
        elif step == "G":
            (g_resid,) = tied(token, g_resid)
            keep2, send2, g_skip, g_upd, g_reset, g_att = call(
                gates_kernel,
                buffers(16)
                + [
                    ("v", (rows, D), F32),
                    ("v", (rows, D), BF16),
                    ("v", (rows, V), BF16),
                    ("v", (rows, V), BF16),
                ],
                [("s", slots), ("v", keep2), ("v", send2), ("h", x), ("v", w_hidden_near)]
                + [("v", t) for t in (mix_low, mixed, attended, cand_pre, g_resid, g_hid)],
                alias={1: 0, 2: 1},
            )
            chunks["B"] = Summed(keep2, send2, halving, whole)
            token = g_skip
        elif step == "T":
            (g_att,) = tied(token, g_att)
            keep3, send3, g_qk, g_shared, g_normed = call(
                functools.partial(attention_kernel, rows),
                buffers(18) + [("v", (3, Z), F32), ("v", (rows, Z), BF16), ("v", (rows, D), F32)],
                [("s", slots)]
                + [
                    ("v", t)
                    for t in (
                        normed,
                        value_pre,
                        value_low,
                        mix_low,
                        mixed,
                        probs,
                        g_att,
                        g_reset,
                        w_value_near,
                    )
                ]
                + [("h", qk_affine)],
            )
            token = g_normed
        elif step == "E":
            (g_upd,) = tied(token, g_upd)
            if far_here:
                g_mixed = jnp.concatenate([g_upd, g_shared, g_reset, g_hid], axis=1)
                g_early = lax.dot_general(
                    g_mixed, w_mix, (((1,), (1,)), ((), ())), preferred_element_type=F32
                )
                sig = jax.nn.sigmoid(pre)
                g_behind, far_log, far_coeff = far_pull(g_early * (sig * (1.0 + pre * (1.0 - sig))))
                far_tables = [("h", jnp.concatenate([far_coeff, far_log], axis=0))]
                g_far = lax.ppermute(g_behind.astype(BF16), "seq", shifted_pairs(seqs, -reach))
                far_back = [("h", g_far.astype(F32))]
            keep3, send3, g_pre, adjoint = call(
                functools.partial(tables_kernel, rows, far_here),
                buffers(18) + [("v", (rows, D), F32), ("v", (H, D), BF16)],
                [("s", slots)]
                + [
                    ("v", t)
                    for t in (
                        keep3,
                        send3,
                        masked,
                        normed,
                        pre,
                        g_upd,
                        g_shared,
                        g_reset,
                        g_hid,
                        g_normed,
                        g_qk,
                        g_ffn_gain,
                        carry,
                        decay,
                        coeff,
                        w_mix_near,
                    )
                ]
                + far_tables
                + [("h", t) for t in (expand, alpha, delta, eta, gain1)],
                [pltpu.VMEM((rows, D), F32), pltpu.VMEM((512, 128), F32)],
                alias={1: 0, 2: 1},
            )
            if by_levels(rows):
                chunks["C"] = SummedWithStates(
                    keep3, send3, halving, whole, adjoint, fades, rows
                )
            else:
                chunks["C"] = Summed(keep3, send3, halving, whole)
                chunks["C"].others = [direct_states(adjoint, fades, rows, -1)]
            token = g_pre
        elif step == "L":
            (g_pre,) = tied(token, g_pre)
            (g_local,) = call(
                functools.partial(local_back_kernel, rows),
                [("v", (rows, D), F32)],
                [("v", t) for t in (g_pre, decay, coeff)],
                [pltpu.VMEM((tall, LANES), F32)],
            )
            token = g_local
        elif step == "K":
            others = chunks["C"].others
            (g_pre,) = tied(token, g_pre)
            (d_input,) = call(
                functools.partial(input_kernel, rows, len(others), far_here),
                [("v", (rows, D), BF16)],
                [("s", limit), ("s", me)]
                + [("v", t) for t in (fades, g_pre, g_local, g_skip, g_normed, decay, coeff)]
                + [("v", t) for t in others]
                + far_back
                + [("h", t) for t in (x, omega, gain1)],
                [pltpu.VMEM((tall, LANES), F32), pltpu.VMEM((rows, D), F32)],
            )
            token = d_input
        else:
            token = advance(chunks[who], who, what, token, slots, results)
    grad_down, grad_up = results["A"]
    grad_hidden, _ = results["B"]
    grad_mix = results["mix"]
    (
        _,
        grad_value,
        g_expand,
        g_alpha,
        g_delta,
        g_eta,
        g_norm_gain,
        g_omega,
        g_ffn_gain,
        g_qk,
    ) = results["C"]
    return (
        out.reshape(inputs.shape),
        d_input.reshape(inputs.shape),
        g_norm_gain.reshape(D),
        g_expand.T,
        g_alpha.T,
        g_delta.T,
        g_eta.T,
        g_omega.reshape(D),
        grad_value,
        grad_mix,
        g_qk,
        grad_hidden,
        g_ffn_gain.reshape(D),
        grad_up,
        grad_down,
    )


def solution(mesh):
    row = P("batch", "seq", None)
    return jax.shard_map(
        on_device,
        mesh=mesh,
        in_specs=(row, P("batch"), P("batch", "seq")) + (P(),) * 13 + (row,),
        out_specs=(row, row) + (P(),) * 13,
        check_vma=False,
    )
```
